32 devices in a mesh: replica: 8 (over z, x), shard: 4 (over y, core).
Axes of the slice: x: 2, y: 2, z: 4, core: 2. Of those that a mesh axis runs over, the one named last changes fastest.
Arguments:
- tokens: bfloat16 [8192, 768], P(('replica', 'shard')), may hold values from -6 to 6
- pass_ids: int32 [8192], P(('replica', 'shard')), may hold values from 0 to 4
- seg_ids: int32 [8192], P('replica'), may hold values from 0 to 19, never falling along the last dimension, each value on 1 to 800 neighbouring positions
- cotangent: bfloat16 [8192, 768], P(('replica', 'shard')), may hold values from -6 to 6
- pass_table: bfloat16 [768, 5], P('shard'), may hold values from -3 to 3
- norm1_gain: bfloat16 [768], P('shard'), may hold values from 0.5 to 1.5
- norm1_bias: bfloat16 [768], P('shard'), may hold values from -2 to 2
- qkv_weight: bfloat16 [768, 2304], P('shard'), may hold values from -0.21875 to 0.21875
- out_weight: bfloat16 [768, 768], P('shard'), may hold values from -0.875 to 0.875
- out_bias: bfloat16 [768], P('shard'), may hold values from -2 to 2
- norm2_gain: bfloat16 [768], P('shard'), may hold values from 0.5 to 1.5
- norm2_bias: bfloat16 [768], P('shard'), may hold values from -2 to 2
- up_weight: bfloat16 [768, 3072], P('shard'), may hold values from -0.21875 to 0.21875
- up_bias: bfloat16 [3072], P('shard'), may hold values from -3 to 3
- down_weight: bfloat16 [3072, 768], P('shard'), may hold values from -0.109375 to 0.109375
- down_bias: bfloat16 [768], P('shard'), may hold values from -2 to 2
Outputs:
- output: bfloat16 [8192, 768], P(('replica', 'shard'))
- tokens_grad: bfloat16 [8192, 768], P(('replica', 'shard'))
- pass_table_grad: float32 [768, 5], P('shard')
- norm1_gain_grad: float32 [768], P('shard')
- norm1_bias_grad: float32 [768], P('shard')
- qkv_weight_grad: float32 [768, 2304], P('shard')
- out_weight_grad: float32 [768, 768], P('shard')
- out_bias_grad: float32 [768], P('shard')
- norm2_gain_grad: float32 [768], P('shard')
- norm2_bias_grad: float32 [768], P('shard')
- up_weight_grad: float32 [768, 3072], P('shard')
- up_bias_grad: float32 [3072], P('shard')
- down_weight_grad: float32 [3072, 768], P('shard')
- down_bias_grad: float32 [768], P('shard')
The draws below stay inside these ranges and needn't reach their ends.
All inputs are finite; a program needn't handle non-finite values.
Results may differ from the reference program's by a relative error of at most 0.014.
Values may be sent and summed in bfloat16 or wider, within the bound.
No kernel may reach another device: no remote copies, remote signals or barrier semaphores. Data moves between devices by JAX's collectives and lax.ppermute only.
A program may use at most 128 MiB of HBM per device.

```python
import math
import jax
import jax.numpy as jnp
import numpy as np
from jax import lax

D = 768
H = 12
HD = 64
FF = 3072
NPASS = 5
SEQ = 1024
TOTAL = 8192


def with_ends(values, stream_key, low, top_value):
    shape = values.shape
    place = [jax.random.randint(jax.random.fold_in(stream_key, axis), (), 0, shape[axis]) for axis in range(len(shape))]
    values = values.at[tuple(place)].set(low)
    longest = shape.index(max(shape))
    place[longest] = (place[longest] + 1) % shape[longest]
    return values.at[tuple(place)].set(top_value)


def block_scale(own_key, dims, split, low, top_value):
    factor_of, own = 1.0, jax.random.fold_in(own_key, 6)
    for position, shards_of in split:
        draws = jnp.exp(jax.random.uniform(jax.random.fold_in(own, position), (shards_of,), jnp.float32, low / len(split), top_value / len(split)))
        factor_of = factor_of * jnp.repeat(draws, dims[position] // shards_of).reshape([-1 if axis == position else 1 for axis in range(len(dims))])
    return factor_of


def length_profile(amount, total, limit, skew):
    weights = [(1 << 20) // math.isqrt(grade ** skew) + 1 for grade in range(2, amount + 1)]
    surplus, counts = total - limit - (amount - 1), [1] * (amount - 1)
    while surplus > 0:
        free = [i for i in range(amount - 1) if counts[i] < limit]
        whole, budget = sum([weights[i] for i in free]), surplus
        for i in free:
            extra = min(limit - counts[i], max(1, budget * weights[i] // whole), surplus)
            counts[i] = counts[i] + extra
            surplus = surplus - extra
    return np.array([limit] + counts)


def ragged(own_key, amount, total, limit, slope):
    if amount == 2:
        one = jax.random.randint(own_key, (), max(1, total - limit), min(limit, total - 1) + 1)
        return jnp.stack([one, total - one])
    lengths = jnp.asarray(length_profile(amount, total, limit, slope), jnp.int32)
    pairs = (amount - 1) // 2
    donor, taker = lengths[1:1 + 2 * pairs:2], lengths[2:2 + 2 * pairs:2]
    room = jnp.minimum(donor - 1, limit - taker)
    passed = jax.random.randint(jax.random.fold_in(own_key, 1), (pairs,), 0, 1 << 20) % (room + 1)
    lengths = lengths.at[1:1 + 2 * pairs:2].set(donor - passed).at[2:2 + 2 * pairs:2].set(taker + passed)
    return lengths[jax.random.permutation(jax.random.fold_in(own_key, 2), amount)]


def scatter_about(stream_key, extent, deviation, bound, shards=(), held_as=jnp.bfloat16):
    level = block_scale(stream_key, extent, shards, -0.22, 0.18) if shards else 1.0
    values = jax.random.normal(stream_key, extent, jnp.float32) * deviation * level
    return jnp.minimum(jnp.maximum(values, -bound), bound).astype(held_as)


def setup_inputs(seed: int = 0) -> dict:
    streams_of = jax.random.split(jax.random.key(seed), 17)
    tokens = scatter_about(streams_of[0], (TOTAL, D), 1.0, 6.0, ((0, 32),))
    pass_ids = with_ends(jax.random.randint(streams_of[1], (TOTAL,), 0, NPASS), jax.random.fold_in(streams_of[1], 1), 0, NPASS - 1).astype(jnp.int32)
    seg_ids = jnp.searchsorted(jnp.cumsum(ragged(streams_of[2], TOTAL // min(400, SEQ // 2), TOTAL, min(800, SEQ), 0)), jnp.arange(TOTAL), side="right").astype(jnp.int32)
    cotangent = scatter_about(streams_of[3], (TOTAL, D), 1.0, 6.0, ((0, 32),))
    pass_table = scatter_about(streams_of[4], (D, NPASS), 0.5, 3.0, ((0, 4),))
    norm1_gain = jnp.clip(1.0 + 0.1 * jax.random.normal(streams_of[5], (D,), jnp.float32), 0.5, 1.5).astype(jnp.bfloat16)
    norm1_bias = scatter_about(streams_of[6], (D,), 0.3, 2.0, ((0, 4),))
    qkv_weight = scatter_about(streams_of[7], (D, 3 * D), D ** -0.5, 0.21875, ((0, 4),))
    out_weight = scatter_about(streams_of[8], (D, D), (D // 16) ** -0.5, 0.875, ((0, 4),))
    out_bias = scatter_about(streams_of[9], (D,), 0.3, 2.0, ((0, 4),))
    norm2_gain = jnp.clip(1.0 + 0.1 * jax.random.normal(streams_of[10], (D,), jnp.float32), 0.5, 1.5).astype(jnp.bfloat16)
    norm2_bias = scatter_about(streams_of[11], (D,), 0.3, 2.0, ((0, 4),))
    up_weight = scatter_about(streams_of[12], (D, FF), D ** -0.5, 0.21875, ((0, 4),))
    up_bias = scatter_about(streams_of[13], (FF,), 0.5, 3.0, ((0, 4),))
    down_weight = scatter_about(streams_of[14], (FF, D), FF ** -0.5, 0.109375, ((0, 4),))
    down_bias = scatter_about(streams_of[15], (D,), 0.3, 2.0, ((0, 4),))
    return {"tokens": tokens, "pass_ids": pass_ids, "seg_ids": seg_ids, "cotangent": cotangent, "pass_table": pass_table, "norm1_gain": norm1_gain, "norm1_bias": norm1_bias, "qkv_weight": qkv_weight, "out_weight": out_weight, "out_bias": out_bias, "norm2_gain": norm2_gain, "norm2_bias": norm2_bias, "up_weight": up_weight, "up_bias": up_bias, "down_weight": down_weight, "down_bias": down_bias}


@jax.custom_vjp
def low(v):
    return lax.optimization_barrier(v.astype(jnp.bfloat16)).astype(jnp.float32)

@jax.custom_vjp
def low_back(v):
    return v

def low_keep(v):
    return (low(v), None)

def low_pass(kept, grad):
    return (grad,)

def back_keep(v):
    return (v, None)

def back_low(kept, grad):
    return (low(grad),)
low.defvjp(low_keep, low_pass)
low_back.defvjp(back_keep, back_low)
epsilon = 1e-05
score_scale = 0.125
masked_score = -1e+30

def layer_norm(values, gain, bias):
    centre = lax.optimization_barrier(jnp.mean(values, -1, keepdims=True))
    centred = values - centre
    variance = lax.optimization_barrier(jnp.mean(centred * centred, -1, keepdims=True))
    return centred * lax.rsqrt(variance + epsilon) * gain + bias

def matmul(left, right):
    return jnp.dot(left, right, precision=lax.Precision.HIGHEST)

def reference(tokens, pass_ids, seg_ids, cotangent, pass_table, norm1_gain, norm1_bias, qkv_weight, out_weight, out_bias, norm2_gain, norm2_bias, up_weight, up_bias, down_weight, down_bias):
    seq_count = tokens.shape[0] // SEQ
    pass_rows = pass_ids.reshape(seq_count, SEQ)
    seg_rows = seg_ids.reshape(seq_count, SEQ)
    floats = tuple((item.astype(jnp.float32) for item in (tokens, pass_table, norm1_gain, norm1_bias, qkv_weight, out_weight, out_bias, norm2_gain, norm2_bias, up_weight, up_bias, down_weight, down_bias)))

    def forward(tokens_f, table, gain_one, bias_one, w_qkv, w_out, b_out, gain_two, bias_two, w_up, b_up, w_down, b_down):

        def one_sequence(items):
            rows_in, passes, segments = items
            stream_in = rows_in + jnp.take(table, passes, axis=1).T
            normed_one = low(layer_norm(stream_in, gain_one, bias_one))
            qkv = low(low_back(matmul(normed_one, w_qkv)))
            queries = qkv[:, :D].reshape(SEQ, H, HD)
            keys = qkv[:, D:2 * D].reshape(SEQ, H, HD)
            values = qkv[:, 2 * D:].reshape(SEQ, H, HD)
            positions = jnp.arange(SEQ)
            visible = (positions[None, :] <= positions[:, None]) & (segments[:, None] == segments[None, :])
            raw = jnp.einsum('qhd,khd->hqk', queries, keys, precision=lax.Precision.HIGHEST)
            scores = low_back(raw * score_scale)
            scores = jnp.where(visible[None], scores, masked_score)
            probs = low(jax.nn.softmax(scores, axis=-1))
            context = jnp.einsum('hqk,khd->qhd', probs, values, precision=lax.Precision.HIGHEST).reshape(SEQ, D)
            context = low(low_back(context))
            branch = low_back(matmul(context, w_out) + b_out)
            stream_mid = stream_in + branch
            normed_two = low(layer_norm(stream_mid, gain_two, bias_two))
            pre_act = low_back(matmul(normed_two, w_up) + b_up)
            act_low = low(jax.nn.gelu(pre_act, approximate=True))
            feed = low_back(matmul(act_low, w_down) + b_down)
            return stream_mid + feed
        result = lax.map(jax.checkpoint(one_sequence), (tokens_f.reshape(seq_count, SEQ, D), pass_rows, seg_rows))
        return result.reshape(seq_count * SEQ, D)
    result, backward = jax.vjp(forward, *floats)
    grads = backward(cotangent.astype(jnp.float32))
    return (result.astype(jnp.bfloat16), grads[0].astype(jnp.bfloat16), grads[1], grads[2], grads[3], grads[4], grads[5], grads[6], grads[7], grads[8], grads[9], grads[10], grads[11], grads[12])
```

```python
import functools

import jax
import jax.numpy as jnp
from jax import lax
from jax.experimental import pallas as pl
from jax.experimental.pallas import tpu as pltpu
from jax.sharding import PartitionSpec as P

HD = 64
epsilon = 1e-05
score_scale = 0.125
masked_score = -1e30
f32 = jnp.float32
bf16 = jnp.bfloat16

CORE = [(i, i ^ 1) for i in range(4)]
ROWY = [(i, i ^ 2) for i in range(4)]


def contract(left, right, ld, rd):
    return lax.dot_general(left, right, (((ld,), (rd,)), ((), ())), preferred_element_type=f32)


def unit_of(values):
    centred = values - jnp.mean(values, -1, keepdims=True)
    inverse = lax.rsqrt(jnp.mean(centred * centred, -1, keepdims=True) + epsilon)
    return centred * inverse, inverse


def norm_back(grad_rows, unit_rows, inverse, gain):
    scaled = grad_rows * gain
    return inverse * (
        scaled
        - jnp.mean(scaled, -1, keepdims=True)
        - unit_rows * jnp.mean(scaled * unit_rows, -1, keepdims=True)
    )


def vmem_call(body, outs, scratch=()):
    return pl.pallas_call(
        body,
        out_shape=[jax.ShapeDtypeStruct(s, d) for s, d in outs],
        out_specs=[pl.BlockSpec(memory_space=pltpu.VMEM)] * len(outs),
        scratch_shapes=[pltpu.VMEM(s, d) for s, d in scratch],
    )


def at_rows(index, size):
    return pl.ds(pl.multiple_of(index * size, size), size)


def front_body(rank_ref, segc_ref, segr_ref, b0, b1, b2, b3, w0, w1, w2, w3, wout_ref,
               send_ref, keep_ref, sin_ref, par_ref, qkv_ref, ctx_ref, lse_ref, nrm_ref, wq_ref, lse_s):
    rank = rank_ref[0]
    blocks = (b0, b1, b2, b3)
    rows, width = sin_ref.shape
    part = width // 4
    ext = [b[rows:rows + 16, 0:part].astype(f32) for b in blocks]
    cols = []
    for j in range(4):
        acc = jnp.zeros_like(ext[0])
        for k in range(4):
            acc = jnp.where((rank ^ k) == j, ext[k], acc)
        cols.append(acc)
    par = jnp.concatenate(cols, axis=1)
    par_ref[...] = par
    table = par[0:8].astype(bf16)
    gain, bias = par[5:6], par[6:7]
    for k in range(4):
        b = blocks[k]
        ids = b[rows + 11:rows + 12, 0:rows].astype(f32)
        one = (lax.broadcasted_iota(jnp.int32, (8, rows), 0).astype(f32) == ids).astype(bf16)
        x = b[0:rows].astype(f32) + contract(one, table, 0, 0)
        if k == 0:
            sin_ref[...] = x
        unit, _ = unit_of(x)
        nrm_ref[at_rows(rank ^ k, rows)] = (unit * gain + bias).astype(bf16)
    for k, w in enumerate((w0, w1, w2, w3)):
        wq_ref[at_rows(rank ^ k, part)] = w[...]
    qkv_ref[...] = jnp.dot(nrm_ref[...], wq_ref[...], preferred_element_type=f32).astype(bf16)
    heads = part // HD
    for h in range(heads):
        q = qkv_ref[:, h * HD:(h + 1) * HD] * jnp.asarray(score_scale, bf16)
        key = qkv_ref[:, part + h * HD:part + (h + 1) * HD]
        val = qkv_ref[:, 2 * part + h * HD:2 * part + (h + 1) * HD]
        for i in range(4):
            lo, nk = i * rows, (i + 1) * rows
            sc = contract(q[lo:nk], key[:nk], 1, 1)
            qpos = lo + lax.broadcasted_iota(jnp.int32, (rows, nk), 0)
            kpos = lax.broadcasted_iota(jnp.int32, (rows, nk), 1)
            seen = (segc_ref[lo:nk] == segr_ref[:, :nk]) & (kpos <= qpos)
            sc = jnp.where(seen, sc, masked_score)
            top = jnp.max(sc, -1, keepdims=True)
            e = jnp.exp(sc - top)
            total = jnp.sum(e, -1, keepdims=True)
            prob = (e * (1.0 / total)).astype(bf16)
            ctx_ref[lo:nk, h * HD:(h + 1) * HD] = jnp.dot(
                prob, val[:nk], preferred_element_type=f32).astype(bf16)
            lse_s[lo:nk, h:h + 1] = top + jnp.log(total)
    lse_ref[...] = lse_s[...].T[0:8]
    for i, k in enumerate((1, 3)):
        send_ref[i * rows:(i + 1) * rows] = jnp.dot(
            ctx_ref[at_rows(rank ^ k, rows)], wout_ref[...], preferred_element_type=f32).astype(bf16)
    for i, k in enumerate((0, 2)):
        keep_ref[i * rows:(i + 1) * rows] = jnp.dot(
            ctx_ref[at_rows(rank ^ k, rows)], wout_ref[...], preferred_element_type=f32)


def mid_body(sin_ref, par_ref, keep_ref, recv_ref, yrecv_ref, mid_ref, nrm_ref):
    mid = (sin_ref[...] + keep_ref[...] + recv_ref[...].astype(f32)
           + yrecv_ref[...].astype(f32) + par_ref[7:8])
    mid_ref[...] = mid
    unit, _ = unit_of(mid)
    nrm_ref[...] = (unit * par_ref[8:9] + par_ref[9:10]).astype(bf16)


def gelu_pair(v):
    c0, c1 = 0.7978845608028654, 0.044715
    sq = v * v
    t = jnp.tanh(c0 * v * (1.0 + c1 * sq))
    half = 0.5 * (1.0 + t)
    return v * half, half + 0.5 * v * (1.0 - t * t) * (c0 * (1.0 + 3.0 * c1 * sq))


def feed_body(rank_ref, n0, n1, n2, n3, c0, c1, c2, c3, u0, u1, u2, u3, ub_ref, dw_ref,
              send_ref, keep_ref, act_ref, pg_ref, wu_s):
    rank = rank_ref[0]
    rows, width = n0.shape
    part = width // 4
    for k, u in enumerate((u0, u1, u2, u3)):
        wu_s[at_rows(rank ^ k, part)] = u[...]
    for k, (n, c) in enumerate(((n0, c0), (n1, c1), (n2, c2), (n3, c3))):
        pre = jnp.dot(n[...], wu_s[...], preferred_element_type=f32) + ub_ref[...]
        act, slope = gelu_pair(pre)
        act_ref[k * rows:(k + 1) * rows] = act.astype(bf16)
        pg = (contract(c[...], dw_ref[...], 1, 1) * slope).astype(bf16)
        pg_ref[k * rows:(k + 1) * rows] = pg
        back = contract(pg, wu_s[...], 1, 1)
        i = k // 2
        if k % 2:
            send_ref[i * rows:(i + 1) * rows] = back.astype(bf16)
        else:
            keep_ref[i * rows:(i + 1) * rows] = back


def feed_grad_body(n0, n1, n2, n3, c0, c1, c2, c3, dw_ref, act_ref, pg_ref,
                   send_ref, keep_ref, gd_ref, gu_ref, small_ref):
    rows, width = n0.shape
    gd = jnp.zeros(gd_ref.shape, f32)
    gu = jnp.zeros(gu_ref.shape, f32)
    up_b = jnp.zeros((1, pg_ref.shape[1]), f32)
    down_b = jnp.zeros((1, width), f32)
    for k, (n, c) in enumerate(((n0, c0), (n1, c1), (n2, c2), (n3, c3))):
        act = act_ref[k * rows:(k + 1) * rows]
        pg = pg_ref[k * rows:(k + 1) * rows]
        out = jnp.dot(act, dw_ref[...], preferred_element_type=f32)
        i = k // 2
        if k % 2:
            send_ref[i * rows:(i + 1) * rows] = out.astype(bf16)
        else:
            keep_ref[i * rows:(i + 1) * rows] = out
        gd = gd + contract(act, c[...], 0, 0)
        gu = gu + contract(n[...], pg, 0, 0)
        up_b = up_b + jnp.sum(pg.astype(f32), 0, keepdims=True)
        down_b = down_b + jnp.sum(c[...].astype(f32), 0, keepdims=True)
    gd_ref[...] = gd.astype(bf16)
    gu_ref[...] = gu.astype(bf16)
    small_ref[0:1] = up_b
    small_ref[1:2] = down_b


def mid_back_body(mid_ref, par_ref, cot_ref, keep_ref, recv_ref, yrecv_ref,
                  grad_ref, branch_ref, small_ref):
    back = keep_ref[...] + recv_ref[...].astype(f32) + yrecv_ref[...].astype(f32)
    unit, inverse = unit_of(mid_ref[...])
    grad = cot_ref[...].astype(f32) + norm_back(back, unit, inverse, par_ref[8:9])
    grad_ref[...] = grad
    branch_ref[...] = grad.astype(bf16)
    small_ref[0:1] = jnp.sum(back * unit, 0, keepdims=True)
    small_ref[1:2] = jnp.sum(back, 0, keepdims=True)


def attn_back_body(rank_ref, segc_ref, segr_ref, g0, g1, g2, g3, qkv_ref, ctx_ref, lse_ref, nrm_ref,
                   wq_ref, wout_ref, send_ref, keep_ref, go_ref, gq_ref, small_ref, dctx_s, del_s, dq_s, dqkv_s):
    rank = rank_ref[0]
    rows, width = g0.shape
    part = width // 4
    total_rows = qkv_ref.shape[0]
    go = jnp.zeros(go_ref.shape, f32)
    ob = jnp.zeros((1, width), f32)
    for k, g in enumerate((g0, g1, g2, g3)):
        at = at_rows(rank ^ k, rows)
        dctx_s[at] = contract(g[...], wout_ref[...], 1, 1).astype(bf16)
        go = go + contract(ctx_ref[at], g[...], 0, 0)
        ob = ob + jnp.sum(g[...].astype(f32), 0, keepdims=True)
    go_ref[...] = go.astype(bf16)
    small_ref[0:1] = ob
    heads = part // HD
    prod = dctx_s[...].astype(f32) * ctx_ref[...].astype(f32)
    for h in range(heads):
        del_s[:, h:h + 1] = jnp.sum(prod[:, h * HD:(h + 1) * HD], -1, keepdims=True)
    delta = del_s[...].T
    for h in range(heads):
        q = qkv_ref[:, h * HD:(h + 1) * HD] * jnp.asarray(score_scale, bf16)
        key = qkv_ref[:, part + h * HD:part + (h + 1) * HD]
        val = qkv_ref[:, 2 * part + h * HD:2 * part + (h + 1) * HD]
        dctx = dctx_s[:, h * HD:(h + 1) * HD]
        for j in range(total_rows // rows):
            lo = j * rows
            hi = lo + rows
            nq = total_rows - lo
            sc = contract(key[lo:hi], q[lo:], 1, 1)
            kpos = lax.broadcasted_iota(jnp.int32, (rows, nq), 0)
            qpos = lax.broadcasted_iota(jnp.int32, (rows, nq), 1)
            seen = (segc_ref[lo:hi] == segr_ref[:, lo:]) & (kpos <= qpos)
            prob = jnp.where(seen, jnp.exp(sc - lse_ref[h:h + 1, lo:]), 0.0)
            dv = jnp.dot(prob.astype(bf16), dctx[lo:], preferred_element_type=f32)
            dprob = contract(val[lo:hi], dctx[lo:], 1, 1)
            ds = (prob * (dprob - delta[h:h + 1, lo:])).astype(bf16)
            dk = jnp.dot(ds, q[lo:], preferred_element_type=f32)
            dq = contract(ds, key[lo:hi], 0, 0)
            if j == 0:
                dq_s[...] = dq
            else:
                dq_s[lo:] += dq
            dqkv_s[lo:hi, part + h * HD:part + (h + 1) * HD] = dk.astype(bf16)
            dqkv_s[lo:hi, 2 * part + h * HD:2 * part + (h + 1) * HD] = dv.astype(bf16)
        dqkv_s[:, h * HD:(h + 1) * HD] = (dq_s[...] * score_scale).astype(bf16)
    for i, k in enumerate((1, 3)):
        send_ref[i * rows:(i + 1) * rows] = contract(
            dqkv_s[at_rows(rank ^ k, rows)], wq_ref[...], 1, 1).astype(bf16)
    for i, k in enumerate((0, 2)):
        keep_ref[i * rows:(i + 1) * rows] = contract(dqkv_s[at_rows(rank ^ k, rows)], wq_ref[...], 1, 1)
    gq_ref[...] = contract(nrm_ref[...], dqkv_s[...], 0, 0).astype(bf16)


def last_body(sin_ref, par_ref, ids_ref, grad_ref, keep_ref, recv_ref, yrecv_ref, tok_ref, small_ref):
    back = keep_ref[...] + recv_ref[...].astype(f32) + yrecv_ref[...].astype(f32)
    unit, inverse = unit_of(sin_ref[...])
    grad = grad_ref[...] + norm_back(back, unit, inverse, par_ref[5:6])
    tok_ref[...] = grad.astype(bf16)
    small_ref[5:6] = jnp.sum(back * unit, 0, keepdims=True)
    small_ref[6:7] = jnp.sum(back, 0, keepdims=True)
    rows = grad.shape[0]
    ids = ids_ref[rows + 11:rows + 12, 0:rows].astype(f32)
    one = (lax.broadcasted_iota(jnp.int32, (8, rows), 0).astype(f32) == ids).astype(f32)
    by_pass = lax.dot_general(one, grad, (((1,), (0,)), ((), ())), precision=lax.Precision.HIGHEST,
                              preferred_element_type=f32)
    small_ref[0:5] = by_pass[0:5]


def gather_rows(block):
    by_core = lax.ppermute(block, "shard", CORE)
    by_row = lax.ppermute(block, "shard", ROWY)
    both = lax.ppermute(by_row, "shard", CORE)
    return block, by_core, by_row, both


def swap_blocks(pick):
    far = lax.ppermute(jnp.stack([pick(2), pick(3)]), "shard", ROWY)
    near = lax.ppermute(pick(1), "shard", CORE)
    both = lax.ppermute(far[1], "shard", CORE)
    return pick(0), near, far[0], both


def scatter_sum(send, keep, rows):
    recv = lax.ppermute(send, "shard", CORE)
    onward = (keep[rows:] + recv[rows:].astype(f32)).astype(bf16)
    far = lax.ppermute(onward, "shard", ROWY)
    return keep[:rows], recv[:rows], far


def masks_of(count):
    masks, bit = [], 1
    while bit < count:
        masks.append(6 if bit == 4 else bit)
        bit *= 2
    return masks


def coordinate(replica, position):
    bit = (replica >> position) & 1
    if position == 1:
        bit = bit ^ ((replica >> 2) & 1)
    return bit


def plane_scatter(value, order, count, replica):
    masks = masks_of(count)
    for position in order:
        pairs = [(i, i ^ masks[position]) for i in range(count)]
        half = value.reshape((2, value.shape[0] // 2) + value.shape[1:])
        own = coordinate(replica, position)
        send = lax.dynamic_index_in_dim(half, 1 - own, 0, keepdims=False)
        keep = lax.dynamic_index_in_dim(half, own, 0, keepdims=False)
        got = lax.ppermute(send.astype(bf16), "replica", pairs)
        value = keep.astype(f32) + got.astype(f32)
    return value


def plane_gather(value, order, count, replica):
    masks = masks_of(count)
    value = value.astype(bf16)
    for position in reversed(order):
        pairs = [(i, i ^ masks[position]) for i in range(count)]
        own = coordinate(replica, position)
        got = lax.ppermute(value, "replica", pairs)
        first = jnp.where(own == 0, value, got)
        second = jnp.where(own == 0, got, value)
        value = jnp.concatenate([first, second], 0)
    return value


def plane_sum(value, order, count, replica):
    rows = value.shape[0]
    parts = value.reshape((count, rows // count) + value.shape[1:])
    piece = plane_scatter(parts, order, count, replica)
    return plane_gather(piece, order, count, replica).reshape(value.shape)


def plane_sum_columns(value, order, count, replica, rank):
    rows, cols = value.shape[0] // 4, value.shape[1]
    parts = value.reshape(4, count, rows // count, cols).transpose(1, 0, 2, 3)
    piece = plane_scatter(parts, order, count, replica)[0].astype(bf16)
    blocks = swap_blocks(lambda k: lax.dynamic_index_in_dim(piece, rank ^ k, 0, keepdims=False))
    stack = jnp.stack(blocks)
    natural = jnp.stack([lax.dynamic_index_in_dim(stack, rank ^ j, 0, keepdims=False) for j in range(4)])
    full = plane_gather(natural[None], order, count, replica)
    return full.transpose(0, 2, 1, 3).reshape(rows, 4, cols)


def shards(replicas, tokens, pass_ids, seg_ids, cotangent, pass_table, norm1_gain, norm1_bias, qkv_weight, out_weight,
           out_bias, norm2_gain, norm2_bias, up_weight, up_bias, down_weight, down_bias):
    rows, width = tokens.shape
    part = width // 4
    seq = seg_ids.shape[0]
    rank = lax.axis_index("shard")
    replica = lax.axis_index("replica")
    rank_s = rank.reshape(1).astype(jnp.int32)
    smem = pl.BlockSpec(memory_space=pltpu.SMEM)
    vmem = pl.BlockSpec(memory_space=pltpu.VMEM)

    def call(body, outs, scratch, *args, ranked=True):
        specs = [smem] * ranked + [vmem] * (len(args) - ranked)
        return pl.pallas_call(
            body,
            out_shape=[jax.ShapeDtypeStruct(s, d) for s, d in outs],
            in_specs=specs,
            out_specs=[vmem] * len(outs),
            scratch_shapes=[pltpu.VMEM(s, d) for s, d in scratch],
        )(*args)

    def row_of(vector):
        return jnp.pad(vector.astype(bf16), (0, width - vector.shape[0]))[None]

    extra = [jnp.pad(pass_table.T, ((0, 0), (0, width - part)))]
    extra += [row_of(v) for v in (norm1_gain, norm1_bias, out_bias, norm2_gain, norm2_bias, down_bias, pass_ids)]
    extra = jnp.concatenate(extra + [jnp.zeros((4, width), bf16)], 0)
    blocks = gather_rows(jnp.concatenate([tokens, extra], 0))

    columns = qkv_weight.reshape(part, 3, 4, part).transpose(2, 0, 1, 3).reshape(4, part, 3 * part)
    wq = swap_blocks(lambda k: lax.dynamic_index_in_dim(columns, rank ^ k, 0, keepdims=False))
    hidden = up_bias.shape[0]
    up_cols = up_weight.reshape(part, 4, hidden).transpose(1, 0, 2)
    wu = swap_blocks(lambda k: lax.dynamic_index_in_dim(up_cols, rank ^ k, 0, keepdims=False))
    cot = gather_rows(cotangent)

    segc, segr = seg_ids[:, None], seg_ids[None, :]
    send, keep, sin, par, qkv, ctx, lse, nrm, wq_full = call(
        front_body,
        [((2 * rows, width), bf16), ((2 * rows, width), f32), ((rows, width), f32), ((16, width), f32),
         ((seq, 3 * part), bf16), ((seq, part), bf16), ((8, seq), f32), ((seq, width), bf16), ((width, 3 * part), bf16)],
        [((seq, 128), f32)],
        rank_s, segc, segr, *blocks, *wq, out_weight)
    mid, nrm2 = call(mid_body, [((rows, width), f32), ((rows, width), bf16)], [],
                     sin, par, *scatter_sum(send, keep, rows), ranked=False)
    n2 = gather_rows(nrm2)
    send, keep, act, pg = call(
        feed_body,
        [((2 * rows, width), bf16), ((2 * rows, width), f32), ((seq, hidden), bf16), ((seq, hidden), bf16)],
        [((width, hidden), bf16)],
        rank_s, *n2, *cot, *wu, up_bias.astype(f32)[None], down_weight)
    back = scatter_sum(send, keep, rows)
    send, keep, grad_down, grad_up, small_feed = call(
        feed_grad_body,
        [((2 * rows, width), bf16), ((2 * rows, width), f32), ((hidden, width), bf16), ((width, hidden), bf16),
         ((8, width), f32)],
        [], *n2, *cot, down_weight, act, pg, ranked=False)
    mid_grad, branch, small_mid = call(
        mid_back_body, [((rows, width), f32), ((rows, width), bf16), ((8, width), f32)], [],
        mid, par, cotangent, *back, ranked=False)
    out_parts = scatter_sum(send, keep, rows)
    output = (mid + out_parts[0] + out_parts[1].astype(f32) + out_parts[2].astype(f32) + par[10:11]).astype(bf16)
    branches = gather_rows(branch)
    send, keep, grad_out, grad_qkv, small_attn = call(
        attn_back_body,
        [((2 * rows, width), bf16), ((2 * rows, width), f32), ((part, width), bf16), ((width, 3 * part), bf16),
         ((8, width), f32)],
        [((seq, part), bf16), ((seq, 128), f32), ((seq, HD), f32), ((seq, 3 * part), bf16)],
        rank_s, segc, segr, *branches, qkv, ctx, lse, nrm, wq_full, out_weight)
    tokens_grad, small_last = call(
        last_body, [((rows, width), bf16), ((8, width), f32)], [],
        sin, par, blocks[0], mid_grad, *scatter_sum(send, keep, rows), ranked=False)

    orders = [list(range(len(masks_of(replicas))))]
    for _ in range(2):
        orders.append(orders[-1][1:] + orders[-1][:1])
    final_down = plane_sum(grad_down, orders[0], replicas, replica).astype(f32)
    final_up = plane_sum_columns(grad_up, orders[1], replicas, replica, rank).astype(f32)
    final_up = final_up.reshape(part, 4 * hidden)
    final_out = plane_sum(grad_out, orders[2], replicas, replica).astype(f32)
    final_qkv = plane_sum_columns(grad_qkv, orders[0], replicas, replica, rank).astype(f32)
    final_qkv = final_qkv.reshape(part, 4, 3, part).transpose(0, 2, 1, 3).reshape(part, 12 * part)

    own = (lax.broadcasted_iota(jnp.int32, (4, 1), 0) == rank).astype(f32)
    up_slots = (own * small_feed[0:1]).reshape(4, hidden)
    complete = jnp.stack([small_feed[1], small_attn[0]]).reshape(2, 4, part) * own[None]
    packed = jnp.concatenate([
        small_last[0:7].reshape(7, 4, part), small_mid[0:2].reshape(2, 4, part), complete,
        up_slots.reshape(4, 4, part).transpose(1, 0, 2)], 0)
    packed = lax.psum(packed, ("replica", "shard"))
    mine = lax.dynamic_index_in_dim(packed, rank, 1, keepdims=False)
    return (
        output,
        tokens_grad,
        mine[0:5].T,
        mine[5],
        mine[6],
        final_qkv,
        final_out,
        mine[10],
        mine[7],
        mine[8],
        final_up,
        mine[11:15].reshape(hidden),
        final_down,
        mine[9],
    )


def solution(mesh):
    row = P(("replica", "shard"), None)
    flat = P(("replica", "shard"))
    w2, w1 = P("shard", None), P("shard")
    return jax.shard_map(
        functools.partial(shards, mesh.shape["replica"]),
        mesh=mesh,
        in_specs=(row, flat, P("replica"), row, w2, w1, w1, w2, w2, w1, w1, w1, w2, w1, w2, w1),
        out_specs=(row, row, w2, w1, w1, w2, w2, w1, w1, w1, w2, w1, w2, w1),
        check_vma=False,
    )
```

```python
import functools

import jax
import jax.numpy as jnp
from jax import lax
from jax.experimental import pallas as pl
from jax.experimental.pallas import tpu as pltpu
from jax.sharding import PartitionSpec as P

HD = 64
epsilon = 1e-05
score_scale = 0.125
masked_score = -1e30
f32 = jnp.float32
bf16 = jnp.bfloat16

CORE = [(i, i ^ 1) for i in range(4)]
ROWY = [(i, i ^ 2) for i in range(4)]
BOTH = [(i, i ^ 3) for i in range(4)]


def contract(left, right, ld, rd):
    return lax.dot_general(left, right, (((ld,), (rd,)), ((), ())), preferred_element_type=f32)


def unit_of(values):
    centred = values - jnp.mean(values, -1, keepdims=True)
    inverse = lax.rsqrt(jnp.mean(centred * centred, -1, keepdims=True) + epsilon)
    return centred * inverse, inverse


def norm_back(grad_rows, unit_rows, inverse, gain):
    scaled = grad_rows * gain
    return inverse * (
        scaled
        - jnp.mean(scaled, -1, keepdims=True)
        - unit_rows * jnp.mean(scaled * unit_rows, -1, keepdims=True)
    )


def at_rows(index, size):
    return pl.ds(pl.multiple_of(index * size, size), size)


def pack_body(x_ref, ids_ref, table_ref, g1_ref, b1_ref, ob_ref, g2_ref, b2_ref, db_ref, out_ref):
    passes, part = table_ref.shape
    rows = ids_ref.shape[0]
    out_ref[0:rows] = x_ref[...]
    ext = jnp.zeros((16, out_ref.shape[1]), bf16)
    out_ref[rows:] = ext
    out_ref[rows:rows + passes, 0:part] = table_ref[...]
    for i, ref in enumerate((g1_ref, b1_ref, ob_ref, g2_ref, b2_ref, db_ref)):
        out_ref[rows + 5 + i:rows + 6 + i, 0:part] = ref[...].astype(f32).reshape(1, part).astype(bf16)
    out_ref[rows + 11:rows + 12, 0:rows] = ids_ref[...].astype(f32).reshape(1, rows).astype(bf16)


def norm_body(rank_ref, x0, x1, x2, x3,
              sin_ref, par_ref, nrm_ref, unit_ref, inv_ref, ids_ref):
    rank = rank_ref[0]
    rows, width = sin_ref.shape
    part = width // 4
    ext = [b[rows:rows + 16, 0:part].astype(f32) for b in (x0, x1, x2, x3)]
    cols = []
    for j in range(4):
        acc = jnp.zeros_like(ext[0])
        for k in range(4):
            acc = jnp.where((rank ^ k) == j, ext[k], acc)
        cols.append(acc)
    par = jnp.concatenate(cols, axis=1)
    par_ref[...] = par
    table = par[0:8].astype(bf16)
    gain, bias = par[5:6], par[6:7]
    for k, b in enumerate((x0, x1, x2, x3)):
        ids = b[rows + 11:rows + 12, 0:rows].astype(f32)
        ids_ref[k:k + 1] = ids
        one = (lax.broadcasted_iota(jnp.int32, (8, rows), 0).astype(f32) == ids).astype(bf16)
        x = b[0:rows].astype(f32) + contract(one, table, 0, 0)
        if k == 0:
            sin_ref[...] = x
        unit, inverse = unit_of(x)
        at = at_rows(rank ^ k, rows)
        unit_ref[at] = unit.astype(bf16)
        inv_ref[at] = inverse
        nrm_ref[at] = (unit * gain + bias).astype(bf16)


def front_body(rank_ref, segc_ref, segr_ref, nrm_ref, w0, w1, w2, w3, wout_ref,
               send_ref, keep_ref, far_ref, qkv_ref, ctx_ref, lse_ref, wq_ref, lse_s):
    rank = rank_ref[0]
    rows, width = keep_ref.shape
    part = width // 4
    for k, w in enumerate((w0[...], w1[...], w2[0:part], w3[...])):
        wq_ref[at_rows(rank ^ k, part)] = w
    qkv_ref[...] = jnp.dot(nrm_ref[...], wq_ref[...], preferred_element_type=f32).astype(bf16)
    heads = part // HD
    for h in range(heads):
        q = qkv_ref[:, h * HD:(h + 1) * HD] * jnp.asarray(score_scale, bf16)
        key = qkv_ref[:, part + h * HD:part + (h + 1) * HD]
        val = qkv_ref[:, 2 * part + h * HD:2 * part + (h + 1) * HD]
        for i in range(4):
            lo, nk = i * rows, (i + 1) * rows
            sc = contract(q[lo:nk], key[:nk], 1, 1)
            qpos = lo + lax.broadcasted_iota(jnp.int32, (rows, nk), 0)
            kpos = lax.broadcasted_iota(jnp.int32, (rows, nk), 1)
            seen = (segc_ref[lo:nk] == segr_ref[:, :nk]) & (kpos <= qpos)
            sc = jnp.where(seen, sc, masked_score)
            top = jnp.max(sc, -1, keepdims=True)
            e = jnp.exp(sc - top)
            total = jnp.sum(e, -1, keepdims=True)
            prob = (e * (1.0 / total)).astype(bf16)
            ctx_ref[lo:nk, h * HD:(h + 1) * HD] = jnp.dot(
                prob, val[:nk], preferred_element_type=f32).astype(bf16)
            lse_s[lo:nk, h:h + 1] = top + jnp.log(total)
    lse_ref[...] = lse_s[...].T[0:8]
    for i, k in enumerate((1, 3)):
        send_ref[i * rows:(i + 1) * rows] = jnp.dot(
            ctx_ref[at_rows(rank ^ k, rows)], wout_ref[...], preferred_element_type=f32).astype(bf16)
    for ref, k in ((keep_ref, 0), (far_ref, 2)):
        ref[...] = jnp.dot(ctx_ref[at_rows(rank ^ k, rows)], wout_ref[...], preferred_element_type=f32)


def mid_body(sin_ref, par_ref, keep_ref, recv_ref, yrecv_ref, mid_ref, nrm_ref):
    rows = sin_ref.shape[0]
    mid = (sin_ref[...] + keep_ref[...] + recv_ref[0:rows].astype(f32)
           + yrecv_ref[...].astype(f32) + par_ref[7:8])
    mid_ref[...] = mid
    unit, _ = unit_of(mid)
    nrm_ref[...] = (unit * par_ref[8:9] + par_ref[9:10]).astype(bf16)


def gelu_pair(v):
    c0, c1 = 0.7978845608028654, 0.044715
    sq = v * v
    t = jnp.tanh(c0 * v * (1.0 + c1 * sq))
    half = 0.5 * (1.0 + t)
    return v * half, half + 0.5 * v * (1.0 - t * t) * (c0 * (1.0 + 3.0 * c1 * sq))


def feed_body(rank_ref, n0, n1, n2, n3, c0, g1, g2, g3, u0, pair_ref, ub_ref, dw_ref,
              send_ref, keep_ref, far_ref, act_ref, pg_ref, wu_s):
    rank = rank_ref[0]
    rows, width = n0.shape
    part = width // 4
    ub_row = ub_ref[...].astype(f32).reshape(1, ub_ref.shape[0])
    side = rank_ref[2]
    wu_s[at_rows(rank, part)] = u0[...]
    wu_s[at_rows(rank ^ 1, part)] = g1[rows:]

    @pl.when(side == 0)
    def _():
        wu_s[at_rows(rank ^ 2, part)] = g2[rows:]
        wu_s[at_rows(rank ^ 3, part)] = pair_ref[...]

    @pl.when(side == 1)
    def _():
        wu_s[at_rows(rank ^ 2, part)] = pair_ref[...]
        wu_s[at_rows(rank ^ 3, part)] = g3[rows:]

    for k, (n, c) in enumerate(((n0, c0[...]), (n1, g1[0:rows]), (n2, g2[0:rows]), (n3, g3[0:rows]))):
        pre = jnp.dot(n[...], wu_s[...], preferred_element_type=f32) + ub_row
        act, slope = gelu_pair(pre)
        act_ref[k * rows:(k + 1) * rows] = act.astype(bf16)
        pg = (contract(c, dw_ref[...], 1, 1) * slope).astype(bf16)
        pg_ref[k * rows:(k + 1) * rows] = pg
        back = contract(pg, wu_s[...], 1, 1)
        if k % 2:
            send_ref[(k // 2) * rows:(k // 2 + 1) * rows] = back.astype(bf16)
        else:
            (far_ref if k else keep_ref)[...] = back


def chunk_at(rank, me, count, p):
    top, next_bit = count // 2, count // 4
    turned = p
    if next_bit:
        turned = (p % next_bit) + jnp.where((p & top) != 0, next_bit, 0) + jnp.where((p & next_bit) != 0, top, 0)
    return me ^ jnp.where((rank & 1) == 0, p, turned)


def chunk_feed(rank, me, count, gd_s, gu_s, keep_ref, gsend_ref):
    down_rows, up_rows = gd_s.shape[0] // count, gu_s.shape[0] // count // 4
    part = gu_s.shape[0] // 4

    def store(target, start):
        def one(p, carry):
            nat = chunk_at(rank, me, count, p + start)
            target[p, 0:down_rows] = gd_s[at_rows(nat, down_rows)].astype(target.dtype)
            for k in range(4):
                at = pl.ds(pl.multiple_of((rank ^ k) * part + nat * up_rows, 8), up_rows)
                lo = down_rows + k * up_rows
                target[p, lo:lo + up_rows] = gu_s[at].astype(target.dtype)
            return carry

        lax.fori_loop(0, count // 2, one, 0)

    store(keep_ref, 0)
    store(gsend_ref, count // 2)


def feed_grad_body(count, rank_ref, n0, n1, n2, n3, c0, g1, g2, g3, act_ref, pg_ref,
                   upb_ref, gkeep_ref, gsend_ref, gd_s, gu_s):
    rank, me = rank_ref[0], rank_ref[1]
    rows, width = n0.shape
    part = width // 4
    up_b = jnp.zeros((1, pg_ref.shape[1]), f32)
    blocks = ((n0, c0[...]), (n1, g1[0:rows]), (n2, g2[0:rows]), (n3, g3[0:rows]))
    for k, (n, c) in enumerate(blocks):
        act = act_ref[k * rows:(k + 1) * rows]
        pg = pg_ref[k * rows:(k + 1) * rows]
        gd = contract(act, c, 0, 0)
        gu = contract(n[...], pg, 0, 0)
        gd_s[...] = gd if k == 0 else gd_s[...] + gd
        gu_s[...] = gu if k == 0 else gu_s[...] + gu
        up_b = up_b + jnp.sum(pg.astype(f32), 0, keepdims=True)
    upb_ref[0:1] = up_b
    if in_kernel(count, width):
        chunk_feed(rank, me, count, gd_s, gu_s, gkeep_ref, gsend_ref)
    else:
        gkeep_ref[...] = gd_s[...]
        gsend_ref[...] = gu_s[...]


def feed_out_body(dw_ref, act_ref, send_ref, keep_ref, far_ref):
    rows = keep_ref.shape[0]
    for k in range(4):
        out = jnp.dot(act_ref[k * rows:(k + 1) * rows], dw_ref[...], preferred_element_type=f32)
        if k % 2:
            send_ref[(k // 2) * rows:(k // 2 + 1) * rows] = out.astype(bf16)
        else:
            (far_ref if k else keep_ref)[...] = out


def in_kernel(count, width):
    return (width // 4 // count) % 24 == 0


def mid_back_body(mid_ref, par_ref, cot_ref, ids_ref, keep_ref, recv_ref, yrecv_ref,
                  grad_ref, branch_ref, small_ref):
    rows = mid_ref.shape[0]
    back = keep_ref[...] + recv_ref[0:rows].astype(f32) + yrecv_ref[...].astype(f32)
    unit, inverse = unit_of(mid_ref[...])
    cot = cot_ref[...].astype(f32)
    grad = cot + norm_back(back, unit, inverse, par_ref[8:9])
    grad_ref[...] = grad
    branch = grad.astype(bf16)
    branch_ref[...] = branch
    one = (lax.broadcasted_iota(jnp.int32, (8, rows), 0).astype(f32) == ids_ref[0:1]).astype(bf16)
    small_ref[0:8] = contract(one, branch, 1, 0)
    small_ref[8:9] = jnp.sum(back * unit, 0, keepdims=True)
    small_ref[9:10] = jnp.sum(back, 0, keepdims=True)
    small_ref[10:11] = jnp.sum(branch.astype(f32), 0, keepdims=True)
    small_ref[11:12] = jnp.sum(cot, 0, keepdims=True)


def heads_back(heads, segc_ref, segr_ref, qkv_ref, lse_ref, delta_ref, dctx_ref, dqkv_ref, dq_s):
    part = dctx_ref.shape[1]
    total_rows = qkv_ref.shape[0]
    rows = total_rows // 4
    for h in heads:
        q = qkv_ref[:, h * HD:(h + 1) * HD] * jnp.asarray(score_scale, bf16)
        key = qkv_ref[:, part + h * HD:part + (h + 1) * HD]
        val = qkv_ref[:, 2 * part + h * HD:2 * part + (h + 1) * HD]
        dctx = dctx_ref[:, h * HD:(h + 1) * HD]
        for j in range(total_rows // rows):
            lo = j * rows
            hi = lo + rows
            nq = total_rows - lo
            sc = contract(key[lo:hi], q[lo:], 1, 1)
            kpos = lax.broadcasted_iota(jnp.int32, (rows, nq), 0)
            qpos = lax.broadcasted_iota(jnp.int32, (rows, nq), 1)
            seen = (segc_ref[lo:hi] == segr_ref[:, lo:]) & (kpos <= qpos)
            prob = jnp.where(seen, jnp.exp(sc - lse_ref[h:h + 1, lo:]), 0.0)
            dv = jnp.dot(prob.astype(bf16), dctx[lo:], preferred_element_type=f32)
            dprob = contract(val[lo:hi], dctx[lo:], 1, 1)
            ds = (prob * (dprob - delta_ref[h:h + 1, lo:])).astype(bf16)
            dk = jnp.dot(ds, q[lo:], preferred_element_type=f32)
            dq = contract(ds, key[lo:hi], 0, 0)
            if j == 0:
                dq_s[...] = dq
            else:
                dq_s[lo:] += dq
            dqkv_ref[lo:hi, part + h * HD:part + (h + 1) * HD] = dk.astype(bf16)
            dqkv_ref[lo:hi, 2 * part + h * HD:2 * part + (h + 1) * HD] = dv.astype(bf16)
        dqkv_ref[:, h * HD:(h + 1) * HD] = (dq_s[...] * score_scale).astype(bf16)


def attn_back_one_body(heads, rank_ref, segc_ref, segr_ref, g0, g1, g2, g3, qkv_ref, ctx_ref, lse_ref, wout_ref,
                       dctx_ref, delta_ref, go_ref, dqkv_ref, del_s, dq_s):
    rank = rank_ref[0]
    rows, width = g0.shape
    part = width // 4
    go = jnp.zeros((part, width), f32)
    for k, g in enumerate((g0, g1, g2, g3)):
        at = at_rows(rank ^ k, rows)
        dctx_ref[at] = contract(g[...], wout_ref[...], 1, 1).astype(bf16)
        go = go + contract(ctx_ref[at], g[...], 0, 0)
    go_ref[...] = go
    prod = dctx_ref[...].astype(f32) * ctx_ref[...].astype(f32)
    for h in range(part // HD):
        del_s[:, h:h + 1] = jnp.sum(prod[:, h * HD:(h + 1) * HD], -1, keepdims=True)
    delta_ref[...] = del_s[...].T[0:8]
    heads_back(heads, segc_ref, segr_ref, qkv_ref, lse_ref, delta_ref, dctx_ref, dqkv_ref, dq_s)


def attn_back_two_body(count, heads, rank_ref, segc_ref, segr_ref, qkv_ref, lse_ref, delta_ref, dctx_ref, dqkv_in,
                       go_s, nrm_ref, unit_ref, inv_ref, ids_ref, par_ref, smid_ref, upb_ref, wq_ref,
                       send_ref, keep_ref, far_ref, gkeep_ref, gsend_ref, sm_ref, dqkv_s,
                       dq_s, gq_s, sm_s):
    dqkv_s[...] = dqkv_in[...]
    rank, me = rank_ref[0], rank_ref[1]
    rows, width = keep_ref.shape
    part = width // 4
    heads_back(heads, segc_ref, segr_ref, qkv_ref, lse_ref, delta_ref, dctx_ref, dqkv_s, dq_s)
    gain = par_ref[5:6]
    by_pass = smid_ref[0:8]
    gain_sum = jnp.zeros((1, width), f32)
    bias_sum = jnp.zeros((1, width), f32)
    for k in range(4):
        at = at_rows(rank ^ k, rows)
        back = contract(dqkv_s[at], wq_ref[...], 1, 1)
        if k % 2:
            send_ref[(k // 2) * rows:(k // 2 + 1) * rows] = back.astype(bf16)
        else:
            (far_ref if k else keep_ref)[...] = back
        unit = unit_ref[at].astype(f32)
        gain_sum = gain_sum + jnp.sum(back * unit, 0, keepdims=True)
        bias_sum = bias_sum + jnp.sum(back, 0, keepdims=True)
        one = (lax.broadcasted_iota(jnp.int32, (8, rows), 0).astype(f32) == ids_ref[k:k + 1]).astype(bf16)
        by_pass = by_pass + contract(one, norm_back(back, unit, inv_ref[at], gain).astype(bf16), 1, 0)
    gq_s[...] = contract(nrm_ref[...], dqkv_s[...], 0, 0)
    full = jnp.concatenate([by_pass[0:5], gain_sum, bias_sum, smid_ref[8:12],
                            jnp.zeros((5, width), f32)], 0)
    up_b = upb_ref[0:1]
    mine = lax.broadcasted_iota(jnp.int32, (16, part), 0)
    for j in range(4):
        sm = full[:, j * part:(j + 1) * part]
        for i in range(4):
            sm = jnp.where((mine == 11 + i) & (rank == j), up_b[:, i * part:(i + 1) * part], sm)
        sm_s[j] = sm
    if in_kernel(count, width):
        chunk_qkv(rank, me, count, gq_s, go_s, sm_s, gkeep_ref, gsend_ref)
        sm_ref[...] = jnp.zeros(sm_ref.shape, f32)
    else:
        gkeep_ref[...] = gq_s[...]
        gsend_ref[...] = go_s[...]
        for k in range(4):
            sm_ref[k] = sm_s[rank ^ k]


def chunk_qkv(rank, me, count, gq_s, go_s, sm_s, keep_ref, gsend_ref):
    part = go_s.shape[0]
    rows = part // count
    small = 16 // count
    wide = gq_s.shape[1]
    step = rows + small

    def store(target, p, nat, place):
        for k in range(4):
            at = pl.ds(pl.multiple_of((rank ^ k) * part + nat * rows, 8), rows)
            target[place, k * step:k * step + rows] = gq_s[at].astype(target.dtype)
        out = go_s[at_rows(nat, rows)]
        third = rows // 3
        target[place, 4 * step:4 * step + rows] = out[:, 0:wide].astype(target.dtype)
        tail = out[:, wide:]
        packed = jnp.concatenate([tail[i * third:(i + 1) * third] for i in range(3)], 1)
        target[place, 4 * step + rows:4 * step + rows + third] = packed.astype(target.dtype)

    for p in range(count):
        target, place = (keep_ref, p) if p < count // 2 else (gsend_ref, p - count // 2)
        nat = chunk_at(rank, me, count, p)
        store(target, p, nat, place)
        for k in range(4):
            sm = sm_s[rank ^ k]
            row = jnp.zeros((small, part), f32)
            for c in range(count):
                row = jnp.where(nat == c, sm[c * small:(c + 1) * small], row)
            target[place, k * step + rows:k * step + rows + small, 0:part] = row.astype(target.dtype)
            target[place, k * step + rows:k * step + rows + small, part:] = jnp.zeros(
                (small, wide - part), target.dtype)


def last_body(sin_ref, par_ref, grad_ref, keep_ref, recv_ref, yrecv_ref, tok_ref):
    rows = sin_ref.shape[0]
    back = keep_ref[...] + recv_ref[0:rows].astype(f32) + yrecv_ref[...].astype(f32)
    unit, inverse = unit_of(sin_ref[...])
    tok_ref[...] = (grad_ref[...] + norm_back(back, unit, inverse, par_ref[5:6])).astype(bf16)


def place_feed_body(rank_ref, g_ref, *refs):
    down_ref, up_ref = refs[-2:]
    rank = rank_ref[0]
    down_rows = down_ref.shape[0]
    up_rows, hidden = up_ref.shape[0], up_ref.shape[1] // 4
    down_ref[...] = g_ref[0, 0:down_rows].astype(f32)
    for k in range(4):
        lo = down_rows + k * up_rows
        up_ref[:, pl.ds(pl.multiple_of((rank ^ k) * hidden, hidden), hidden)] = g_ref[0, lo:lo + up_rows].astype(f32)


def place_qkv_body(count, start, rank_ref, g_ref, *refs):
    rank, me = rank_ref[0], rank_ref[1]
    if start:
        sm_in, _, _, qkv_ref, out_ref = refs[:5]
        small_refs, stage_s, sm_s = refs[5:-2], refs[-2], refs[-1]
    else:
        qkv_ref, out_ref, sm_s, stage_s = refs
    step = pl.program_id(0)
    rows, third = out_ref.shape[0], out_ref.shape[0] // 3
    width = out_ref.shape[1]
    part = width // 4
    wide = g_ref.shape[2]
    small = 16 // count
    if start:
        @pl.when(step == 0)
        def _():
            sm_s[...] = sm_in[...]
    stage_s[...] = g_ref[0, 0:4 * rows].astype(f32)
    for j in range(4):
        block = stage_s[at_rows(rank ^ j, rows)]
        for i in range(3):
            qkv_ref[:, i * width + j * part:i * width + (j + 1) * part] = block[:, i * part:(i + 1) * part]
    sm_s[chunk_at(rank, me, count, step + start)] = g_ref[0, 4 * rows:4 * rows + small, 0:part].astype(f32)
    lo = 4 * rows + small
    out_ref[:, 0:wide] = g_ref[0, lo:lo + rows].astype(f32)
    packed = g_ref[0, lo + rows:lo + rows + third].astype(f32)
    out_ref[:, wide:] = jnp.concatenate([packed[:, i * part:(i + 1) * part] for i in range(3)], 0)
    if start:
        @pl.when(step == pl.num_programs(0) - 1)
        def _():
            rows_of = [sm_s[i // small, i % small:i % small + 1] for i in range(16)]
            table_ref = small_refs[0]
            for i in range(table_ref.shape[0]):
                table_ref[i:i + 1] = rows_of[i]
            for ref, i in zip(small_refs[1:7], (5, 6, 9, 7, 8, 10)):
                ref[...] = rows_of[i].reshape(part)
            for i in range(4):
                small_refs[7][i * part:(i + 1) * part] = rows_of[11 + i].reshape(part)


def qkv_blocks_body(rank_ref, w_ref, own_ref, near_ref, far_ref, stage_s):
    rank = rank_ref[0]
    part = w_ref.shape[0]
    for t in range(4):
        stage_s[t] = jnp.concatenate(
            [w_ref[:, (4 * i + t) * part:(4 * i + t + 1) * part] for i in range(3)], 1)
    own_ref[...] = stage_s[rank]
    near_ref[...] = stage_s[rank ^ 1]
    far_ref[0:part] = stage_s[rank ^ 2]
    far_ref[part:] = stage_s[rank ^ 3]


def up_blocks_body(rank_ref, w_ref, cot_ref, own_ref, near_ref, far_ref):
    rank, side = rank_ref[0], rank_ref[2]
    rows = cot_ref.shape[0]
    hidden = own_ref.shape[1]

    def block(k):
        return w_ref[:, pl.ds(pl.multiple_of((rank ^ k) * hidden, hidden), hidden)]

    own_ref[...] = block(0)
    near_ref[0:rows] = cot_ref[...]
    near_ref[rows:] = block(1)
    far_ref[0:rows] = cot_ref[...]
    far_ref[rows:] = block(2 + side)


def by_core(value):
    return lax.ppermute(value, "shard", CORE)


def by_row(value):
    return lax.ppermute(value, "shard", ROWY)


def gather_rows(block):
    far = by_row(block)
    return block, by_core(block), far, by_core(far)


def scatter_sum(send, keep, far, rows, *first):
    recv = by_core(send)
    if first:
        recv = after(recv, *first)
    onward = (far + recv[rows:].astype(f32)).astype(bf16)
    return keep, recv, by_row(onward), onward


def after(value, *others):
    return lax.optimization_barrier((value,) + others)[0]


def phases_of(count):
    return (count - 1).bit_length()


def order_of(count, core):
    order = list(range(phases_of(count)))
    if core and len(order) > 1:
        order[0], order[1] = order[1], order[0]
    return order


def plane_pairs(count, phase):
    pairs = []
    for r in range(count):
        for s in range(4):
            pairs.append((4 * r + s, 4 * (r ^ (1 << order_of(count, s % 2)[phase])) + s))
    return pairs


def chunk_index(count, replica):
    total = jnp.zeros((), jnp.int32)
    for position in order_of(count, 0):
        total = total * 2 + ((replica >> position) & 1)
    return total


def plane_swap(value, count, phase):
    return lax.ppermute(value, ("replica", "shard"), plane_pairs(count, phase))


def split_step(keep, got):
    half = keep.shape[0] // 2
    total = (keep.astype(f32) + got.astype(f32)).astype(bf16)
    return total[:half], total[half:]


def shards(replicas, tokens, pass_ids, seg_ids, cotangent, pass_table, norm1_gain, norm1_bias, qkv_weight, out_weight,
           out_bias, norm2_gain, norm2_bias, up_weight, up_bias, down_weight, down_bias):
    rows, width = tokens.shape
    part = width // 4
    seq = seg_ids.shape[0]
    hidden = up_bias.shape[0]
    phases = phases_of(replicas)
    packed = in_kernel(replicas, width)
    rank = lax.axis_index("shard").astype(jnp.int32)
    replica = lax.axis_index("replica").astype(jnp.int32)
    me = chunk_index(replicas, replica)
    place = jnp.stack([rank, me, replica & 1])
    smem = pl.BlockSpec(memory_space=pltpu.SMEM)
    vmem = pl.BlockSpec(memory_space=pltpu.VMEM)

    def call(body, micros, outs, scratch, *args, ranked=True, aliases=None):
        specs = [smem] * ranked + [vmem] * (len(args) - ranked)
        return pl.pallas_call(
            body,
            out_shape=[jax.ShapeDtypeStruct(s, d) for s, d in outs],
            in_specs=specs,
            out_specs=[vmem] * len(outs),
            scratch_shapes=[pltpu.VMEM(s, d) for s, d in scratch],
            input_output_aliases=aliases or {},
            cost_estimate=pl.CostEstimate(flops=int(micros * 1.1e9), bytes_accessed=0, transcendentals=0),
        )(*args)

    def placed(body, values, start, shapes, blocks_of, extra, scratch, aliases):
        def at_chunk(p, s):
            return (chunk_at(s[0], s[1], replicas, p + start), 0)

        def whole(shape):
            return pl.BlockSpec(shape, lambda p, s: (0,) * len(shape))

        return pl.pallas_call(
            body,
            out_shape=[jax.ShapeDtypeStruct(s, f32) for s in shapes],
            grid_spec=pltpu.PrefetchScalarGridSpec(
                num_scalar_prefetch=1, grid=(replicas // 2,),
                in_specs=[pl.BlockSpec((1,) + values.shape[1:], lambda p, s: (p, 0, 0))]
                + [whole(e.shape) if e.ndim == 3 else pl.BlockSpec(memory_space=pl.ANY) for e in extra],
                out_specs=[pl.BlockSpec(b, at_chunk) if b else whole(s) for s, b in zip(shapes, blocks_of)],
                scratch_shapes=[pltpu.VMEM(s, f32) for s in scratch]),
            input_output_aliases=aliases,
            cost_estimate=pl.CostEstimate(flops=int(2.2e9), bytes_accessed=0, transcendentals=0),
        )(place, values, *extra)

    block, = call(pack_body, 1, [((rows + 16, width), bf16)], [], tokens, pass_ids, pass_table.T, norm1_gain, norm1_bias,
                  out_bias, norm2_gain, norm2_bias, down_bias, ranked=False)
    x1, x2 = by_core(block), by_row(block)
    own_q, near_q, far_q = call(
        qkv_blocks_body, 0, [((part, 3 * part), bf16), ((part, 3 * part), bf16), ((2 * part, 3 * part), bf16)],
        [((4, part, 3 * part), bf16)], place, after(qkv_weight, block))
    far_q = by_row(far_q)
    own_u, near_u, far_u = call(
        up_blocks_body, 0,
        [((part, hidden), bf16), ((rows + part, width), bf16), ((rows + part, width), bf16)],
        [], place, up_weight, after(cotangent, own_q))
    x2 = after(x2, own_u)
    blocks = block, x1, x2, by_core(x2)
    sin, par, nrm, unit, inv, ids = call(
        norm_body, 0,
        [((rows, width), f32), ((16, width), f32), ((seq, width), bf16), ((seq, width), bf16), ((seq, 1), f32),
         ((8, rows), f32)], [], place, *blocks)
    far_q = after(far_q, nrm)
    wq = own_q, by_core(near_q), far_q, by_core(far_q[part:])
    far_u = by_row(far_u)
    group = by_core(near_u), far_u, by_core(far_u)
    pair_u = lax.ppermute(far_u[rows:], ("replica", "shard"), [
        (4 * r + s, 4 * (r ^ 1) + (s ^ (r & 1))) for r in range(replicas) for s in range(4)])

    segc, segr = seg_ids[:, None], seg_ids[None, :]
    half_f, half_b, row_f, row_b = ((2 * rows, width), f32), ((2 * rows, width), bf16), ((rows, width), f32), ((rows, width), bf16)
    send, keep, far, qkv, ctx, lse, wq_full = call(
        front_body, 0.5,
        [half_b, row_f, row_f, ((seq, 3 * part), bf16), ((seq, part), bf16), ((8, seq), f32), ((width, 3 * part), bf16)],
        [((seq, 128), f32)],
        place, segc, segr, nrm, *wq, out_weight)
    parts = scatter_sum(send, keep, far, rows, far_u)
    mid, nrm2 = call(mid_body, 1, [row_f, row_b], [], sin, par, *parts[:2], after(parts[2], pair_u), ranked=False)
    n2 = gather_rows(nrm2)
    send, keep, far, act, pg = call(
        feed_body, 5, [half_b, row_f, row_f, ((seq, hidden), bf16), ((seq, hidden), bf16)],
        [((width, hidden), bf16)],
        place, *n2, cotangent, *group, own_u, pair_u, up_bias, down_weight)
    *back, onward = scatter_sum(send, keep, far, rows)
    feed_rows = hidden // replicas + 4 * (part // replicas)
    if packed:
        grads = [((replicas // 2, feed_rows, width), bf16)] * 2
    else:
        grads = [((hidden, width), f32), ((width, hidden), f32)]
    up_b, gkeep, gsend = call(
        functools.partial(feed_grad_body, replicas), 8, [((8, hidden), f32)] + grads,
        [((hidden, width), f32), ((width, hidden), f32)],
        place, *n2, cotangent, *group, after(act, onward), pg)
    if not packed:
        nat = chunk_at(rank, me, replicas, jnp.arange(replicas))
        downs = gkeep.reshape(replicas, -1, width)[nat]
        ups = gsend.reshape(4, replicas, -1, hidden)[rank ^ jnp.arange(4)][:, nat].transpose(1, 0, 2, 3)
        both = jnp.concatenate([downs, ups.reshape(replicas, -1, width)], 1)
        both = both.astype(bf16)
        gkeep, gsend = both[:replicas // 2], both[replicas // 2:]
    got = plane_swap(gsend, replicas, 0)
    mid_grad, branch, small_mid = call(
        mid_back_body, 1, [row_f, row_b, ((16, width), f32)], [], mid, par, after(cotangent, up_b), ids, *back, ranked=False)
    branches = gather_rows(branch)
    got = after(got, branches[1])
    for phase in range(1, max(phases - 1, 1)):
        gkeep, gsend = split_step(gkeep, got)
        got = plane_swap(gsend, replicas, phase)

    small = max(16, replicas)
    step = part // replicas + small // replicas
    qkv_rows = 4 * step + part // replicas + part // replicas // 3
    if packed:
        grads = [((replicas // 2, qkv_rows, 3 * part), bf16)] * 2
    else:
        grads = [((width, 3 * part), f32), ((part, width), f32)]
    heads = part // HD
    first, rest = range(heads - 1), range(heads - 1, heads)
    dctx, delta, grad_out, dqkv = call(
        functools.partial(attn_back_one_body, first), 6,
        [((seq, part), bf16), ((8, seq), f32), ((part, width), f32), ((seq, 3 * part), bf16)],
        [((seq, 128), f32), ((seq, HD), f32)],
        place, segc, segr, *branches, qkv, ctx, lse, out_weight)
    if phases > 1:
        gkeep, gsend = split_step(gkeep, after(got, delta))
        got = plane_swap(gsend, replicas, phases - 1)
    send, keep, far, qkeep, qsend, smalls = call(
        functools.partial(attn_back_two_body, replicas, rest), 6,
        [half_b, row_f, row_f] + grads + [((4, 16, part), f32)],
        [((seq, 3 * part), bf16), ((seq, HD), f32), ((width, 3 * part), f32), ((4, 16, part), f32)],
        place, segc, segr, qkv, lse, after(delta, gsend), dctx, dqkv, grad_out, nrm, unit, inv, ids, par, small_mid, up_b,
        wq_full)
    if not packed:
        qs = qkeep.reshape(4, replicas, -1, 3 * part)[rank ^ jnp.arange(4)][:, nat].transpose(1, 0, 2, 3)
        sm = jnp.pad(smalls, ((0, 0), (0, small - 16), (0, 2 * part)))
        sm = sm.reshape(4, replicas, -1, 3 * part)[:, nat].transpose(1, 0, 2, 3)
        os = qsend.reshape(replicas, -1, width)[nat]
        both = jnp.concatenate([
            jnp.concatenate([qs, sm], 2).reshape(replicas, -1, 3 * part), os[:, :, :3 * part],
            os[:, :, 3 * part:].reshape(replicas, -1, 3 * part)], 1)
        both = both.astype(bf16)
        qkeep, qsend = both[:replicas // 2], both[replicas // 2:]
    qgot = plane_swap(qsend, replicas, 0)
    lo, ur = hidden // replicas, part // replicas

    last_phase = phases - 1
    now = {"turn": qkeep, "feed": got, "qkv": qgot}

    def swap_piece(at):
        return by_core(at(1)), by_row(at(2)), lax.ppermute(at(3), "shard", BOTH)

    def feed_swap():
        piece = (gkeep.astype(f32) + after(now["feed"], now["turn"]).astype(f32))[0].astype(bf16)
        now["swapped"] = swap_piece(lambda k: piece[lo + k * ur:lo + (k + 1) * ur])
        now["piece"], now["turn"] = piece, now["swapped"][0]

    def feed_first():
        now["feed_all"] = jnp.concatenate(
            [now["piece"][:lo + ur]] + [after(s, now["turn"]) for s in now["swapped"]], 0)[None]
        now["feed"] = plane_swap(now["feed_all"], replicas, last_phase)
        now["turn"] = now["feed_all"]

    def feed_join(phase):
        now["feed_all"] = jnp.concatenate([now["feed_all"], after(now["feed"], now["turn"])], 0)
        now["feed"] = plane_swap(now["feed_all"], replicas, phase)
        now["turn"] = now["feed_all"]

    def qkv_split(phase):
        now["qkeep"], qsend = split_step(now.get("qkeep", qkeep), after(now["qkv"], now["turn"]))
        now["qkv"] = plane_swap(qsend, replicas, phase)
        now["turn"] = qsend

    def qkv_swap():
        low = (now.get("qkeep", qkeep).astype(f32) + after(now["qkv"], now["turn"]).astype(f32))[0].astype(bf16)
        now["quads"] = swap_piece(lambda k: low[k * step:(k + 1) * step])
        now["low"], now["turn"] = low, now["quads"][0]

    def qkv_first():
        low = now["low"]
        quads = [low[:step]] + [after(s, now["turn"]) for s in now["quads"]]
        own_small = sum(q[ur:].astype(f32) for q in quads).astype(bf16)
        now["qkv_all"] = jnp.concatenate([q[:ur] for q in quads] + [own_small, low[4 * step:]], 0)[None]
        now["qkv"] = plane_swap(now["qkv_all"], replicas, last_phase)
        now["turn"] = now["qkv_all"]

    def qkv_join(phase):
        now["qkv_all"] = jnp.concatenate([now["qkv_all"], after(now["qkv"], now["turn"])], 0)
        now["qkv"] = plane_swap(now["qkv_all"], replicas, phase)
        now["turn"] = now["qkv_all"]

    recv = by_core(send)

    def tokens_onward():
        onward = (far + after(recv, now["turn"])[rows:].astype(f32)).astype(bf16)
        now["tokens"], now["turn"] = by_row(onward), onward

    def tokens_end():
        now["tokens_grad"], = call(last_body, 1, [row_b], [], sin, par, after(mid_grad, now["turn"]), keep, recv,
                                   now["tokens"], ranked=False)
        now["turn"] = now["tokens_grad"]

    def out_start():
        now["out"] = call(feed_out_body, 0, [half_b, row_f, row_f], [], down_weight, after(act, now["turn"]),
                          ranked=False)
        now["turn"] = now["out"][0]
        now["recv_o"] = by_core(now["out"][0])

    def out_onward():
        onward = (now["out"][2] + after(now["recv_o"], now["turn"])[rows:].astype(f32)).astype(bf16)
        now["far_o"], now["turn"] = by_row(onward), onward

    def out_end():
        now["output"] = (mid + now["out"][1] + now["recv_o"][:rows].astype(f32)
                         + after(now["far_o"], now["turn"]).astype(f32) + par[10:11]).astype(bf16)
        now["turn"] = now["output"]

    def feed_place():
        if packed:
            now["filled"] = placed(place_feed_body, after(now["feed_all"], now["turn"]), 0, *feed_shapes, [], [], {})
            now["turn"] = now["filled"][0]

    def qkv_place():
        if packed:
            now["qfilled"] = placed(
                functools.partial(place_qkv_body, replicas, 0), after(now["qkv_all"], now["turn"]), 0,
                qkv_shapes[0] + [sm_shape], qkv_shapes[1] + [None], [], [stage], {})
            now["turn"] = now["qfilled"][0]

    feed_shapes = [(hidden, width), (part, 4 * hidden)], [(lo, width), (ur, 4 * hidden)]
    qkv_shapes = [(part, 12 * part), (part, width)], [(ur, 12 * part), (ur, width)]
    stage, sm_shape = (4 * ur, 3 * part), (replicas, 16 // replicas, part)
    feed_joins = [functools.partial(feed_join, p) for p in reversed(range(last_phase))]
    qkv_joins = [functools.partial(qkv_join, p) for p in reversed(range(last_phase))]
    splits = [functools.partial(qkv_split, p) for p in range(1, phases)]
    for run in ([feed_swap, tokens_onward, out_start, feed_first] + splits[:1] + [tokens_end] + splits[1:]
                + feed_joins[:-1] + [qkv_swap, out_onward, qkv_first] + feed_joins[-1:] + [feed_place]
                + qkv_joins + [out_end, qkv_place]):
        run()
    tokens_grad, output, feed_all, got, qkv_all, qgot = (
        now[n] for n in ("tokens_grad", "output", "feed_all", "feed", "qkv_all", "qkv"))

    if packed:
        final_down, final_up = placed(
            place_feed_body, after(got, now["turn"]), replicas // 2, *feed_shapes, list(now["filled"]), [], {2: 0, 3: 1})
        filled = now["qfilled"]
        shapes, split = qkv_shapes
        vectors = [pass_table.T.shape] + [(part,)] * 6 + [(hidden,)]
        final_qkv, final_out, table, g1, b1, ob, g2, b2, db, ub = placed(
            functools.partial(place_qkv_body, replicas, replicas // 2), qgot, replicas // 2, shapes + vectors,
            split + [None] * 8, [filled[2], filled[0], filled[1]], [stage, sm_shape], {3: 0, 4: 1})
    else:
        back_at = jnp.argsort(nat)
        feed_all = jnp.concatenate([feed_all, got], 0)[back_at].astype(f32)
        qkv_all = jnp.concatenate([qkv_all, qgot], 0)[back_at].astype(f32)
        final_down = feed_all[:, :lo].reshape(hidden, width)
        final_up = feed_all[:, lo:].reshape(replicas, 4, ur, hidden)[:, rank ^ jnp.arange(4)]
        final_up = final_up.transpose(0, 2, 1, 3).reshape(part, 4 * hidden)
        final_qkv = qkv_all[:, :4 * ur].reshape(replicas, 4, ur, 3, part)[:, rank ^ jnp.arange(4)]
        final_qkv = final_qkv.transpose(0, 2, 3, 1, 4).reshape(part, 12 * part)
        hi = 4 * ur + small // replicas
        mine = qkv_all[:, 4 * ur:hi, :part].reshape(small, part)
        final_out = jnp.concatenate(
            [qkv_all[:, hi:hi + ur].reshape(part, 3 * part), qkv_all[:, hi + ur:].reshape(part, part)], 1)
        table, g1, b1, ob, g2, b2, db = mine[0:5], mine[5], mine[6], mine[9], mine[7], mine[8], mine[10]
        ub = mine[11:15].reshape(hidden)
    return (output, tokens_grad, table.T, g1, b1, final_qkv, final_out, ob, g2, b2, final_up, ub, final_down, db)


def solution(mesh):
    row = P(("replica", "shard"), None)
    flat = P(("replica", "shard"))
    w2, w1 = P("shard", None), P("shard")
    return jax.shard_map(
        functools.partial(shards, mesh.shape["replica"]),
        mesh=mesh,
        in_specs=(row, flat, P("replica"), row, w2, w1, w1, w2, w2, w1, w1, w1, w2, w1, w2, w1),
        out_specs=(row, row, w2, w1, w1, w2, w2, w1, w1, w1, w2, w1, w2, w1),
        check_vma=False,
    )
```

```python
import functools

import jax
import jax.numpy as jnp
from jax import lax
from jax.experimental import pallas as pl
from jax.experimental.pallas import tpu as pltpu
from jax.sharding import PartitionSpec as P

HD = 64
epsilon = 1e-05
score_scale = 0.125
masked_score = -1e30
f32 = jnp.float32
bf16 = jnp.bfloat16

CORE = [(i, i ^ 1) for i in range(4)]
ROWY = [(i, i ^ 2) for i in range(4)]
BOTH = [(i, i ^ 3) for i in range(4)]


def contract(left, right, ld, rd):
    return lax.dot_general(left, right, (((ld,), (rd,)), ((), ())), preferred_element_type=f32)


def unit_of(values):
    centred = values - jnp.mean(values, -1, keepdims=True)
    inverse = lax.rsqrt(jnp.mean(centred * centred, -1, keepdims=True) + epsilon)
    return centred * inverse, inverse


def norm_back(grad_rows, unit_rows, inverse, gain):
    scaled = grad_rows * gain
    return inverse * (
        scaled
        - jnp.mean(scaled, -1, keepdims=True)
        - unit_rows * jnp.mean(scaled * unit_rows, -1, keepdims=True)
    )


def at_rows(index, size):
    return pl.ds(pl.multiple_of(index * size, size), size)


def pack_body(x_ref, ids_ref, table_ref, g1_ref, b1_ref, ob_ref, g2_ref, b2_ref, db_ref, out_ref):
    passes, part = table_ref.shape
    rows = ids_ref.shape[0]
    out_ref[0:rows] = x_ref[...]
    ext = jnp.zeros((16, out_ref.shape[1]), bf16)
    out_ref[rows:] = ext
    out_ref[rows:rows + passes, 0:part] = table_ref[...]
    for i, ref in enumerate((g1_ref, b1_ref, ob_ref, g2_ref, b2_ref, db_ref)):
        out_ref[rows + 5 + i:rows + 6 + i, 0:part] = ref[...].astype(f32).reshape(1, part).astype(bf16)
    out_ref[rows + 11:rows + 12, 0:rows] = ids_ref[...].astype(f32).reshape(1, rows).astype(bf16)


def norm_body(rank_ref, x0, x1, x2, x3,
              sin_ref, par_ref, nrm_ref, late_ref, unit_ref, inv_ref, ids_ref):
    rank = rank_ref[0]
    rows, width = sin_ref.shape
    part = width // 4
    ext = [b[rows:rows + 16, 0:part].astype(f32) for b in (x0, x1, x2, x3)]
    cols = []
    for j in range(4):
        acc = jnp.zeros_like(ext[0])
        for k in range(4):
            acc = jnp.where((rank ^ k) == j, ext[k], acc)
        cols.append(acc)
    par = jnp.concatenate(cols, axis=1)
    par_ref[...] = par
    table = par[0:8].astype(bf16)
    gain, bias = par[5:6], par[6:7]
    for k, b in enumerate((x0, x1, x2, x3)):
        ids = b[rows + 11:rows + 12, 0:rows].astype(f32)
        ids_ref[k:k + 1] = ids
        one = (lax.broadcasted_iota(jnp.int32, (8, rows), 0).astype(f32) == ids).astype(bf16)
        x = b[0:rows].astype(f32) + contract(one, table, 0, 0)
        if k == 0:
            sin_ref[...] = x
        unit, inverse = unit_of(x)
        at = at_rows(rank ^ k, rows)
        unit_ref[at] = unit.astype(bf16)
        inv_ref[at] = inverse
        normed = (unit * gain + bias).astype(bf16)
        nrm_ref[at] = normed
        late_ref[at] = normed


def front_body(rank_ref, segc_ref, segr_ref, nrm_ref, w0, w1, w2, w3, wout_ref,
               send_ref, keep_ref, far_ref, qkv_ref, ctx_ref, lse_ref, wq_ref, lse_s):
    rank = rank_ref[0]
    rows, width = keep_ref.shape
    part = width // 4
    for k, w in enumerate((w0[...], w1[...], w2[0:part], w3[...])):
        wq_ref[at_rows(rank ^ k, part)] = w
    qkv_ref[...] = jnp.dot(nrm_ref[...], wq_ref[...], preferred_element_type=f32).astype(bf16)
    heads = part // HD
    for h in range(heads):
        q = qkv_ref[:, h * HD:(h + 1) * HD] * jnp.asarray(score_scale, bf16)
        key = qkv_ref[:, part + h * HD:part + (h + 1) * HD]
        val = qkv_ref[:, 2 * part + h * HD:2 * part + (h + 1) * HD]
        for i in range(4):
            lo, nk = i * rows, (i + 1) * rows
            sc = contract(q[lo:nk], key[:nk], 1, 1)
            qpos = lo + lax.broadcasted_iota(jnp.int32, (rows, nk), 0)
            kpos = lax.broadcasted_iota(jnp.int32, (rows, nk), 1)
            seen = (segc_ref[lo:nk] == segr_ref[:, :nk]) & (kpos <= qpos)
            sc = jnp.where(seen, sc, masked_score)
            top = jnp.max(sc, -1, keepdims=True)
            e = jnp.exp(sc - top)
            total = jnp.sum(e, -1, keepdims=True)
            prob = (e * (1.0 / total)).astype(bf16)
            ctx_ref[lo:nk, h * HD:(h + 1) * HD] = jnp.dot(
                prob, val[:nk], preferred_element_type=f32).astype(bf16)
            lse_s[lo:nk, h:h + 1] = top + jnp.log(total)
    lse_ref[...] = lse_s[...].T[0:8]
    for i, k in enumerate((1, 3)):
        send_ref[i * rows:(i + 1) * rows] = jnp.dot(
            ctx_ref[at_rows(rank ^ k, rows)], wout_ref[...], preferred_element_type=f32).astype(bf16)
    for ref, k in ((keep_ref, 0), (far_ref, 2)):
        ref[...] = jnp.dot(ctx_ref[at_rows(rank ^ k, rows)], wout_ref[...], preferred_element_type=f32)


def mid_body(sin_ref, par_ref, keep_ref, recv_ref, yrecv_ref, mid_ref, nrm_ref):
    rows = sin_ref.shape[0]
    mid = (sin_ref[...] + keep_ref[...] + recv_ref[0:rows].astype(f32)
           + yrecv_ref[...].astype(f32) + par_ref[7:8])
    mid_ref[...] = mid
    unit, _ = unit_of(mid)
    nrm_ref[...] = (unit * par_ref[8:9] + par_ref[9:10]).astype(bf16)


def gelu_pair(v):
    c0, c1 = 0.7978845608028654, 0.044715
    sq = v * v
    t = jnp.tanh(c0 * v * (1.0 + c1 * sq))
    half = 0.5 * (1.0 + t)
    return v * half, half + 0.5 * v * (1.0 - t * t) * (c0 * (1.0 + 3.0 * c1 * sq))


def feed_body(rank_ref, n0, n1, n2, n3, c0, g1, g2, g3, u0, pair_ref, ub_ref, dw_ref,
              send_ref, keep_ref, far_ref, act_ref, pg_ref, wu_s):
    rank = rank_ref[0]
    rows, width = n0.shape
    part = width // 4
    ub_row = ub_ref[...].astype(f32).reshape(1, ub_ref.shape[0])
    side = rank_ref[2]
    wu_s[at_rows(rank, part)] = u0[...]
    wu_s[at_rows(rank ^ 1, part)] = g1[rows:]

    @pl.when(side == 0)
    def _():
        wu_s[at_rows(rank ^ 2, part)] = g2[rows:]
        wu_s[at_rows(rank ^ 3, part)] = pair_ref[...]

    @pl.when(side == 1)
    def _():
        wu_s[at_rows(rank ^ 2, part)] = pair_ref[...]
        wu_s[at_rows(rank ^ 3, part)] = g3[rows:]

    for k, (n, c) in enumerate(((n0, c0[...]), (n1, g1[0:rows]), (n2, g2[0:rows]), (n3, g3[0:rows]))):
        pre = jnp.dot(n[...], wu_s[...], preferred_element_type=f32) + ub_row
        act, slope = gelu_pair(pre)
        act_ref[k * rows:(k + 1) * rows] = act.astype(bf16)
        pg = (contract(c, dw_ref[...], 1, 1) * slope).astype(bf16)
        pg_ref[k * rows:(k + 1) * rows] = pg
        back = contract(pg, wu_s[...], 1, 1)
        if k % 2:
            send_ref[(k // 2) * rows:(k // 2 + 1) * rows] = back.astype(bf16)
        else:
            (far_ref if k else keep_ref)[...] = back


def chunk_at(rank, me, count, p):
    top, next_bit = count // 2, count // 4
    turned = p
    if next_bit:
        turned = (p % next_bit) + jnp.where((p & top) != 0, next_bit, 0) + jnp.where((p & next_bit) != 0, top, 0)
    return me ^ jnp.where((rank & 1) == 0, p, turned)


def chunk_feed(rank, me, count, gd_s, gu_s, keep_ref, gsend_ref):
    down_rows, up_rows = gd_s.shape[0] // count, gu_s.shape[0] // count // 4
    part = gu_s.shape[0] // 4

    def store(target, start):
        def one(p, carry):
            nat = chunk_at(rank, me, count, p + start)
            target[p, 0:down_rows] = gd_s[at_rows(nat, down_rows)].astype(target.dtype)
            for k in range(4):
                at = pl.ds(pl.multiple_of((rank ^ k) * part + nat * up_rows, 8), up_rows)
                lo = down_rows + k * up_rows
                target[p, lo:lo + up_rows] = gu_s[at].astype(target.dtype)
            return carry

        lax.fori_loop(0, count // 2, one, 0)

    store(keep_ref, 0)
    store(gsend_ref, count // 2)


def feed_grad_body(count, rank_ref, n0, n1, n2, n3, c0, g1, g2, g3, act_ref, pg_ref,
                   upb_ref, gkeep_ref, gsend_ref, gd_s, gu_s):
    rank, me = rank_ref[0], rank_ref[1]
    rows, width = n0.shape
    part = width // 4
    up_b = jnp.zeros((1, pg_ref.shape[1]), f32)
    blocks = ((n0, c0[...]), (n1, g1[0:rows]), (n2, g2[0:rows]), (n3, g3[0:rows]))
    for k, (n, c) in enumerate(blocks):
        act = act_ref[k * rows:(k + 1) * rows]
        pg = pg_ref[k * rows:(k + 1) * rows]
        gd = contract(act, c, 0, 0)
        gu = contract(n[...], pg, 0, 0)
        gd_s[...] = gd if k == 0 else gd_s[...] + gd
        gu_s[...] = gu if k == 0 else gu_s[...] + gu
        up_b = up_b + jnp.sum(pg.astype(f32), 0, keepdims=True)
    upb_ref[0:1] = up_b
    if in_kernel(count, width):
        chunk_feed(rank, me, count, gd_s, gu_s, gkeep_ref, gsend_ref)
    else:
        gkeep_ref[...] = gd_s[...]
        gsend_ref[...] = gu_s[...]


def feed_out_body(dw_ref, act_ref, send_ref, keep_ref, far_ref):
    rows = keep_ref.shape[0]
    for k in range(4):
        out = jnp.dot(act_ref[k * rows:(k + 1) * rows], dw_ref[...], preferred_element_type=f32)
        if k % 2:
            send_ref[(k // 2) * rows:(k // 2 + 1) * rows] = out.astype(bf16)
        else:
            (far_ref if k else keep_ref)[...] = out


def in_kernel(count, width):
    return (width // 4 // count) % 24 == 0


def mid_back_body(mid_ref, par_ref, cot_ref, ids_ref, keep_ref, recv_ref, yrecv_ref,
                  grad_ref, branch_ref, small_ref):
    rows = mid_ref.shape[0]
    back = keep_ref[...] + recv_ref[0:rows].astype(f32) + yrecv_ref[...].astype(f32)
    unit, inverse = unit_of(mid_ref[...])
    cot = cot_ref[...].astype(f32)
    grad = cot + norm_back(back, unit, inverse, par_ref[8:9])
    grad_ref[...] = grad
    branch = grad.astype(bf16)
    branch_ref[...] = branch
    one = (lax.broadcasted_iota(jnp.int32, (8, rows), 0).astype(f32) == ids_ref[0:1]).astype(bf16)
    small_ref[0:8] = contract(one, branch, 1, 0)
    small_ref[8:9] = jnp.sum(back * unit, 0, keepdims=True)
    small_ref[9:10] = jnp.sum(back, 0, keepdims=True)
    small_ref[10:11] = jnp.sum(branch.astype(f32), 0, keepdims=True)
    small_ref[11:12] = jnp.sum(cot, 0, keepdims=True)


def heads_back(heads, segc_ref, segr_ref, qkv_ref, lse_ref, delta_ref, dctx_ref, dqkv_ref, dq_s):
    part = dctx_ref.shape[1]
    total_rows = qkv_ref.shape[0]
    rows = total_rows // 4
    for h in heads:
        q = qkv_ref[:, h * HD:(h + 1) * HD] * jnp.asarray(score_scale, bf16)
        key = qkv_ref[:, part + h * HD:part + (h + 1) * HD]
        val = qkv_ref[:, 2 * part + h * HD:2 * part + (h + 1) * HD]
        dctx = dctx_ref[:, h * HD:(h + 1) * HD]
        for j in range(total_rows // rows):
            lo = j * rows
            hi = lo + rows
            nq = total_rows - lo
            sc = contract(key[lo:hi], q[lo:], 1, 1)
            kpos = lax.broadcasted_iota(jnp.int32, (rows, nq), 0)
            qpos = lax.broadcasted_iota(jnp.int32, (rows, nq), 1)
            seen = (segc_ref[lo:hi] == segr_ref[:, lo:]) & (kpos <= qpos)
            prob = jnp.where(seen, jnp.exp(sc - lse_ref[h:h + 1, lo:]), 0.0)
            dv = jnp.dot(prob.astype(bf16), dctx[lo:], preferred_element_type=f32)
            dprob = contract(val[lo:hi], dctx[lo:], 1, 1)
            ds = (prob * (dprob - delta_ref[h:h + 1, lo:])).astype(bf16)
            dk = jnp.dot(ds, q[lo:], preferred_element_type=f32)
            dq = contract(ds, key[lo:hi], 0, 0)
            if j == 0:
                dq_s[...] = dq
            else:
                dq_s[lo:] += dq
            dqkv_ref[lo:hi, part + h * HD:part + (h + 1) * HD] = dk.astype(bf16)
            dqkv_ref[lo:hi, 2 * part + h * HD:2 * part + (h + 1) * HD] = dv.astype(bf16)
        dqkv_ref[:, h * HD:(h + 1) * HD] = (dq_s[...] * score_scale).astype(bf16)


def attn_back_one_body(heads, rank_ref, segc_ref, segr_ref, g0, g1, g2, g3, qkv_ref, ctx_ref, lse_ref, wout_ref,
                       dctx_ref, delta_ref, go_ref, dqkv_ref, del_s, dq_s):
    rank = rank_ref[0]
    rows, width = g0.shape
    part = width // 4
    go = jnp.zeros((part, width), f32)
    for k, g in enumerate((g0, g1, g2, g3)):
        at = at_rows(rank ^ k, rows)
        dctx_ref[at] = contract(g[...], wout_ref[...], 1, 1).astype(bf16)
        go = go + contract(ctx_ref[at], g[...], 0, 0)
    go_ref[...] = go
    prod = dctx_ref[...].astype(f32) * ctx_ref[...].astype(f32)
    for h in range(part // HD):
        del_s[:, h:h + 1] = jnp.sum(prod[:, h * HD:(h + 1) * HD], -1, keepdims=True)
    delta_ref[...] = del_s[...].T[0:8]
    heads_back(heads, segc_ref, segr_ref, qkv_ref, lse_ref, delta_ref, dctx_ref, dqkv_ref, dq_s)


def attn_back_two_body(count, heads, rank_ref, segc_ref, segr_ref, qkv_ref, lse_ref, delta_ref, dctx_ref, dqkv_in,
                       go_s, nrm_ref, unit_ref, inv_ref, ids_ref, par_ref, smid_ref, upb_ref, wq_ref,
                       send_ref, keep_ref, far_ref, gkeep_ref, gsend_ref, sm_ref, dqkv_s,
                       dq_s, gq_s, sm_s):
    dqkv_s[...] = dqkv_in[...]
    rank, me = rank_ref[0], rank_ref[1]
    rows, width = keep_ref.shape
    part = width // 4
    heads_back(heads, segc_ref, segr_ref, qkv_ref, lse_ref, delta_ref, dctx_ref, dqkv_s, dq_s)
    gain = par_ref[5:6]
    by_pass = smid_ref[0:8]
    gain_sum = jnp.zeros((1, width), f32)
    bias_sum = jnp.zeros((1, width), f32)
    for k in range(4):
        at = at_rows(rank ^ k, rows)
        back = contract(dqkv_s[at], wq_ref[...], 1, 1)
        if k % 2:
            send_ref[(k // 2) * rows:(k // 2 + 1) * rows] = back.astype(bf16)
        else:
            (far_ref if k else keep_ref)[...] = back
        unit = unit_ref[at].astype(f32)
        gain_sum = gain_sum + jnp.sum(back * unit, 0, keepdims=True)
        bias_sum = bias_sum + jnp.sum(back, 0, keepdims=True)
        one = (lax.broadcasted_iota(jnp.int32, (8, rows), 0).astype(f32) == ids_ref[k:k + 1]).astype(bf16)
        by_pass = by_pass + contract(one, norm_back(back, unit, inv_ref[at], gain).astype(bf16), 1, 0)
    gq_s[...] = contract(nrm_ref[...], dqkv_s[...], 0, 0)
    full = jnp.concatenate([by_pass[0:5], gain_sum, bias_sum, smid_ref[8:12],
                            jnp.zeros((5, width), f32)], 0)
    up_b = upb_ref[0:1]
    mine = lax.broadcasted_iota(jnp.int32, (16, part), 0)
    for j in range(4):
        sm = full[:, j * part:(j + 1) * part]
        for i in range(4):
            sm = jnp.where((mine == 11 + i) & (rank == j), up_b[:, i * part:(i + 1) * part], sm)
        sm_s[j] = sm
    if in_kernel(count, width):
        chunk_qkv(rank, me, count, gq_s, go_s, sm_s, gkeep_ref, gsend_ref)
        sm_ref[...] = jnp.zeros(sm_ref.shape, f32)
    else:
        gkeep_ref[...] = gq_s[...]
        gsend_ref[...] = go_s[...]
        for k in range(4):
            sm_ref[k] = sm_s[rank ^ k]


def chunk_qkv(rank, me, count, gq_s, go_s, sm_s, keep_ref, gsend_ref):
    part = go_s.shape[0]
    rows = part // count
    small = 16 // count
    wide = gq_s.shape[1]
    step = rows + small

    def store(target, p, nat, place):
        for k in range(4):
            at = pl.ds(pl.multiple_of((rank ^ k) * part + nat * rows, 8), rows)
            target[place, k * step:k * step + rows] = gq_s[at].astype(target.dtype)
        out = go_s[at_rows(nat, rows)]
        third = rows // 3
        target[place, 4 * step:4 * step + rows] = out[:, 0:wide].astype(target.dtype)
        tail = out[:, wide:]
        packed = jnp.concatenate([tail[i * third:(i + 1) * third] for i in range(3)], 1)
        target[place, 4 * step + rows:4 * step + rows + third] = packed.astype(target.dtype)

    for p in range(count):
        target, place = (keep_ref, p) if p < count // 2 else (gsend_ref, p - count // 2)
        nat = chunk_at(rank, me, count, p)
        store(target, p, nat, place)
        for k in range(4):
            sm = sm_s[rank ^ k]
            row = jnp.zeros((small, part), f32)
            for c in range(count):
                row = jnp.where(nat == c, sm[c * small:(c + 1) * small], row)
            target[place, k * step + rows:k * step + rows + small, 0:part] = row.astype(target.dtype)
            target[place, k * step + rows:k * step + rows + small, part:] = jnp.zeros(
                (small, wide - part), target.dtype)


def last_body(sin_ref, par_ref, grad_ref, keep_ref, recv_ref, yrecv_ref, tok_ref):
    rows = sin_ref.shape[0]
    back = keep_ref[...] + recv_ref[0:rows].astype(f32) + yrecv_ref[...].astype(f32)
    unit, inverse = unit_of(sin_ref[...])
    tok_ref[...] = (grad_ref[...] + norm_back(back, unit, inverse, par_ref[5:6])).astype(bf16)


def place_feed_body(rank_ref, g_ref, *refs):
    down_ref, up_ref = refs[-2:]
    rank = rank_ref[0]
    down_rows = down_ref.shape[0]
    up_rows, hidden = up_ref.shape[0], up_ref.shape[1] // 4
    down_ref[...] = g_ref[0, 0:down_rows].astype(f32)
    for k in range(4):
        lo = down_rows + k * up_rows
        up_ref[:, pl.ds(pl.multiple_of((rank ^ k) * hidden, hidden), hidden)] = g_ref[0, lo:lo + up_rows].astype(f32)


def place_qkv_body(count, start, rank_ref, g_ref, *refs):
    rank, me = rank_ref[0], rank_ref[1]
    if start:
        sm_in, _, _, qkv_ref, out_ref = refs[:5]
        small_refs, stage_s, sm_s = refs[5:-2], refs[-2], refs[-1]
    else:
        qkv_ref, out_ref, sm_s, stage_s = refs
    step = pl.program_id(0)
    rows, third = out_ref.shape[0], out_ref.shape[0] // 3
    width = out_ref.shape[1]
    part = width // 4
    wide = g_ref.shape[2]
    small = 16 // count
    if start:
        @pl.when(step == 0)
        def _():
            sm_s[...] = sm_in[...]
    stage_s[...] = g_ref[0, 0:4 * rows].astype(f32)
    for j in range(4):
        block = stage_s[at_rows(rank ^ j, rows)]
        for i in range(3):
            qkv_ref[:, i * width + j * part:i * width + (j + 1) * part] = block[:, i * part:(i + 1) * part]
    sm_s[chunk_at(rank, me, count, step + start)] = g_ref[0, 4 * rows:4 * rows + small, 0:part].astype(f32)
    lo = 4 * rows + small
    out_ref[:, 0:wide] = g_ref[0, lo:lo + rows].astype(f32)
    packed = g_ref[0, lo + rows:lo + rows + third].astype(f32)
    out_ref[:, wide:] = jnp.concatenate([packed[:, i * part:(i + 1) * part] for i in range(3)], 0)
    if start:
        @pl.when(step == pl.num_programs(0) - 1)
        def _():
            rows_of = [sm_s[i // small, i % small:i % small + 1] for i in range(16)]
            table_ref = small_refs[0]
            for i in range(table_ref.shape[0]):
                table_ref[i:i + 1] = rows_of[i]
            for ref, i in zip(small_refs[1:7], (5, 6, 9, 7, 8, 10)):
                ref[...] = rows_of[i].reshape(part)
            for i in range(4):
                small_refs[7][i * part:(i + 1) * part] = rows_of[11 + i].reshape(part)


def qkv_blocks_body(rank_ref, w_ref, own_ref, near_ref, far_ref, stage_s):
    rank = rank_ref[0]
    part = w_ref.shape[0]
    for t in range(4):
        stage_s[t] = jnp.concatenate(
            [w_ref[:, (4 * i + t) * part:(4 * i + t + 1) * part] for i in range(3)], 1)
    own_ref[...] = stage_s[rank]
    near_ref[...] = stage_s[rank ^ 1]
    far_ref[0:part] = stage_s[rank ^ 2]
    far_ref[part:] = stage_s[rank ^ 3]


def up_blocks_body(rank_ref, w_ref, cot_ref, own_ref, near_ref, far_ref):
    rank, side = rank_ref[0], rank_ref[2]
    rows = cot_ref.shape[0]
    hidden = own_ref.shape[1]

    def block(k):
        return w_ref[:, pl.ds(pl.multiple_of((rank ^ k) * hidden, hidden), hidden)]

    own_ref[...] = block(0)
    near_ref[0:rows] = cot_ref[...]
    near_ref[rows:] = block(1)
    far_ref[0:rows] = cot_ref[...]
    far_ref[rows:] = block(2 + side)


def by_core(value):
    return lax.ppermute(value, "shard", CORE)


def by_row(value):
    return lax.ppermute(value, "shard", ROWY)


def gather_rows(block):
    far = by_row(block)
    return block, by_core(block), far, by_core(far)


def scatter_sum(send, keep, far, rows):
    recv = by_core(send)
    onward = (far + recv[rows:].astype(f32)).astype(bf16)
    return keep, recv, by_row(onward), onward


def after(value, *others):
    return lax.optimization_barrier((value,) + others)[0]


def phases_of(count):
    return (count - 1).bit_length()


def order_of(count, core):
    order = list(range(phases_of(count)))
    if core and len(order) > 1:
        order[0], order[1] = order[1], order[0]
    return order


def plane_pairs(count, phase):
    pairs = []
    for r in range(count):
        for s in range(4):
            pairs.append((4 * r + s, 4 * (r ^ (1 << order_of(count, s % 2)[phase])) + s))
    return pairs


def chunk_index(count, replica):
    total = jnp.zeros((), jnp.int32)
    for position in order_of(count, 0):
        total = total * 2 + ((replica >> position) & 1)
    return total


def plane_swap(value, count, phase):
    return lax.ppermute(value, ("replica", "shard"), plane_pairs(count, phase))


def split_step(keep, got):
    half = keep.shape[0] // 2
    total = (keep.astype(f32) + got.astype(f32)).astype(bf16)
    return total[:half], total[half:]


def shards(replicas, tokens, pass_ids, seg_ids, cotangent, pass_table, norm1_gain, norm1_bias, qkv_weight, out_weight,
           out_bias, norm2_gain, norm2_bias, up_weight, up_bias, down_weight, down_bias):
    rows, width = tokens.shape
    part = width // 4
    seq = seg_ids.shape[0]
    hidden = up_bias.shape[0]
    phases = phases_of(replicas)
    packed = in_kernel(replicas, width)
    rank = lax.axis_index("shard").astype(jnp.int32)
    replica = lax.axis_index("replica").astype(jnp.int32)
    me = chunk_index(replicas, replica)
    place = jnp.stack([rank, me, replica & 1])
    smem = pl.BlockSpec(memory_space=pltpu.SMEM)
    vmem = pl.BlockSpec(memory_space=pltpu.VMEM)

    def call(body, micros, outs, scratch, *args, ranked=True, aliases=None, wide=False):
        specs = [smem] * ranked + [vmem] * (len(args) - ranked)
        return pl.pallas_call(
            body,
            out_shape=[jax.ShapeDtypeStruct(s, d) for s, d in outs],
            in_specs=specs,
            out_specs=[vmem] * len(outs),
            scratch_shapes=[pltpu.VMEM(s, d) for s, d in scratch],
            input_output_aliases=aliases or {},
            compiler_params=pltpu.CompilerParams(vmem_limit_bytes=None if wide else 24 * 2**20),
            cost_estimate=pl.CostEstimate(flops=int(micros * 1.1e9), bytes_accessed=0, transcendentals=0),
        )(*args)

    def placed(body, values, start, shapes, blocks_of, extra, scratch, aliases):
        def at_chunk(p, s):
            return (chunk_at(s[0], s[1], replicas, p + start), 0)

        def whole(shape):
            return pl.BlockSpec(shape, lambda p, s: (0,) * len(shape))

        return pl.pallas_call(
            body,
            out_shape=[jax.ShapeDtypeStruct(s, f32) for s in shapes],
            grid_spec=pltpu.PrefetchScalarGridSpec(
                num_scalar_prefetch=1, grid=(replicas // 2,),
                in_specs=[pl.BlockSpec((1,) + values.shape[1:], lambda p, s: (p, 0, 0))]
                + [whole(e.shape) if e.ndim == 3 else pl.BlockSpec(memory_space=pl.ANY) for e in extra],
                out_specs=[pl.BlockSpec(b, at_chunk) if b else whole(s) for s, b in zip(shapes, blocks_of)],
                scratch_shapes=[pltpu.VMEM(s, f32) for s in scratch]),
            input_output_aliases=aliases,
            compiler_params=pltpu.CompilerParams(vmem_limit_bytes=24 * 2**20),
            cost_estimate=pl.CostEstimate(flops=int(2.2e9), bytes_accessed=0, transcendentals=0),
        )(place, values, *extra)

    block, = call(pack_body, 1, [((rows + 16, width), bf16)], [], tokens, pass_ids, pass_table.T, norm1_gain, norm1_bias,
                  out_bias, norm2_gain, norm2_bias, down_bias, ranked=False, wide=True)
    x1, x2 = by_core(block), by_row(block)
    own_q, near_q, far_q = call(
        qkv_blocks_body, 0, [((part, 3 * part), bf16), ((part, 3 * part), bf16), ((2 * part, 3 * part), bf16)],
        [((4, part, 3 * part), bf16)], place, after(qkv_weight, block))
    far_q = by_row(far_q)
    own_u, near_u, far_u = call(
        up_blocks_body, 0,
        [((part, hidden), bf16), ((rows + part, width), bf16), ((rows + part, width), bf16)],
        [], place, up_weight, after(cotangent, own_q))
    x2 = after(x2, own_u)
    blocks = block, x1, x2, by_core(x2)
    sin, par, nrm, nrm_late, unit, inv, ids = call(
        norm_body, 0,
        [((rows, width), f32), ((16, width), f32), ((seq, width), bf16), ((seq, width), bf16), ((seq, width), bf16),
         ((seq, 1), f32), ((8, rows), f32)], [], place, *blocks)
    far_q = after(far_q, nrm)
    wq = own_q, by_core(near_q), far_q, by_core(far_q[part:])
    far_u = by_row(far_u)
    group = by_core(near_u), far_u, by_core(far_u)
    pair_u = lax.ppermute(far_u[rows:], ("replica", "shard"), [
        (4 * r + s, 4 * (r ^ 1) + (s ^ (r & 1))) for r in range(replicas) for s in range(4)])

    segc, segr = seg_ids[:, None], seg_ids[None, :]
    half_f, half_b, row_f, row_b = ((2 * rows, width), f32), ((2 * rows, width), bf16), ((rows, width), f32), ((rows, width), bf16)
    send, keep, far, qkv, ctx, lse, wq_full = call(
        front_body, 4,
        [half_b, row_f, row_f, ((seq, 3 * part), bf16), ((seq, part), bf16), ((8, seq), f32), ((width, 3 * part), bf16)],
        [((seq, 128), f32)],
        place, segc, segr, nrm, *wq, out_weight)
    parts = scatter_sum(after(send, far_u), keep, far, rows)
    mid, nrm2 = call(mid_body, 1, [row_f, row_b], [], sin, par, *parts[:2], after(parts[2], pair_u), ranked=False)
    n2 = gather_rows(nrm2)
    send, keep, far, act, pg = call(
        feed_body, 5, [half_b, row_f, row_f, ((seq, hidden), bf16), ((seq, hidden), bf16)],
        [((width, hidden), bf16)],
        place, *n2, cotangent, *group, own_u, pair_u, up_bias, down_weight)
    *back, onward = scatter_sum(send, keep, far, rows)
    feed_rows = hidden // replicas + 4 * (part // replicas)
    if packed:
        grads = [((replicas // 2, feed_rows, width), bf16)] * 2
    else:
        grads = [((hidden, width), f32), ((width, hidden), f32)]
    up_b, gkeep, gsend = call(
        functools.partial(feed_grad_body, replicas), 8, [((8, hidden), f32)] + grads,
        [((hidden, width), f32), ((width, hidden), f32)],
        place, *n2, cotangent, *group, after(act, onward), pg)
    if not packed:
        nat = chunk_at(rank, me, replicas, jnp.arange(replicas))
        downs = gkeep.reshape(replicas, -1, width)[nat]
        ups = gsend.reshape(4, replicas, -1, hidden)[rank ^ jnp.arange(4)][:, nat].transpose(1, 0, 2, 3)
        both = jnp.concatenate([downs, ups.reshape(replicas, -1, width)], 1)
        both = both.astype(bf16)
        gkeep, gsend = both[:replicas // 2], both[replicas // 2:]
    got = plane_swap(gsend, replicas, 0)
    mid_grad, branch, small_mid = call(
        mid_back_body, 1, [row_f, row_b, ((16, width), f32)], [], mid, par, after(cotangent, up_b), ids, *back, ranked=False)
    branches = gather_rows(branch)
    got = after(got, branches[1])
    for phase in range(1, max(phases - 1, 1)):
        gkeep, gsend = split_step(gkeep, got)
        got = plane_swap(gsend, replicas, phase)

    small = max(16, replicas)
    step = part // replicas + small // replicas
    qkv_rows = 4 * step + part // replicas + part // replicas // 3
    if packed:
        grads = [((replicas // 2, qkv_rows, 3 * part), bf16)] * 2
    else:
        grads = [((width, 3 * part), f32), ((part, width), f32)]
    heads = part // HD
    first, rest = range(heads - 1), range(heads - 1, heads)
    dctx, delta, grad_out, dqkv = call(
        functools.partial(attn_back_one_body, first), 6,
        [((seq, part), bf16), ((8, seq), f32), ((part, width), f32), ((seq, 3 * part), bf16)],
        [((seq, 128), f32), ((seq, HD), f32)],
        place, segc, segr, *branches, qkv, ctx, lse, out_weight)
    if phases > 1:
        gkeep, gsend = split_step(gkeep, after(got, delta))
        got = plane_swap(gsend, replicas, phases - 1)
    send, keep, far, qkeep, qsend, smalls = call(
        functools.partial(attn_back_two_body, replicas, rest), 6,
        [half_b, row_f, row_f] + grads + [((4, 16, part), f32)],
        [((seq, 3 * part), bf16), ((seq, HD), f32), ((width, 3 * part), f32), ((4, 16, part), f32)],
        place, segc, segr, qkv, lse, after(delta, gsend), dctx, dqkv, grad_out, nrm_late, unit, inv, ids, par, small_mid, up_b,
        wq_full)
    if not packed:
        qs = qkeep.reshape(4, replicas, -1, 3 * part)[rank ^ jnp.arange(4)][:, nat].transpose(1, 0, 2, 3)
        sm = jnp.pad(smalls, ((0, 0), (0, small - 16), (0, 2 * part)))
        sm = sm.reshape(4, replicas, -1, 3 * part)[:, nat].transpose(1, 0, 2, 3)
        os = qsend.reshape(replicas, -1, width)[nat]
        both = jnp.concatenate([
            jnp.concatenate([qs, sm], 2).reshape(replicas, -1, 3 * part), os[:, :, :3 * part],
            os[:, :, 3 * part:].reshape(replicas, -1, 3 * part)], 1)
        both = both.astype(bf16)
        qkeep, qsend = both[:replicas // 2], both[replicas // 2:]
    qgot = plane_swap(qsend, replicas, 0)
    lo, ur = hidden // replicas, part // replicas

    last_phase = phases - 1
    now = {"turn": qkeep, "feed": got, "qkv": qgot}

    def swap_piece(at):
        return by_core(at(1)), by_row(at(2)), lax.ppermute(at(3), "shard", BOTH)

    def feed_swap():
        piece = (gkeep.astype(f32) + after(now["feed"], now["turn"]).astype(f32))[0].astype(bf16)
        now["swapped"] = swap_piece(lambda k: piece[lo + k * ur:lo + (k + 1) * ur])
        now["piece"], now["turn"] = piece, now["swapped"][0]

    def feed_first():
        now["feed_all"] = jnp.concatenate(
            [now["piece"][:lo + ur]] + [after(s, now["turn"]) for s in now["swapped"]], 0)[None]
        now["feed"] = plane_swap(now["feed_all"], replicas, last_phase)
        now["turn"] = now["feed_all"]

    def feed_join(phase):
        now["feed_all"] = jnp.concatenate([now["feed_all"], after(now["feed"], now["turn"])], 0)
        now["feed"] = plane_swap(now["feed_all"], replicas, phase)
        now["turn"] = now["feed_all"]

    def qkv_split(phase):
        now["qkeep"], qsend = split_step(now.get("qkeep", qkeep), after(now["qkv"], now["turn"]))
        now["qkv"] = plane_swap(qsend, replicas, phase)
        now["turn"] = qsend

    def qkv_swap():
        low = (now.get("qkeep", qkeep).astype(f32) + after(now["qkv"], now["turn"]).astype(f32))[0].astype(bf16)
        now["quads"] = swap_piece(lambda k: low[k * step:(k + 1) * step])
        now["low"], now["turn"] = low, now["quads"][0]

    def qkv_first():
        low = now["low"]
        quads = [low[:step]] + [after(s, now["turn"]) for s in now["quads"]]
        own_small = sum(q[ur:].astype(f32) for q in quads).astype(bf16)
        now["qkv_all"] = jnp.concatenate([q[:ur] for q in quads] + [own_small, low[4 * step:]], 0)[None]
        now["qkv"] = plane_swap(now["qkv_all"], replicas, last_phase)
        now["turn"] = now["qkv_all"]

    def qkv_join(phase):
        now["qkv_all"] = jnp.concatenate([now["qkv_all"], after(now["qkv"], now["turn"])], 0)
        now["qkv"] = plane_swap(now["qkv_all"], replicas, phase)
        now["turn"] = now["qkv_all"]

    recv = by_core(send)

    def tokens_onward():
        onward = (far + after(recv, now["turn"])[rows:].astype(f32)).astype(bf16)
        now["tokens"], now["turn"] = by_row(onward), onward

    def tokens_end():
        now["tokens_grad"], = call(last_body, 1, [row_b], [], sin, par, after(mid_grad, now["turn"]), keep, recv,
                                   now["tokens"], ranked=False)
        now["turn"] = now["tokens_grad"]

    def out_start():
        now["out"] = call(feed_out_body, 0, [half_b, row_f, row_f], [], down_weight, after(act, now["turn"]),
                          ranked=False)
        now["turn"] = now["out"][0]
        now["recv_o"] = by_core(now["out"][0])

    def out_onward():
        onward = (now["out"][2] + after(now["recv_o"], now["turn"])[rows:].astype(f32)).astype(bf16)
        now["far_o"], now["turn"] = by_row(onward), onward

    def out_end():
        now["output"] = (mid + now["out"][1] + now["recv_o"][:rows].astype(f32)
                         + after(now["far_o"], now["turn"]).astype(f32) + par[10:11]).astype(bf16)
        now["turn"] = now["output"]

    def feed_place():
        if packed:
            now["filled"] = placed(place_feed_body, after(now["feed_all"], now["turn"]), 0, *feed_shapes, [], [], {})
            now["turn"] = now["filled"][0]

    def qkv_place():
        if packed:
            now["qfilled"] = placed(
                functools.partial(place_qkv_body, replicas, 0), after(now["qkv_all"], now["turn"]), 0,
                qkv_shapes[0] + [sm_shape], qkv_shapes[1] + [None], [], [stage], {})
            now["turn"] = now["qfilled"][0]

    feed_shapes = [(hidden, width), (part, 4 * hidden)], [(lo, width), (ur, 4 * hidden)]
    qkv_shapes = [(part, 12 * part), (part, width)], [(ur, 12 * part), (ur, width)]
    stage, sm_shape = (4 * ur, 3 * part), (replicas, 16 // replicas, part)
    feed_joins = [functools.partial(feed_join, p) for p in reversed(range(last_phase))]
    qkv_joins = [functools.partial(qkv_join, p) for p in reversed(range(last_phase))]
    splits = [functools.partial(qkv_split, p) for p in range(1, phases)]
    for run in ([feed_swap, tokens_onward, out_start, feed_first] + splits[:1] + [tokens_end] + splits[1:]
                + feed_joins[:-1] + [qkv_swap, out_onward, qkv_first] + feed_joins[-1:] + [feed_place]
                + qkv_joins + [out_end, qkv_place]):
        run()
    tokens_grad, output, feed_all, got, qkv_all, qgot = (
        now[n] for n in ("tokens_grad", "output", "feed_all", "feed", "qkv_all", "qkv"))

    if packed:
        final_down, final_up = placed(
            place_feed_body, after(got, now["turn"]), replicas // 2, *feed_shapes, list(now["filled"]), [], {2: 0, 3: 1})
        filled = now["qfilled"]
        shapes, split = qkv_shapes
        vectors = [pass_table.T.shape] + [(part,)] * 6 + [(hidden,)]
        final_qkv, final_out, table, g1, b1, ob, g2, b2, db, ub = placed(
            functools.partial(place_qkv_body, replicas, replicas // 2), qgot, replicas // 2, shapes + vectors,
            split + [None] * 8, [filled[2], filled[0], filled[1]], [stage, sm_shape], {3: 0, 4: 1})
    else:
        back_at = jnp.argsort(nat)
        feed_all = jnp.concatenate([feed_all, got], 0)[back_at].astype(f32)
        qkv_all = jnp.concatenate([qkv_all, qgot], 0)[back_at].astype(f32)
        final_down = feed_all[:, :lo].reshape(hidden, width)
        final_up = feed_all[:, lo:].reshape(replicas, 4, ur, hidden)[:, rank ^ jnp.arange(4)]
        final_up = final_up.transpose(0, 2, 1, 3).reshape(part, 4 * hidden)
        final_qkv = qkv_all[:, :4 * ur].reshape(replicas, 4, ur, 3, part)[:, rank ^ jnp.arange(4)]
        final_qkv = final_qkv.transpose(0, 2, 3, 1, 4).reshape(part, 12 * part)
        hi = 4 * ur + small // replicas
        mine = qkv_all[:, 4 * ur:hi, :part].reshape(small, part)
        final_out = jnp.concatenate(
            [qkv_all[:, hi:hi + ur].reshape(part, 3 * part), qkv_all[:, hi + ur:].reshape(part, part)], 1)
        table, g1, b1, ob, g2, b2, db = mine[0:5], mine[5], mine[6], mine[9], mine[7], mine[8], mine[10]
        ub = mine[11:15].reshape(hidden)
    return (output, tokens_grad, table.T, g1, b1, final_qkv, final_out, ob, g2, b2, final_up, ub, final_down, db)


def solution(mesh):
    row = P(("replica", "shard"), None)
    flat = P(("replica", "shard"))
    w2, w1 = P("shard", None), P("shard")
    return jax.shard_map(
        functools.partial(shards, mesh.shape["replica"]),
        mesh=mesh,
        in_specs=(row, flat, P("replica"), row, w2, w1, w1, w2, w2, w1, w1, w1, w2, w1, w2, w1),
        out_specs=(row, row, w2, w1, w1, w2, w2, w1, w1, w1, w2, w1, w2, w1),
        check_vma=False,
    )
```

```python
import functools

import jax
import jax.numpy as jnp
from jax import lax
from jax.experimental import pallas as pl
from jax.experimental.pallas import tpu as pltpu
from jax.sharding import PartitionSpec as P

HD = 64
epsilon = 1e-05
score_scale = 0.125
masked_score = -1e30
f32 = jnp.float32
bf16 = jnp.bfloat16

CORE = [(i, i ^ 1) for i in range(4)]
ROWY = [(i, i ^ 2) for i in range(4)]
BOTH = [(i, i ^ 3) for i in range(4)]


def contract(left, right, ld, rd):
    return lax.dot_general(left, right, (((ld,), (rd,)), ((), ())), preferred_element_type=f32)


def unit_of(values):
    centred = values - jnp.mean(values, -1, keepdims=True)
    inverse = lax.rsqrt(jnp.mean(centred * centred, -1, keepdims=True) + epsilon)
    return centred * inverse, inverse


def norm_back(grad_rows, unit_rows, inverse, gain):
    scaled = grad_rows * gain
    return inverse * (
        scaled
        - jnp.mean(scaled, -1, keepdims=True)
        - unit_rows * jnp.mean(scaled * unit_rows, -1, keepdims=True)
    )


def at_rows(index, size):
    return pl.ds(pl.multiple_of(index * size, size), size)


def pack_body(x_ref, ids_ref, table_ref, g1_ref, b1_ref, ob_ref, g2_ref, b2_ref, db_ref, out_ref):
    passes, part = table_ref.shape
    rows = ids_ref.shape[0]
    out_ref[0:rows] = x_ref[...]
    ext = jnp.zeros((16, out_ref.shape[1]), bf16)
    out_ref[rows:] = ext
    out_ref[rows:rows + passes, 0:part] = table_ref[...]
    for i, ref in enumerate((g1_ref, b1_ref, ob_ref, g2_ref, b2_ref, db_ref)):
        out_ref[rows + 5 + i:rows + 6 + i, 0:part] = ref[...].astype(f32).reshape(1, part).astype(bf16)
    out_ref[rows + 11:rows + 12, 0:rows] = ids_ref[...].astype(f32).reshape(1, rows).astype(bf16)


def norm_body(rank_ref, x0, x1, x2, x3,
              sin_ref, par_ref, nrm_ref, late_ref, unit_ref, inv_ref, ids_ref):
    rank = rank_ref[0]
    rows, width = sin_ref.shape
    part = width // 4
    ext = [b[rows:rows + 16, 0:part].astype(f32) for b in (x0, x1, x2, x3)]
    cols = []
    for j in range(4):
        acc = jnp.zeros_like(ext[0])
        for k in range(4):
            acc = jnp.where((rank ^ k) == j, ext[k], acc)
        cols.append(acc)
    par = jnp.concatenate(cols, axis=1)
    par_ref[...] = par
    table = par[0:8].astype(bf16)
    gain, bias = par[5:6], par[6:7]
    for k, b in enumerate((x0, x1, x2, x3)):
        ids = b[rows + 11:rows + 12, 0:rows].astype(f32)
        ids_ref[k:k + 1] = ids
        one = (lax.broadcasted_iota(jnp.int32, (8, rows), 0).astype(f32) == ids).astype(bf16)
        x = b[0:rows].astype(f32) + contract(one, table, 0, 0)
        if k == 0:
            sin_ref[...] = x
        unit, inverse = unit_of(x)
        at = at_rows(rank ^ k, rows)
        unit_ref[at] = unit.astype(bf16)
        inv_ref[at] = inverse
        normed = (unit * gain + bias).astype(bf16)
        nrm_ref[at] = normed
        late_ref[at] = normed


def front_body(rank_ref, segc_ref, segr_ref, nrm_ref, w0, w1, w2, w3, wout_ref,
               send_ref, keep_ref, far_ref, qkv_ref, ctx_ref, lse_ref, wq_ref, lse_s, head_s, ctx_s, top_s):
    rank = rank_ref[0]
    rows, width = keep_ref.shape
    part = width // 4
    for k, w in enumerate((w0[...], w1[...], w2[0:part], w3[...])):
        wq_ref[at_rows(rank ^ k, part)] = w
    qkv_ref[...] = jnp.dot(nrm_ref[...], wq_ref[...], preferred_element_type=f32).astype(bf16)
    heads = part // HD
    total_rows = nrm_ref.shape[0]
    for i in range(3 * heads):
        head = qkv_ref[:, i * HD:(i + 1) * HD]
        head_s[i] = head * jnp.asarray(score_scale, bf16) if i < heads else head

    def one_head(h, carry):
        q, key, val = head_s[h], head_s[heads + h], head_s[2 * heads + h]
        for i in range(total_rows // rows):
            lo, nk = i * rows, (i + 1) * rows
            sc = contract(q[lo:nk], key[:nk], 1, 1)
            qpos = lo + lax.broadcasted_iota(jnp.int32, (rows, nk), 0)
            kpos = lax.broadcasted_iota(jnp.int32, (rows, nk), 1)
            seen = (segc_ref[lo:nk] == segr_ref[:, :nk]) & (kpos <= qpos)
            sc = jnp.where(seen, sc, masked_score)
            top = jnp.max(sc, -1, keepdims=True)
            e = jnp.exp(sc - top)
            total = jnp.sum(e, -1, keepdims=True)
            prob = (e * (1.0 / total)).astype(bf16)
            ctx_s[h, lo:nk] = jnp.dot(prob, val[:nk], preferred_element_type=f32).astype(bf16)
            top_s[h, lo:nk] = top + jnp.log(total)
        return carry

    lax.fori_loop(0, heads, one_head, 0)
    for h in range(heads):
        ctx_ref[:, h * HD:(h + 1) * HD] = ctx_s[h]
        lse_s[:, h:h + 1] = top_s[h]
    lse_ref[...] = lse_s[...].T[0:8]
    for i, k in enumerate((1, 3)):
        send_ref[i * rows:(i + 1) * rows] = jnp.dot(
            ctx_ref[at_rows(rank ^ k, rows)], wout_ref[...], preferred_element_type=f32).astype(bf16)
    for ref, k in ((keep_ref, 0), (far_ref, 2)):
        ref[...] = jnp.dot(ctx_ref[at_rows(rank ^ k, rows)], wout_ref[...], preferred_element_type=f32)


def mid_body(sin_ref, par_ref, keep_ref, recv_ref, yrecv_ref, mid_ref, nrm_ref):
    rows = sin_ref.shape[0]
    mid = (sin_ref[...] + keep_ref[...] + recv_ref[0:rows].astype(f32)
           + yrecv_ref[...].astype(f32) + par_ref[7:8])
    mid_ref[...] = mid
    unit, _ = unit_of(mid)
    nrm_ref[...] = (unit * par_ref[8:9] + par_ref[9:10]).astype(bf16)


def gelu_pair(v):
    c0, c1 = 0.7978845608028654, 0.044715
    sq = v * v
    t = jnp.tanh(c0 * v * (1.0 + c1 * sq))
    half = 0.5 * (1.0 + t)
    return v * half, half + 0.5 * v * (1.0 - t * t) * (c0 * (1.0 + 3.0 * c1 * sq))


def feed_body(rank_ref, n0, n1, n2, n3, c0, g1, g2, g3, u0, pair_ref, ub_ref, dw_ref,
              send_ref, keep_ref, far_ref, act_ref, pg_ref, wu_s):
    rank = rank_ref[0]
    rows, width = n0.shape
    part = width // 4
    ub_row = ub_ref[...].astype(f32).reshape(1, ub_ref.shape[0])
    side = rank_ref[2]
    wu_s[at_rows(rank, part)] = u0[...]
    wu_s[at_rows(rank ^ 1, part)] = g1[rows:]

    @pl.when(side == 0)
    def _():
        wu_s[at_rows(rank ^ 2, part)] = g2[rows:]
        wu_s[at_rows(rank ^ 3, part)] = pair_ref[...]

    @pl.when(side == 1)
    def _():
        wu_s[at_rows(rank ^ 2, part)] = pair_ref[...]
        wu_s[at_rows(rank ^ 3, part)] = g3[rows:]

    for k, (n, c) in enumerate(((n0, c0[...]), (n1, g1[0:rows]), (n2, g2[0:rows]), (n3, g3[0:rows]))):
        pre = jnp.dot(n[...], wu_s[...], preferred_element_type=f32) + ub_row
        act, slope = gelu_pair(pre)
        act_ref[k * rows:(k + 1) * rows] = act.astype(bf16)
        pg = (contract(c, dw_ref[...], 1, 1) * slope).astype(bf16)
        pg_ref[k * rows:(k + 1) * rows] = pg
        back = contract(pg, wu_s[...], 1, 1)
        if k % 2:
            send_ref[(k // 2) * rows:(k // 2 + 1) * rows] = back.astype(bf16)
        else:
            (far_ref if k else keep_ref)[...] = back


def chunk_at(rank, me, count, p):
    top, next_bit = count // 2, count // 4
    turned = p
    if next_bit:
        turned = (p % next_bit) + jnp.where((p & top) != 0, next_bit, 0) + jnp.where((p & next_bit) != 0, top, 0)
    return me ^ jnp.where((rank & 1) == 0, p, turned)


def chunk_feed(rank, me, count, gd_s, gu_s, keep_ref, gsend_ref):
    down_rows, up_rows = gd_s.shape[0] // count, gu_s.shape[0] // count // 4
    part = gu_s.shape[0] // 4

    def store(target, start):
        def one(p, carry):
            nat = chunk_at(rank, me, count, p + start)
            target[p, 0:down_rows] = gd_s[at_rows(nat, down_rows)].astype(target.dtype)
            for k in range(4):
                at = pl.ds(pl.multiple_of((rank ^ k) * part + nat * up_rows, 8), up_rows)
                lo = down_rows + k * up_rows
                target[p, lo:lo + up_rows] = gu_s[at].astype(target.dtype)
            return carry

        lax.fori_loop(0, count // 2, one, 0)

    store(keep_ref, 0)
    store(gsend_ref, count // 2)


def feed_grad_body(count, rank_ref, n0, n1, n2, n3, c0, g1, g2, g3, act_ref, pg_ref,
                   upb_ref, gkeep_ref, gsend_ref, gd_s, gu_s):
    rank, me = rank_ref[0], rank_ref[1]
    rows, width = n0.shape
    part = width // 4
    up_b = jnp.zeros((1, pg_ref.shape[1]), f32)
    blocks = ((n0, c0[...]), (n1, g1[0:rows]), (n2, g2[0:rows]), (n3, g3[0:rows]))
    for k, (n, c) in enumerate(blocks):
        act = act_ref[k * rows:(k + 1) * rows]
        pg = pg_ref[k * rows:(k + 1) * rows]
        gd = contract(act, c, 0, 0)
        gu = contract(n[...], pg, 0, 0)
        gd_s[...] = gd if k == 0 else gd_s[...] + gd
        gu_s[...] = gu if k == 0 else gu_s[...] + gu
        up_b = up_b + jnp.sum(pg.astype(f32), 0, keepdims=True)
    upb_ref[0:1] = up_b
    if in_kernel(count, width):
        chunk_feed(rank, me, count, gd_s, gu_s, gkeep_ref, gsend_ref)
    else:
        gkeep_ref[...] = gd_s[...]
        gsend_ref[...] = gu_s[...]


def feed_out_body(dw_ref, act_ref, send_ref, keep_ref, far_ref):
    rows = keep_ref.shape[0]
    for k in range(4):
        out = jnp.dot(act_ref[k * rows:(k + 1) * rows], dw_ref[...], preferred_element_type=f32)
        if k % 2:
            send_ref[(k // 2) * rows:(k // 2 + 1) * rows] = out.astype(bf16)
        else:
            (far_ref if k else keep_ref)[...] = out


def in_kernel(count, width):
    return (width // 4 // count) % 24 == 0


def mid_back_body(mid_ref, par_ref, cot_ref, ids_ref, keep_ref, recv_ref, yrecv_ref,
                  grad_ref, branch_ref, small_ref):
    rows = mid_ref.shape[0]
    back = keep_ref[...] + recv_ref[0:rows].astype(f32) + yrecv_ref[...].astype(f32)
    unit, inverse = unit_of(mid_ref[...])
    cot = cot_ref[...].astype(f32)
    grad = cot + norm_back(back, unit, inverse, par_ref[8:9])
    grad_ref[...] = grad
    branch = grad.astype(bf16)
    branch_ref[...] = branch
    one = (lax.broadcasted_iota(jnp.int32, (8, rows), 0).astype(f32) == ids_ref[0:1]).astype(bf16)
    small_ref[0:8] = contract(one, branch, 1, 0)
    small_ref[8:9] = jnp.sum(back * unit, 0, keepdims=True)
    small_ref[9:10] = jnp.sum(back, 0, keepdims=True)
    small_ref[10:11] = jnp.sum(branch.astype(f32), 0, keepdims=True)
    small_ref[11:12] = jnp.sum(cot, 0, keepdims=True)


def heads_back(heads, segc_ref, segr_ref, qkv_ref, lse_ref, delta_ref, dctx_ref, dqkv_ref, dq_s):
    part = dctx_ref.shape[1]
    total_rows = qkv_ref.shape[0]
    rows = total_rows // 4
    for h in heads:
        q = qkv_ref[:, h * HD:(h + 1) * HD] * jnp.asarray(score_scale, bf16)
        key = qkv_ref[:, part + h * HD:part + (h + 1) * HD]
        val = qkv_ref[:, 2 * part + h * HD:2 * part + (h + 1) * HD]
        dctx = dctx_ref[:, h * HD:(h + 1) * HD]
        for j in range(total_rows // rows):
            lo = j * rows
            hi = lo + rows
            nq = total_rows - lo
            sc = contract(key[lo:hi], q[lo:], 1, 1)
            kpos = lax.broadcasted_iota(jnp.int32, (rows, nq), 0)
            qpos = lax.broadcasted_iota(jnp.int32, (rows, nq), 1)
            seen = (segc_ref[lo:hi] == segr_ref[:, lo:]) & (kpos <= qpos)
            prob = jnp.where(seen, jnp.exp(sc - lse_ref[h:h + 1, lo:]), 0.0)
            dv = jnp.dot(prob.astype(bf16), dctx[lo:], preferred_element_type=f32)
            dprob = contract(val[lo:hi], dctx[lo:], 1, 1)
            ds = (prob * (dprob - delta_ref[h:h + 1, lo:])).astype(bf16)
            dk = jnp.dot(ds, q[lo:], preferred_element_type=f32)
            dq = contract(ds, key[lo:hi], 0, 0)
            if j == 0:
                dq_s[...] = dq
            else:
                dq_s[lo:] += dq
            dqkv_ref[lo:hi, part + h * HD:part + (h + 1) * HD] = dk.astype(bf16)
            dqkv_ref[lo:hi, 2 * part + h * HD:2 * part + (h + 1) * HD] = dv.astype(bf16)
        dqkv_ref[:, h * HD:(h + 1) * HD] = (dq_s[...] * score_scale).astype(bf16)


def attn_back_one_body(heads, rank_ref, segc_ref, segr_ref, g0, g1, g2, g3, qkv_ref, ctx_ref, lse_ref, wout_ref,
                       dctx_ref, delta_ref, go_ref, dqkv_ref, del_s, dq_s):
    rank = rank_ref[0]
    rows, width = g0.shape
    part = width // 4
    go = jnp.zeros((part, width), f32)
    for k, g in enumerate((g0, g1, g2, g3)):
        at = at_rows(rank ^ k, rows)
        dctx_ref[at] = contract(g[...], wout_ref[...], 1, 1).astype(bf16)
        go = go + contract(ctx_ref[at], g[...], 0, 0)
    go_ref[...] = go
    prod = dctx_ref[...].astype(f32) * ctx_ref[...].astype(f32)
    for h in range(part // HD):
        del_s[:, h:h + 1] = jnp.sum(prod[:, h * HD:(h + 1) * HD], -1, keepdims=True)
    delta_ref[...] = del_s[...].T[0:8]
    heads_back(heads, segc_ref, segr_ref, qkv_ref, lse_ref, delta_ref, dctx_ref, dqkv_ref, dq_s)


def attn_back_two_body(count, heads, rank_ref, segc_ref, segr_ref, qkv_ref, lse_ref, delta_ref, dctx_ref, dqkv_in,
                       go_s, nrm_ref, unit_ref, inv_ref, ids_ref, par_ref, smid_ref, upb_ref, wq_ref,
                       send_ref, keep_ref, far_ref, gkeep_ref, gsend_ref, sm_ref, dqkv_s,
                       dq_s, gq_s, sm_s):
    dqkv_s[...] = dqkv_in[...]
    rank, me = rank_ref[0], rank_ref[1]
    rows, width = keep_ref.shape
    part = width // 4
    heads_back(heads, segc_ref, segr_ref, qkv_ref, lse_ref, delta_ref, dctx_ref, dqkv_s, dq_s)
    gain = par_ref[5:6]
    by_pass = smid_ref[0:8]
    gain_sum = jnp.zeros((1, width), f32)
    bias_sum = jnp.zeros((1, width), f32)
    for k in range(4):
        at = at_rows(rank ^ k, rows)
        back = contract(dqkv_s[at], wq_ref[...], 1, 1)
        if k % 2:
            send_ref[(k // 2) * rows:(k // 2 + 1) * rows] = back.astype(bf16)
        else:
            (far_ref if k else keep_ref)[...] = back
        unit = unit_ref[at].astype(f32)
        gain_sum = gain_sum + jnp.sum(back * unit, 0, keepdims=True)
        bias_sum = bias_sum + jnp.sum(back, 0, keepdims=True)
        one = (lax.broadcasted_iota(jnp.int32, (8, rows), 0).astype(f32) == ids_ref[k:k + 1]).astype(bf16)
        by_pass = by_pass + contract(one, norm_back(back, unit, inv_ref[at], gain).astype(bf16), 1, 0)
    gq_s[...] = contract(nrm_ref[...], dqkv_s[...], 0, 0)
    full = jnp.concatenate([by_pass[0:5], gain_sum, bias_sum, smid_ref[8:12],
                            jnp.zeros((5, width), f32)], 0)
    up_b = upb_ref[0:1]
    mine = lax.broadcasted_iota(jnp.int32, (16, part), 0)
    for j in range(4):
        sm = full[:, j * part:(j + 1) * part]
        for i in range(4):
            sm = jnp.where((mine == 11 + i) & (rank == j), up_b[:, i * part:(i + 1) * part], sm)
        sm_s[j] = sm
    if in_kernel(count, width):
        chunk_qkv(rank, me, count, gq_s, go_s, sm_s, gkeep_ref, gsend_ref)
        sm_ref[...] = jnp.zeros(sm_ref.shape, f32)
    else:
        gkeep_ref[...] = gq_s[...]
        gsend_ref[...] = go_s[...]
        for k in range(4):
            sm_ref[k] = sm_s[rank ^ k]


def chunk_qkv(rank, me, count, gq_s, go_s, sm_s, keep_ref, gsend_ref):
    part = go_s.shape[0]
    rows = part // count
    small = 16 // count
    wide = gq_s.shape[1]
    step = rows + small

    def store(target, p, nat, place):
        for k in range(4):
            at = pl.ds(pl.multiple_of((rank ^ k) * part + nat * rows, 8), rows)
            target[place, k * step:k * step + rows] = gq_s[at].astype(target.dtype)
        out = go_s[at_rows(nat, rows)]
        third = rows // 3
        target[place, 4 * step:4 * step + rows] = out[:, 0:wide].astype(target.dtype)
        tail = out[:, wide:]
        packed = jnp.concatenate([tail[i * third:(i + 1) * third] for i in range(3)], 1)
        target[place, 4 * step + rows:4 * step + rows + third] = packed.astype(target.dtype)

    for p in range(count):
        target, place = (keep_ref, p) if p < count // 2 else (gsend_ref, p - count // 2)
        nat = chunk_at(rank, me, count, p)
        store(target, p, nat, place)
        for k in range(4):
            sm = sm_s[rank ^ k]
            row = jnp.zeros((small, part), f32)
            for c in range(count):
                row = jnp.where(nat == c, sm[c * small:(c + 1) * small], row)
            target[place, k * step + rows:k * step + rows + small, 0:part] = row.astype(target.dtype)
            target[place, k * step + rows:k * step + rows + small, part:] = jnp.zeros(
                (small, wide - part), target.dtype)


def last_body(sin_ref, par_ref, grad_ref, keep_ref, recv_ref, yrecv_ref, tok_ref):
    rows = sin_ref.shape[0]
    back = keep_ref[...] + recv_ref[0:rows].astype(f32) + yrecv_ref[...].astype(f32)
    unit, inverse = unit_of(sin_ref[...])
    tok_ref[...] = (grad_ref[...] + norm_back(back, unit, inverse, par_ref[5:6])).astype(bf16)


def place_feed_body(rank_ref, g_ref, *refs):
    down_ref, up_ref = refs[-2:]
    rank = rank_ref[0]
    down_rows = down_ref.shape[0]
    up_rows, hidden = up_ref.shape[0], up_ref.shape[1] // 4
    down_ref[...] = g_ref[0, 0:down_rows].astype(f32)
    for k in range(4):
        lo = down_rows + k * up_rows
        up_ref[:, pl.ds(pl.multiple_of((rank ^ k) * hidden, hidden), hidden)] = g_ref[0, lo:lo + up_rows].astype(f32)


def place_qkv_body(count, start, rank_ref, g_ref, *refs):
    rank, me = rank_ref[0], rank_ref[1]
    if start:
        sm_in, _, _, qkv_ref, out_ref = refs[:5]
        small_refs, stage_s, sm_s = refs[5:-2], refs[-2], refs[-1]
    else:
        qkv_ref, out_ref, sm_s, stage_s = refs
    step = pl.program_id(0)
    rows, third = out_ref.shape[0], out_ref.shape[0] // 3
    width = out_ref.shape[1]
    part = width // 4
    wide = g_ref.shape[2]
    small = 16 // count
    if start:
        @pl.when(step == 0)
        def _():
            sm_s[...] = sm_in[...]
    stage_s[...] = g_ref[0, 0:4 * rows].astype(f32)
    for j in range(4):
        block = stage_s[at_rows(rank ^ j, rows)]
        for i in range(3):
            qkv_ref[:, i * width + j * part:i * width + (j + 1) * part] = block[:, i * part:(i + 1) * part]
    sm_s[chunk_at(rank, me, count, step + start)] = g_ref[0, 4 * rows:4 * rows + small, 0:part].astype(f32)
    lo = 4 * rows + small
    out_ref[:, 0:wide] = g_ref[0, lo:lo + rows].astype(f32)
    packed = g_ref[0, lo + rows:lo + rows + third].astype(f32)
    out_ref[:, wide:] = jnp.concatenate([packed[:, i * part:(i + 1) * part] for i in range(3)], 0)
    if start:
        @pl.when(step == pl.num_programs(0) - 1)
        def _():
            rows_of = [sm_s[i // small, i % small:i % small + 1] for i in range(16)]
            table_ref = small_refs[0]
            for i in range(table_ref.shape[0]):
                table_ref[i:i + 1] = rows_of[i]
            for ref, i in zip(small_refs[1:7], (5, 6, 9, 7, 8, 10)):
                ref[...] = rows_of[i].reshape(part)
            for i in range(4):
                small_refs[7][i * part:(i + 1) * part] = rows_of[11 + i].reshape(part)


def qkv_blocks_body(rank_ref, w_ref, own_ref, near_ref, far_ref, stage_s):
    rank = rank_ref[0]
    part = w_ref.shape[0]
    for t in range(4):
        stage_s[t] = jnp.concatenate(
            [w_ref[:, (4 * i + t) * part:(4 * i + t + 1) * part] for i in range(3)], 1)
    own_ref[...] = stage_s[rank]
    near_ref[...] = stage_s[rank ^ 1]
    far_ref[0:part] = stage_s[rank ^ 2]
    far_ref[part:] = stage_s[rank ^ 3]


def up_blocks_body(rank_ref, w_ref, cot_ref, own_ref, near_ref, far_ref):
    rank, side = rank_ref[0], rank_ref[2]
    rows = cot_ref.shape[0]
    hidden = own_ref.shape[1]

    def block(k):
        return w_ref[:, pl.ds(pl.multiple_of((rank ^ k) * hidden, hidden), hidden)]

    own_ref[...] = block(0)
    near_ref[0:rows] = cot_ref[...]
    near_ref[rows:] = block(1)
    far_ref[0:rows] = cot_ref[...]
    far_ref[rows:] = block(2 + side)


def by_core(value):
    return lax.ppermute(value, "shard", CORE)


def by_row(value):
    return lax.ppermute(value, "shard", ROWY)


def gather_rows(block):
    far = by_row(block)
    return block, by_core(block), far, by_core(far)


def scatter_sum(send, keep, far, rows):
    recv = by_core(send)
    onward = (far + recv[rows:].astype(f32)).astype(bf16)
    return keep, recv, by_row(onward), onward


def after(value, *others):
    return lax.optimization_barrier((value,) + others)[0]


def phases_of(count):
    return (count - 1).bit_length()


def order_of(count, core):
    order = list(range(phases_of(count)))
    if core and len(order) > 1:
        order[0], order[1] = order[1], order[0]
    return order


def plane_pairs(count, phase):
    pairs = []
    for r in range(count):
        for s in range(4):
            pairs.append((4 * r + s, 4 * (r ^ (1 << order_of(count, s % 2)[phase])) + s))
    return pairs


def chunk_index(count, replica):
    total = jnp.zeros((), jnp.int32)
    for position in order_of(count, 0):
        total = total * 2 + ((replica >> position) & 1)
    return total


def plane_swap(value, count, phase):
    return lax.ppermute(value, ("replica", "shard"), plane_pairs(count, phase))


def split_step(keep, got):
    half = keep.shape[0] // 2
    total = (keep.astype(f32) + got.astype(f32)).astype(bf16)
    return total[:half], total[half:]


def shards(replicas, tokens, pass_ids, seg_ids, cotangent, pass_table, norm1_gain, norm1_bias, qkv_weight, out_weight,
           out_bias, norm2_gain, norm2_bias, up_weight, up_bias, down_weight, down_bias):
    rows, width = tokens.shape
    part = width // 4
    seq = seg_ids.shape[0]
    hidden = up_bias.shape[0]
    phases = phases_of(replicas)
    packed = in_kernel(replicas, width)
    rank = lax.axis_index("shard").astype(jnp.int32)
    replica = lax.axis_index("replica").astype(jnp.int32)
    me = chunk_index(replicas, replica)
    place = jnp.stack([rank, me, replica & 1])
    smem = pl.BlockSpec(memory_space=pltpu.SMEM)
    vmem = pl.BlockSpec(memory_space=pltpu.VMEM)

    def call(body, micros, outs, scratch, *args, ranked=True, aliases=None, wide=False):
        specs = [smem] * ranked + [vmem] * (len(args) - ranked)
        return pl.pallas_call(
            body,
            out_shape=[jax.ShapeDtypeStruct(s, d) for s, d in outs],
            in_specs=specs,
            out_specs=[vmem] * len(outs),
            scratch_shapes=[pltpu.VMEM(s, d) for s, d in scratch],
            input_output_aliases=aliases or {},
            compiler_params=pltpu.CompilerParams(vmem_limit_bytes=None if wide else 24 * 2**20),
            cost_estimate=pl.CostEstimate(flops=int(micros * 1.1e9), bytes_accessed=0, transcendentals=0),
        )(*args)

    def placed(body, values, start, shapes, blocks_of, extra, scratch, aliases):
        def at_chunk(p, s):
            return (chunk_at(s[0], s[1], replicas, p + start), 0)

        def whole(shape):
            return pl.BlockSpec(shape, lambda p, s: (0,) * len(shape))

        return pl.pallas_call(
            body,
            out_shape=[jax.ShapeDtypeStruct(s, f32) for s in shapes],
            grid_spec=pltpu.PrefetchScalarGridSpec(
                num_scalar_prefetch=1, grid=(replicas // 2,),
                in_specs=[pl.BlockSpec((1,) + values.shape[1:], lambda p, s: (p, 0, 0))]
                + [whole(e.shape) if e.ndim == 3 else pl.BlockSpec(memory_space=pl.ANY) for e in extra],
                out_specs=[pl.BlockSpec(b, at_chunk) if b else whole(s) for s, b in zip(shapes, blocks_of)],
                scratch_shapes=[pltpu.VMEM(s, f32) for s in scratch]),
            input_output_aliases=aliases,
            compiler_params=pltpu.CompilerParams(vmem_limit_bytes=24 * 2**20),
            cost_estimate=pl.CostEstimate(flops=int(2.2e9), bytes_accessed=0, transcendentals=0),
        )(place, values, *extra)

    block, = call(pack_body, 1, [((rows + 16, width), bf16)], [], tokens, pass_ids, pass_table.T, norm1_gain, norm1_bias,
                  out_bias, norm2_gain, norm2_bias, down_bias, ranked=False, wide=True)
    x1, x2 = by_core(block), by_row(block)
    own_q, near_q, far_q = call(
        qkv_blocks_body, 0, [((part, 3 * part), bf16), ((part, 3 * part), bf16), ((2 * part, 3 * part), bf16)],
        [((4, part, 3 * part), bf16)], place, after(qkv_weight, block))
    far_q = by_row(far_q)
    own_u, near_u, far_u = call(
        up_blocks_body, 0,
        [((part, hidden), bf16), ((rows + part, width), bf16), ((rows + part, width), bf16)],
        [], place, up_weight, after(cotangent, own_q))
    x2 = after(x2, own_u)
    blocks = block, x1, x2, by_core(x2)
    sin, par, nrm, nrm_late, unit, inv, ids = call(
        norm_body, 0,
        [((rows, width), f32), ((16, width), f32), ((seq, width), bf16), ((seq, width), bf16), ((seq, width), bf16),
         ((seq, 1), f32), ((8, rows), f32)], [], place, *blocks)
    far_q = after(far_q, nrm)
    wq = own_q, by_core(near_q), far_q, by_core(far_q[part:])
    far_u = by_row(far_u)
    group = by_core(near_u), far_u, by_core(far_u)
    pair_u = lax.ppermute(far_u[rows:], ("replica", "shard"), [
        (4 * r + s, 4 * (r ^ 1) + (s ^ (r & 1))) for r in range(replicas) for s in range(4)])

    segc, segr = seg_ids[:, None], seg_ids[None, :]
    heads = part // HD
    half_f, half_b, row_f, row_b = ((2 * rows, width), f32), ((2 * rows, width), bf16), ((rows, width), f32), ((rows, width), bf16)
    send, keep, far, qkv, ctx, lse, wq_full = call(
        front_body, 4,
        [half_b, row_f, row_f, ((seq, 3 * part), bf16), ((seq, part), bf16), ((8, seq), f32), ((width, 3 * part), bf16)],
        [((seq, 128), f32), ((3 * heads, seq, HD), bf16), ((heads, seq, HD), bf16), ((heads, seq, 1), f32)],
        place, segc, segr, nrm, *wq, out_weight)
    parts = scatter_sum(after(send, far_u), keep, far, rows)
    mid, nrm2 = call(mid_body, 1, [row_f, row_b], [], sin, par, *parts[:2], after(parts[2], pair_u), ranked=False)
    n2 = gather_rows(nrm2)
    send, keep, far, act, pg = call(
        feed_body, 5, [half_b, row_f, row_f, ((seq, hidden), bf16), ((seq, hidden), bf16)],
        [((width, hidden), bf16)],
        place, *n2, cotangent, *group, own_u, pair_u, up_bias, down_weight)
    *back, onward = scatter_sum(send, keep, far, rows)
    feed_rows = hidden // replicas + 4 * (part // replicas)
    if packed:
        grads = [((replicas // 2, feed_rows, width), bf16)] * 2
    else:
        grads = [((hidden, width), f32), ((width, hidden), f32)]
    up_b, gkeep, gsend = call(
        functools.partial(feed_grad_body, replicas), 8, [((8, hidden), f32)] + grads,
        [((hidden, width), f32), ((width, hidden), f32)],
        place, *n2, cotangent, *group, after(act, onward), pg)
    if not packed:
        nat = chunk_at(rank, me, replicas, jnp.arange(replicas))
        downs = gkeep.reshape(replicas, -1, width)[nat]
        ups = gsend.reshape(4, replicas, -1, hidden)[rank ^ jnp.arange(4)][:, nat].transpose(1, 0, 2, 3)
        both = jnp.concatenate([downs, ups.reshape(replicas, -1, width)], 1)
        both = both.astype(bf16)
        gkeep, gsend = both[:replicas // 2], both[replicas // 2:]
    got = plane_swap(gsend, replicas, 0)
    mid_grad, branch, small_mid = call(
        mid_back_body, 6, [row_f, row_b, ((16, width), f32)], [], mid, par, after(cotangent, up_b), ids, *back, ranked=False)
    branches = gather_rows(branch)
    got = after(got, branches[1])
    for phase in range(1, max(phases - 1, 1)):
        gkeep, gsend = split_step(gkeep, got)
        got = plane_swap(gsend, replicas, phase)

    small = max(16, replicas)
    step = part // replicas + small // replicas
    qkv_rows = 4 * step + part // replicas + part // replicas // 3
    if packed:
        grads = [((replicas // 2, qkv_rows, 3 * part), bf16)] * 2
    else:
        grads = [((width, 3 * part), f32), ((part, width), f32)]
    first, rest = range(heads - 1), range(heads - 1, heads)
    dctx, delta, grad_out, dqkv = call(
        functools.partial(attn_back_one_body, first), 6,
        [((seq, part), bf16), ((8, seq), f32), ((part, width), f32), ((seq, 3 * part), bf16)],
        [((seq, 128), f32), ((seq, HD), f32)],
        place, segc, segr, *branches, qkv, ctx, lse, out_weight)
    if phases > 1:
        gkeep, gsend = split_step(gkeep, after(got, delta))
        got = plane_swap(gsend, replicas, phases - 1)
    send, keep, far, qkeep, qsend, smalls = call(
        functools.partial(attn_back_two_body, replicas, rest), 6,
        [half_b, row_f, row_f] + grads + [((4, 16, part), f32)],
        [((seq, 3 * part), bf16), ((seq, HD), f32), ((width, 3 * part), f32), ((4, 16, part), f32)],
        place, segc, segr, qkv, lse, after(delta, gsend), dctx, dqkv, grad_out, nrm_late, unit, inv, ids, par, small_mid, up_b,
        wq_full)
    if not packed:
        qs = qkeep.reshape(4, replicas, -1, 3 * part)[rank ^ jnp.arange(4)][:, nat].transpose(1, 0, 2, 3)
        sm = jnp.pad(smalls, ((0, 0), (0, small - 16), (0, 2 * part)))
        sm = sm.reshape(4, replicas, -1, 3 * part)[:, nat].transpose(1, 0, 2, 3)
        os = qsend.reshape(replicas, -1, width)[nat]
        both = jnp.concatenate([
            jnp.concatenate([qs, sm], 2).reshape(replicas, -1, 3 * part), os[:, :, :3 * part],
            os[:, :, 3 * part:].reshape(replicas, -1, 3 * part)], 1)
        both = both.astype(bf16)
        qkeep, qsend = both[:replicas // 2], both[replicas // 2:]
    qgot = plane_swap(qsend, replicas, 0)
    lo, ur = hidden // replicas, part // replicas

    last_phase = phases - 1
    now = {"turn": qkeep, "feed": got, "qkv": qgot}

    def swap_piece(at):
        return by_core(at(1)), by_row(at(2)), lax.ppermute(at(3), "shard", BOTH)

    def feed_swap():
        piece = (gkeep.astype(f32) + after(now["feed"], now["turn"]).astype(f32))[0].astype(bf16)
        now["swapped"] = swap_piece(lambda k: piece[lo + k * ur:lo + (k + 1) * ur])
        now["piece"], now["turn"] = piece, now["swapped"][0]

    def feed_first():
        now["feed_all"] = jnp.concatenate(
            [now["piece"][:lo + ur]] + [after(s, now["turn"]) for s in now["swapped"]], 0)[None]
        now["feed"] = plane_swap(now["feed_all"], replicas, last_phase)
        now["turn"] = now["feed_all"]

    def feed_join(phase):
        now["feed_all"] = jnp.concatenate([now["feed_all"], after(now["feed"], now["turn"])], 0)
        now["feed"] = plane_swap(now["feed_all"], replicas, phase)
        now["turn"] = now["feed_all"]

    def qkv_split(phase):
        now["qkeep"], qsend = split_step(now.get("qkeep", qkeep), after(now["qkv"], now["turn"]))
        now["qkv"] = plane_swap(qsend, replicas, phase)
        now["turn"] = qsend

    def qkv_swap():
        low = (now.get("qkeep", qkeep).astype(f32) + after(now["qkv"], now["turn"]).astype(f32))[0].astype(bf16)
        now["quads"] = swap_piece(lambda k: low[k * step:(k + 1) * step])
        now["low"], now["turn"] = low, now["quads"][0]

    def qkv_first():
        low = now["low"]
        quads = [low[:step]] + [after(s, now["turn"]) for s in now["quads"]]
        own_small = sum(q[ur:].astype(f32) for q in quads).astype(bf16)
        now["qkv_all"] = jnp.concatenate([q[:ur] for q in quads] + [own_small, low[4 * step:]], 0)[None]
        now["qkv"] = plane_swap(now["qkv_all"], replicas, last_phase)
        now["turn"] = now["qkv_all"]

    def qkv_join(phase):
        now["qkv_all"] = jnp.concatenate([now["qkv_all"], after(now["qkv"], now["turn"])], 0)
        now["qkv"] = plane_swap(now["qkv_all"], replicas, phase)
        now["turn"] = now["qkv_all"]

    recv = by_core(send)

    def tokens_onward():
        onward = (far + after(recv, now["turn"])[rows:].astype(f32)).astype(bf16)
        now["tokens"], now["turn"] = by_row(onward), onward

    def tokens_end():
        now["tokens_grad"], = call(last_body, 1, [row_b], [], sin, par, after(mid_grad, now["turn"]), keep, recv,
                                   now["tokens"], ranked=False)
        now["turn"] = now["tokens_grad"]

    def out_start():
        now["out"] = call(feed_out_body, 0, [half_b, row_f, row_f], [], down_weight, after(act, now["turn"]),
                          ranked=False)
        now["turn"] = now["out"][0]
        now["recv_o"] = by_core(now["out"][0])

    def out_onward():
        onward = (now["out"][2] + after(now["recv_o"], now["turn"])[rows:].astype(f32)).astype(bf16)
        now["far_o"], now["turn"] = by_row(onward), onward

    def out_end():
        now["output"] = (mid + now["out"][1] + now["recv_o"][:rows].astype(f32)
                         + after(now["far_o"], now["turn"]).astype(f32) + par[10:11]).astype(bf16)
        now["turn"] = now["output"]

    def feed_place():
        if packed:
            now["filled"] = placed(place_feed_body, after(now["feed_all"], now["turn"]), 0, *feed_shapes, [], [], {})
            now["turn"] = now["filled"][0]

    def qkv_place():
        if packed:
            now["qfilled"] = placed(
                functools.partial(place_qkv_body, replicas, 0), after(now["qkv_all"], now["turn"]), 0,
                qkv_shapes[0] + [sm_shape], qkv_shapes[1] + [None], [], [stage], {})
            now["turn"] = now["qfilled"][0]

    feed_shapes = [(hidden, width), (part, 4 * hidden)], [(lo, width), (ur, 4 * hidden)]
    qkv_shapes = [(part, 12 * part), (part, width)], [(ur, 12 * part), (ur, width)]
    stage, sm_shape = (4 * ur, 3 * part), (replicas, 16 // replicas, part)
    feed_joins = [functools.partial(feed_join, p) for p in reversed(range(last_phase))]
    qkv_joins = [functools.partial(qkv_join, p) for p in reversed(range(last_phase))]
    splits = [functools.partial(qkv_split, p) for p in range(1, phases)]
    for run in ([feed_swap, tokens_onward, out_start, feed_first] + splits[:1] + [tokens_end] + splits[1:]
                + feed_joins[:-1] + [qkv_swap, out_onward, qkv_first] + feed_joins[-1:] + [feed_place]
                + qkv_joins + [out_end, qkv_place]):
        run()
    tokens_grad, output, feed_all, got, qkv_all, qgot = (
        now[n] for n in ("tokens_grad", "output", "feed_all", "feed", "qkv_all", "qkv"))

    if packed:
        final_down, final_up = placed(
            place_feed_body, after(got, now["turn"]), replicas // 2, *feed_shapes, list(now["filled"]), [], {2: 0, 3: 1})
        filled = now["qfilled"]
        shapes, split = qkv_shapes
        vectors = [pass_table.T.shape] + [(part,)] * 6 + [(hidden,)]
        final_qkv, final_out, table, g1, b1, ob, g2, b2, db, ub = placed(
            functools.partial(place_qkv_body, replicas, replicas // 2), after(qgot, final_down), replicas // 2, shapes + vectors,
            split + [None] * 8, [filled[2], filled[0], filled[1]], [stage, sm_shape], {3: 0, 4: 1})
    else:
        back_at = jnp.argsort(nat)
        feed_all = jnp.concatenate([feed_all, got], 0)[back_at].astype(f32)
        qkv_all = jnp.concatenate([qkv_all, qgot], 0)[back_at].astype(f32)
        final_down = feed_all[:, :lo].reshape(hidden, width)
        final_up = feed_all[:, lo:].reshape(replicas, 4, ur, hidden)[:, rank ^ jnp.arange(4)]
        final_up = final_up.transpose(0, 2, 1, 3).reshape(part, 4 * hidden)
        final_qkv = qkv_all[:, :4 * ur].reshape(replicas, 4, ur, 3, part)[:, rank ^ jnp.arange(4)]
        final_qkv = final_qkv.transpose(0, 2, 3, 1, 4).reshape(part, 12 * part)
        hi = 4 * ur + small // replicas
        mine = qkv_all[:, 4 * ur:hi, :part].reshape(small, part)
        final_out = jnp.concatenate(
            [qkv_all[:, hi:hi + ur].reshape(part, 3 * part), qkv_all[:, hi + ur:].reshape(part, part)], 1)
        table, g1, b1, ob, g2, b2, db = mine[0:5], mine[5], mine[6], mine[9], mine[7], mine[8], mine[10]
        ub = mine[11:15].reshape(hidden)
    return (output, tokens_grad, table.T, g1, b1, final_qkv, final_out, ob, g2, b2, final_up, ub, final_down, db)


def solution(mesh):
    row = P(("replica", "shard"), None)
    flat = P(("replica", "shard"))
    w2, w1 = P("shard", None), P("shard")
    return jax.shard_map(
        functools.partial(shards, mesh.shape["replica"]),
        mesh=mesh,
        in_specs=(row, flat, P("replica"), row, w2, w1, w1, w2, w2, w1, w1, w1, w2, w1, w2, w1),
        out_specs=(row, row, w2, w1, w1, w2, w2, w1, w1, w1, w2, w1, w2, w1),
        check_vma=False,
    )
```

```python
import functools

import jax
import jax.numpy as jnp
from jax import lax
from jax.experimental import pallas as pl
from jax.experimental.pallas import tpu as pltpu
from jax.sharding import PartitionSpec as P

HD = 64
epsilon = 1e-05
score_scale = 0.125
masked_score = -1e30
f32 = jnp.float32
bf16 = jnp.bfloat16

CORE = [(i, i ^ 1) for i in range(4)]
ROWY = [(i, i ^ 2) for i in range(4)]
BOTH = [(i, i ^ 3) for i in range(4)]


def contract(left, right, ld, rd):
    return lax.dot_general(left, right, (((ld,), (rd,)), ((), ())), preferred_element_type=f32)


def unit_of(values):
    centred = values - jnp.mean(values, -1, keepdims=True)
    inverse = lax.rsqrt(jnp.mean(centred * centred, -1, keepdims=True) + epsilon)
    return centred * inverse, inverse


def norm_back(grad_rows, unit_rows, inverse, gain):
    scaled = grad_rows * gain
    return inverse * (
        scaled
        - jnp.mean(scaled, -1, keepdims=True)
        - unit_rows * jnp.mean(scaled * unit_rows, -1, keepdims=True)
    )


def at_rows(index, size):
    return pl.ds(pl.multiple_of(index * size, size), size)


def pack_body(x_ref, ids_ref, table_ref, g1_ref, b1_ref, ob_ref, g2_ref, b2_ref, db_ref, out_ref):
    passes, part = table_ref.shape
    rows = ids_ref.shape[0]
    out_ref[0:rows] = x_ref[...]
    ext = jnp.zeros((16, out_ref.shape[1]), bf16)
    out_ref[rows:] = ext
    out_ref[rows:rows + passes, 0:part] = table_ref[...]
    for i, ref in enumerate((g1_ref, b1_ref, ob_ref, g2_ref, b2_ref, db_ref)):
        out_ref[rows + 5 + i:rows + 6 + i, 0:part] = ref[...].astype(f32).reshape(1, part).astype(bf16)
    out_ref[rows + 11:rows + 12, 0:rows] = ids_ref[...].astype(f32).reshape(1, rows).astype(bf16)


def norm_body(rank_ref, seg_ref, x0, x1, x2, x3,
              segc_ref, segr_ref, sin_ref, par_ref, nrm_ref, late_ref, unit_ref, inv_ref, ids_ref):
    rank = rank_ref[0]
    rows, width = sin_ref.shape
    part = width // 4
    seg = seg_ref[...].astype(f32).reshape(1, seg_ref.shape[0])
    segr_ref[...] = jnp.broadcast_to(seg, segr_ref.shape)
    segc_ref[...] = jnp.broadcast_to(seg, (128, seg.shape[1])).T[:, 0:1]
    ext = [b[rows:rows + 16, 0:part].astype(f32) for b in (x0, x1, x2, x3)]
    cols = []
    for j in range(4):
        acc = jnp.zeros_like(ext[0])
        for k in range(4):
            acc = jnp.where((rank ^ k) == j, ext[k], acc)
        cols.append(acc)
    par = jnp.concatenate(cols, axis=1)
    par_ref[...] = par
    table = par[0:8].astype(bf16)
    gain, bias = par[5:6], par[6:7]
    for k, b in enumerate((x0, x1, x2, x3)):
        ids = b[rows + 11:rows + 12, 0:rows].astype(f32)
        ids_ref[k:k + 1] = ids
        one = (lax.broadcasted_iota(jnp.int32, (8, rows), 0).astype(f32) == ids).astype(bf16)
        x = b[0:rows].astype(f32) + contract(one, table, 0, 0)
        if k == 0:
            sin_ref[...] = x
        unit, inverse = unit_of(x)
        at = at_rows(rank ^ k, rows)
        unit_ref[at] = unit.astype(bf16)
        inv_ref[at] = inverse
        normed = (unit * gain + bias).astype(bf16)
        nrm_ref[at] = normed
        late_ref[at] = normed


def front_body(rank_ref, segc_ref, segr_ref, nrm_ref, w0, w1, w2, w3, wout_ref,
               send_ref, keep_ref, far_ref, qkv_ref, ctx_ref, lse_ref, wq_ref, lse_s, head_s, ctx_s, top_s):
    rank = rank_ref[0]
    rows, width = keep_ref.shape
    part = width // 4
    for k, w in enumerate((w0[...], w1[...], w2[0:part], w3[...])):
        wq_ref[at_rows(rank ^ k, part)] = w
    qkv_ref[...] = jnp.dot(nrm_ref[...], wq_ref[...], preferred_element_type=f32).astype(bf16)
    heads = part // HD
    total_rows = nrm_ref.shape[0]
    for i in range(3 * heads):
        head = qkv_ref[:, i * HD:(i + 1) * HD]
        head_s[i] = head * jnp.asarray(score_scale, bf16) if i < heads else head

    def one_head(h, carry):
        q, key, val = head_s[h], head_s[heads + h], head_s[2 * heads + h]
        for i in range(total_rows // rows):
            lo, nk = i * rows, (i + 1) * rows
            sc = contract(q[lo:nk], key[:nk], 1, 1)
            qpos = lo + lax.broadcasted_iota(jnp.int32, (rows, nk), 0)
            kpos = lax.broadcasted_iota(jnp.int32, (rows, nk), 1)
            seen = (segc_ref[lo:nk] == segr_ref[0:1, :nk]) & (kpos <= qpos)
            sc = jnp.where(seen, sc, masked_score)
            top = jnp.max(sc, -1, keepdims=True)
            e = jnp.exp(sc - top)
            total = jnp.sum(e, -1, keepdims=True)
            prob = (e * (1.0 / total)).astype(bf16)
            ctx_s[h, lo:nk] = jnp.dot(prob, val[:nk], preferred_element_type=f32).astype(bf16)
            top_s[h, lo:nk] = top + jnp.log(total)
        return carry

    lax.fori_loop(0, heads, one_head, 0)
    for h in range(heads):
        ctx_ref[:, h * HD:(h + 1) * HD] = ctx_s[h]
        lse_s[:, h:h + 1] = top_s[h]
    lse_ref[...] = lse_s[...].T[0:8]
    for i, k in enumerate((1, 3)):
        send_ref[i * rows:(i + 1) * rows] = jnp.dot(
            ctx_ref[at_rows(rank ^ k, rows)], wout_ref[...], preferred_element_type=f32).astype(bf16)
    for ref, k in ((keep_ref, 0), (far_ref, 2)):
        ref[...] = jnp.dot(ctx_ref[at_rows(rank ^ k, rows)], wout_ref[...], preferred_element_type=f32)


def mid_body(start, sin_ref, par_ref, keep_ref, recv_ref, yrecv_ref, mid_ref, nrm_ref):
    at = slice(start, start + yrecv_ref.shape[0])
    mid = (sin_ref[at] + keep_ref[at] + recv_ref[at].astype(f32)
           + yrecv_ref[...].astype(f32) + par_ref[7:8])
    mid_ref[...] = mid
    unit, _ = unit_of(mid)
    nrm_ref[...] = (unit * par_ref[8:9] + par_ref[9:10]).astype(bf16)


def gelu_pair(v):
    c0, c1 = 0.7978845608028654, 0.044715
    sq = v * v
    t = jnp.tanh(c0 * v * (1.0 + c1 * sq))
    half = 0.5 * (1.0 + t)
    return v * half, half + 0.5 * v * (1.0 - t * t) * (c0 * (1.0 + 3.0 * c1 * sq))


def whole_block(halves):
    return jnp.concatenate([half[...] for half in halves], 0)


def feed_body(rank_ref, n0, m0, n1, m1, n2, m2, n3, m3, c0, g1, g2, g3, u0, pair_ref, ub_ref, dw_ref,
              send_ref, keep_ref, far_ref, act_ref, pg_ref, wu_s):
    rank = rank_ref[0]
    rows, width = c0.shape
    part = width // 4
    ub_row = ub_ref[...].astype(f32).reshape(1, ub_ref.shape[0])
    side = rank_ref[2]
    wu_s[at_rows(rank, part)] = u0[...]
    wu_s[at_rows(rank ^ 1, part)] = g1[rows:]

    @pl.when(side == 0)
    def _():
        wu_s[at_rows(rank ^ 2, part)] = g2[rows:]
        wu_s[at_rows(rank ^ 3, part)] = pair_ref[...]

    @pl.when(side == 1)
    def _():
        wu_s[at_rows(rank ^ 2, part)] = pair_ref[...]
        wu_s[at_rows(rank ^ 3, part)] = g3[rows:]

    for k, (n, c) in enumerate((
            ((n0, m0), c0[...]), ((n1, m1), g1[0:rows]), ((n2, m2), g2[0:rows]), ((n3, m3), g3[0:rows]))):
        pre = jnp.dot(whole_block(n), wu_s[...], preferred_element_type=f32) + ub_row
        act, slope = gelu_pair(pre)
        act_ref[k * rows:(k + 1) * rows] = act.astype(bf16)
        pg = (contract(c, dw_ref[...], 1, 1) * slope).astype(bf16)
        pg_ref[k * rows:(k + 1) * rows] = pg
        back = contract(pg, wu_s[...], 1, 1)
        if k % 2:
            send_ref[(k // 2) * rows:(k // 2 + 1) * rows] = back.astype(bf16)
        else:
            (far_ref if k else keep_ref)[...] = back


def chunk_at(rank, me, count, p):
    top, next_bit = count // 2, count // 4
    turned = p
    if next_bit:
        turned = (p % next_bit) + jnp.where((p & top) != 0, next_bit, 0) + jnp.where((p & next_bit) != 0, top, 0)
    return me ^ jnp.where((rank & 1) == 0, p, turned)


def chunk_feed(rank, me, count, gd_s, gu_s, keep_ref, gsend_ref):
    down_rows, up_rows = gd_s.shape[0] // count, gu_s.shape[0] // count // 4
    part = gu_s.shape[0] // 4

    def store(target, start):
        def one(p, carry):
            nat = chunk_at(rank, me, count, p + start)
            target[p, 0:down_rows] = gd_s[at_rows(nat, down_rows)].astype(target.dtype)
            for k in range(4):
                at = pl.ds(pl.multiple_of((rank ^ k) * part + nat * up_rows, 8), up_rows)
                lo = down_rows + k * up_rows
                target[p, lo:lo + up_rows] = gu_s[at].astype(target.dtype)
            return carry

        lax.fori_loop(0, count // 2, one, 0)

    store(keep_ref, 0)
    store(gsend_ref, count // 2)


def feed_grad_body(count, rank_ref, n0, m0, n1, m1, n2, m2, n3, m3, c0, g1, g2, g3, act_ref, pg_ref,
                   upb_ref, gkeep_ref, gsend_ref, gd_s, gu_s):
    rank, me = rank_ref[0], rank_ref[1]
    rows, width = c0.shape
    part = width // 4
    up_b = jnp.zeros((1, pg_ref.shape[1]), f32)
    blocks = (
        ((n0, m0), c0[...]), ((n1, m1), g1[0:rows]), ((n2, m2), g2[0:rows]), ((n3, m3), g3[0:rows]))
    for k, (n, c) in enumerate(blocks):
        act = act_ref[k * rows:(k + 1) * rows]
        pg = pg_ref[k * rows:(k + 1) * rows]
        gd = contract(act, c, 0, 0)
        gu = contract(whole_block(n), pg, 0, 0)
        gd_s[...] = gd if k == 0 else gd_s[...] + gd
        gu_s[...] = gu if k == 0 else gu_s[...] + gu
        up_b = up_b + jnp.sum(pg.astype(f32), 0, keepdims=True)
    upb_ref[0:1] = up_b
    if in_kernel(count, width):
        chunk_feed(rank, me, count, gd_s, gu_s, gkeep_ref, gsend_ref)
    else:
        gkeep_ref[...] = gd_s[...]
        gsend_ref[...] = gu_s[...]


def feed_out_body(rank_ref, dw_ref, act_ref, send_ref, keep_ref, far_ref):
    rows = keep_ref.shape[0]
    del rank_ref
    for k in range(4):
        out = jnp.dot(act_ref[k * rows:(k + 1) * rows], dw_ref[...], preferred_element_type=f32)
        if k % 2:
            send_ref[(k // 2) * rows:(k // 2 + 1) * rows] = out.astype(bf16)
        else:
            (far_ref if k else keep_ref)[...] = out


def in_kernel(count, width):
    return (width // 4 // count) % 24 == 0


def mid_back_body(start, mid_ref, par_ref, cot_ref, ids_ref, keep_ref, recv_ref, yrecv_ref,
                  grad_ref, branch_ref, small_ref):
    rows = mid_ref.shape[0]
    at = slice(start, start + rows)
    back = keep_ref[at] + recv_ref[at].astype(f32) + yrecv_ref[...].astype(f32)
    unit, inverse = unit_of(mid_ref[...])
    cot = cot_ref[at].astype(f32)
    grad = cot + norm_back(back, unit, inverse, par_ref[8:9])
    grad_ref[...] = grad
    branch = grad.astype(bf16)
    branch_ref[...] = branch
    one = (lax.broadcasted_iota(jnp.int32, (8, rows), 0).astype(f32) == ids_ref[0:1, at]).astype(bf16)
    small_ref[0:8] = contract(one, branch, 1, 0)
    small_ref[8:9] = jnp.sum(back * unit, 0, keepdims=True)
    small_ref[9:10] = jnp.sum(back, 0, keepdims=True)
    small_ref[10:11] = jnp.sum(branch.astype(f32), 0, keepdims=True)
    small_ref[11:12] = jnp.sum(cot, 0, keepdims=True)


def heads_back(heads, segc_ref, segr_ref, qkv_ref, lse_ref, delta_ref, dctx_ref, dqkv_ref, dq_s):
    part = dctx_ref.shape[1]
    total_rows = qkv_ref.shape[0]
    rows = total_rows // 4
    for h in heads:
        q = qkv_ref[:, h * HD:(h + 1) * HD] * jnp.asarray(score_scale, bf16)
        key = qkv_ref[:, part + h * HD:part + (h + 1) * HD]
        val = qkv_ref[:, 2 * part + h * HD:2 * part + (h + 1) * HD]
        dctx = dctx_ref[:, h * HD:(h + 1) * HD]
        for j in range(total_rows // rows):
            lo = j * rows
            hi = lo + rows
            nq = total_rows - lo
            sc = contract(key[lo:hi], q[lo:], 1, 1)
            kpos = lax.broadcasted_iota(jnp.int32, (rows, nq), 0)
            qpos = lax.broadcasted_iota(jnp.int32, (rows, nq), 1)
            seen = (segc_ref[lo:hi] == segr_ref[0:1, lo:]) & (kpos <= qpos)
            prob = jnp.where(seen, jnp.exp(sc - lse_ref[h:h + 1, lo:]), 0.0)
            dv = jnp.dot(prob.astype(bf16), dctx[lo:], preferred_element_type=f32)
            dprob = contract(val[lo:hi], dctx[lo:], 1, 1)
            ds = (prob * (dprob - delta_ref[h:h + 1, lo:])).astype(bf16)
            dk = jnp.dot(ds, q[lo:], preferred_element_type=f32)
            dq = contract(ds, key[lo:hi], 0, 0)
            if j == 0:
                dq_s[...] = dq
            else:
                dq_s[lo:] += dq
            dqkv_ref[lo:hi, part + h * HD:part + (h + 1) * HD] = dk.astype(bf16)
            dqkv_ref[lo:hi, 2 * part + h * HD:2 * part + (h + 1) * HD] = dv.astype(bf16)
        dqkv_ref[:, h * HD:(h + 1) * HD] = (dq_s[...] * score_scale).astype(bf16)


def attn_back_one_body(heads, rank_ref, segc_ref, segr_ref, g0, f0, g1, f1, g2, f2, g3, f3, qkv_ref, ctx_ref, lse_ref, wout_ref,
                       dctx_ref, delta_ref, go_ref, dqkv_ref, del_s, dq_s):
    rank = rank_ref[0]
    rows, width = 2 * g0.shape[0], g0.shape[1]
    part = width // 4
    go = jnp.zeros((part, width), f32)
    for k, halves in enumerate(((g0, f0), (g1, f1), (g2, f2), (g3, f3))):
        at = at_rows(rank ^ k, rows)
        g = whole_block(halves)
        dctx_ref[at] = contract(g, wout_ref[...], 1, 1).astype(bf16)
        go = go + contract(ctx_ref[at], g, 0, 0)
    go_ref[...] = go
    prod = dctx_ref[...].astype(f32) * ctx_ref[...].astype(f32)
    for h in range(part // HD):
        del_s[:, h:h + 1] = jnp.sum(prod[:, h * HD:(h + 1) * HD], -1, keepdims=True)
    delta_ref[...] = del_s[...].T[0:8]
    heads_back(heads, segc_ref, segr_ref, qkv_ref, lse_ref, delta_ref, dctx_ref, dqkv_ref, dq_s)


def attn_back_two_body(count, rank_ref, dqkv_s, go_s, nrm_ref, unit_ref, inv_ref, ids_ref, par_ref, smid_ref, smid2_ref, upb_ref, wq_ref,
                       send_ref, keep_ref, far_ref, gkeep_ref, gsend_ref, sm_ref, gq_s, sm_s):
    rank, me = rank_ref[0], rank_ref[1]
    rows, width = keep_ref.shape
    part = width // 4
    gain = par_ref[5:6]
    smid = smid_ref[...] + smid2_ref[...]
    by_pass = smid[0:8]
    gain_sum = jnp.zeros((1, width), f32)
    bias_sum = jnp.zeros((1, width), f32)
    for k in range(4):
        at = at_rows(rank ^ k, rows)
        back = contract(dqkv_s[at], wq_ref[...], 1, 1)
        if k % 2:
            send_ref[(k // 2) * rows:(k // 2 + 1) * rows] = back.astype(bf16)
        else:
            (far_ref if k else keep_ref)[...] = back
        unit = unit_ref[at].astype(f32)
        gain_sum = gain_sum + jnp.sum(back * unit, 0, keepdims=True)
        bias_sum = bias_sum + jnp.sum(back, 0, keepdims=True)
        one = (lax.broadcasted_iota(jnp.int32, (8, rows), 0).astype(f32) == ids_ref[k:k + 1]).astype(bf16)
        by_pass = by_pass + contract(one, norm_back(back, unit, inv_ref[at], gain).astype(bf16), 1, 0)
    gq_s[...] = contract(nrm_ref[...], dqkv_s[...], 0, 0)
    full = jnp.concatenate([by_pass[0:5], gain_sum, bias_sum, smid[8:12],
                            jnp.zeros((5, width), f32)], 0)
    up_b = upb_ref[0:1]
    mine = lax.broadcasted_iota(jnp.int32, (16, part), 0)
    for j in range(4):
        sm = full[:, j * part:(j + 1) * part]
        for i in range(4):
            sm = jnp.where((mine == 11 + i) & (rank == j), up_b[:, i * part:(i + 1) * part], sm)
        sm_s[j] = sm
    if in_kernel(count, width):
        chunk_qkv(rank, me, count, gq_s, go_s, sm_s, gkeep_ref, gsend_ref)
        sm_ref[...] = jnp.zeros(sm_ref.shape, f32)
    else:
        gkeep_ref[...] = gq_s[...]
        gsend_ref[...] = go_s[...]
        for k in range(4):
            sm_ref[k] = sm_s[rank ^ k]


def chunk_qkv(rank, me, count, gq_s, go_s, sm_s, keep_ref, gsend_ref):
    part = go_s.shape[0]
    rows = part // count
    small = 16 // count
    wide = gq_s.shape[1]
    step = rows + small

    def store(target, p, nat, place):
        for k in range(4):
            at = pl.ds(pl.multiple_of((rank ^ k) * part + nat * rows, 8), rows)
            target[place, k * step:k * step + rows] = gq_s[at].astype(target.dtype)
        out = go_s[at_rows(nat, rows)]
        third = rows // 3
        target[place, 4 * step:4 * step + rows] = out[:, 0:wide].astype(target.dtype)
        tail = out[:, wide:]
        packed = jnp.concatenate([tail[i * third:(i + 1) * third] for i in range(3)], 1)
        target[place, 4 * step + rows:4 * step + rows + third] = packed.astype(target.dtype)

    for p in range(count):
        target, place = (keep_ref, p) if p < count // 2 else (gsend_ref, p - count // 2)
        nat = chunk_at(rank, me, count, p)
        store(target, p, nat, place)
        for k in range(4):
            sm = sm_s[rank ^ k]
            row = jnp.zeros((small, part), f32)
            for c in range(count):
                row = jnp.where(nat == c, sm[c * small:(c + 1) * small], row)
            target[place, k * step + rows:k * step + rows + small, 0:part] = row.astype(target.dtype)
            target[place, k * step + rows:k * step + rows + small, part:] = jnp.zeros(
                (small, wide - part), target.dtype)


def last_body(sin_ref, par_ref, grad_a, grad_b, keep_ref, recv_ref, yrecv_ref, tok_ref):
    rows = sin_ref.shape[0]
    back = keep_ref[...] + recv_ref[0:rows].astype(f32) + yrecv_ref[...].astype(f32)
    unit, inverse = unit_of(sin_ref[...])
    tok_ref[...] = (whole_block((grad_a, grad_b)) + norm_back(back, unit, inverse, par_ref[5:6])).astype(bf16)


def place_feed_body(rank_ref, g_ref, *refs):
    down_ref, up_ref = refs[-2:]
    rank = rank_ref[0]
    down_rows = down_ref.shape[0]
    up_rows, hidden = up_ref.shape[0], up_ref.shape[1] // 4
    down_ref[...] = g_ref[0, 0:down_rows].astype(f32)
    for k in range(4):
        lo = down_rows + k * up_rows
        up_ref[:, pl.ds(pl.multiple_of((rank ^ k) * hidden, hidden), hidden)] = g_ref[0, lo:lo + up_rows].astype(f32)


def place_qkv_body(count, start, rank_ref, g_ref, *refs):
    rank, me = rank_ref[0], rank_ref[1]
    if start:
        sm_in, _, _, qkv_ref, out_ref = refs[:5]
        small_refs, stage_s, sm_s = refs[5:-2], refs[-2], refs[-1]
    else:
        qkv_ref, out_ref, sm_s, stage_s = refs
    step = pl.program_id(0)
    rows, third = out_ref.shape[0], out_ref.shape[0] // 3
    width = out_ref.shape[1]
    part = width // 4
    wide = g_ref.shape[2]
    small = 16 // count
    if start:
        @pl.when(step == 0)
        def _():
            sm_s[...] = sm_in[...]
    stage_s[...] = g_ref[0, 0:4 * rows].astype(f32)
    for j in range(4):
        block = stage_s[at_rows(rank ^ j, rows)]
        for i in range(3):
            qkv_ref[:, i * width + j * part:i * width + (j + 1) * part] = block[:, i * part:(i + 1) * part]
    sm_s[chunk_at(rank, me, count, step + start)] = g_ref[0, 4 * rows:4 * rows + small, 0:part].astype(f32)
    lo = 4 * rows + small
    out_ref[:, 0:wide] = g_ref[0, lo:lo + rows].astype(f32)
    packed = g_ref[0, lo + rows:lo + rows + third].astype(f32)
    out_ref[:, wide:] = jnp.concatenate([packed[:, i * part:(i + 1) * part] for i in range(3)], 0)
    if start:
        @pl.when(step == pl.num_programs(0) - 1)
        def _():
            rows_of = [sm_s[i // small, i % small:i % small + 1] for i in range(16)]
            table_ref = small_refs[0]
            for i in range(table_ref.shape[0]):
                table_ref[i:i + 1] = rows_of[i]
            for ref, i in zip(small_refs[1:7], (5, 6, 9, 7, 8, 10)):
                ref[...] = rows_of[i].reshape(part)
            for i in range(4):
                small_refs[7][i * part:(i + 1) * part] = rows_of[11 + i].reshape(part)


def join_qkv_body(low_ref, b1, b2, b3, out_ref):
    step = b1.shape[0]
    small = (low_ref.shape[0] - out_ref.shape[0]) // 3
    rows = step - small
    total = low_ref[rows:step].astype(f32)
    out_ref[0:rows] = low_ref[0:rows]
    for k, b in enumerate((b1, b2, b3)):
        out_ref[(k + 1) * rows:(k + 2) * rows] = b[0:rows]
        total = total + b[rows:step].astype(f32)
    out_ref[4 * rows:4 * rows + small] = total.astype(bf16)
    out_ref[4 * rows + small:] = low_ref[4 * step:]


def qkv_blocks_body(rank_ref, w_ref, own_ref, near_ref, far_ref, stage_s):
    rank = rank_ref[0]
    part = w_ref.shape[0]
    for t in range(4):
        stage_s[t] = jnp.concatenate(
            [w_ref[:, (4 * i + t) * part:(4 * i + t + 1) * part] for i in range(3)], 1)
    own_ref[...] = stage_s[rank]
    near_ref[...] = stage_s[rank ^ 1]
    far_ref[0:part] = stage_s[rank ^ 2]
    far_ref[part:] = stage_s[rank ^ 3]


def up_blocks_body(rank_ref, w_ref, cot_ref, own_ref, near_ref, far_ref):
    rank, side = rank_ref[0], rank_ref[2]
    rows = cot_ref.shape[0]
    hidden = own_ref.shape[1]

    def block(k):
        return w_ref[:, pl.ds(pl.multiple_of((rank ^ k) * hidden, hidden), hidden)]

    own_ref[...] = block(0)
    near_ref[0:rows] = cot_ref[...]
    near_ref[rows:] = block(1)
    far_ref[0:rows] = cot_ref[...]
    far_ref[rows:] = block(2 + side)


def by_core(value):
    return lax.ppermute(value, "shard", CORE)


def by_row(value):
    return lax.ppermute(value, "shard", ROWY)


def gather_rows(block):
    far = by_row(block)
    return block, by_core(block), far, by_core(far)


def scatter_sum(send, keep, far, rows):
    recv = by_core(send)
    half = rows // 2
    onward = [(far[i:i + half] + recv[rows + i:rows + i + half].astype(f32)).astype(bf16) for i in (0, half)]
    return keep, recv, [by_row(o) for o in onward], onward


def gather_halves(first, second, near):
    far = by_row(first), by_row(second)
    return first, second, near, by_core(second), *far, by_core(far[0]), by_core(far[1])


def after(value, *others):
    return lax.optimization_barrier((value,) + others)[0]


def phases_of(count):
    return (count - 1).bit_length()


def order_of(count, core):
    order = list(range(phases_of(count)))
    if core and len(order) > 1:
        order[0], order[1] = order[1], order[0]
    return order


def plane_pairs(count, phase):
    pairs = []
    for r in range(count):
        for s in range(4):
            pairs.append((4 * r + s, 4 * (r ^ (1 << order_of(count, s % 2)[phase])) + s))
    return pairs


def chunk_index(count, replica):
    total = jnp.zeros((), jnp.int32)
    for position in order_of(count, 0):
        total = total * 2 + ((replica >> position) & 1)
    return total


def plane_swap(value, count, phase):
    return lax.ppermute(value, ("replica", "shard"), plane_pairs(count, phase))


def split_step(keep, got):
    half = keep.shape[0] // 2
    total = (keep.astype(f32) + got.astype(f32)).astype(bf16)
    return total[:half], total[half:]


def shards(replicas, tokens, pass_ids, seg_ids, cotangent, pass_table, norm1_gain, norm1_bias, qkv_weight, out_weight,
           out_bias, norm2_gain, norm2_bias, up_weight, up_bias, down_weight, down_bias):
    rows, width = tokens.shape
    part = width // 4
    seq = seg_ids.shape[0]
    hidden = up_bias.shape[0]
    phases = phases_of(replicas)
    packed = in_kernel(replicas, width)
    rank = lax.axis_index("shard").astype(jnp.int32)
    replica = lax.axis_index("replica").astype(jnp.int32)
    me = chunk_index(replicas, replica)
    place = jnp.stack([rank, me, replica & 1])
    smem = pl.BlockSpec(memory_space=pltpu.SMEM)
    vmem = pl.BlockSpec(memory_space=pltpu.VMEM)

    def call(body, micros, outs, scratch, *args, ranked=True, aliases=None, wide=False):
        specs = [smem] * ranked + [vmem] * (len(args) - ranked)
        return pl.pallas_call(
            body,
            out_shape=[jax.ShapeDtypeStruct(s, d) for s, d in outs],
            in_specs=specs,
            out_specs=[vmem] * len(outs),
            scratch_shapes=[pltpu.VMEM(s, d) for s, d in scratch],
            input_output_aliases=aliases or {},
            compiler_params=pltpu.CompilerParams(vmem_limit_bytes=None if wide else 8 * 2**20),
            cost_estimate=pl.CostEstimate(flops=int(micros * 1.1e9), bytes_accessed=0, transcendentals=0),
        )(*args)

    def placed(body, values, start, shapes, blocks_of, extra, scratch, aliases, *first):
        def at_chunk(p, s):
            return (chunk_at(s[0], s[1], replicas, p + start), 0)

        def whole(shape):
            return pl.BlockSpec(shape, lambda p, s: (0,) * len(shape))

        return pl.pallas_call(
            body,
            out_shape=[jax.ShapeDtypeStruct(s, f32) for s in shapes],
            grid_spec=pltpu.PrefetchScalarGridSpec(
                num_scalar_prefetch=1, grid=(replicas // 2,),
                in_specs=[pl.BlockSpec((1,) + values.shape[1:], lambda p, s: (p, 0, 0))]
                + [whole(e.shape) if e.ndim == 3 else pl.BlockSpec(memory_space=pl.ANY) for e in extra],
                out_specs=[pl.BlockSpec(b, at_chunk) if b else whole(s) for s, b in zip(shapes, blocks_of)],
                scratch_shapes=[pltpu.VMEM(s, f32) for s in scratch]),
            input_output_aliases=aliases,
            compiler_params=pltpu.CompilerParams(vmem_limit_bytes=8 * 2**20),
            cost_estimate=pl.CostEstimate(flops=int(2.2e9), bytes_accessed=0, transcendentals=0),
        )(after(place, *first) if first else place, values, *extra)

    block, = call(pack_body, 1, [((rows + 16, width), bf16)], [], tokens, pass_ids, pass_table.T, norm1_gain, norm1_bias,
                  out_bias, norm2_gain, norm2_bias, down_bias, ranked=False, wide=True)
    x1, x2 = by_core(block), by_row(block)
    own_q, near_q, far_q = call(
        qkv_blocks_body, 0, [((part, 3 * part), bf16), ((part, 3 * part), bf16), ((2 * part, 3 * part), bf16)],
        [((4, part, 3 * part), bf16)], place, after(qkv_weight, block))
    far_q = by_row(far_q)
    own_u, near_u, far_u = call(
        up_blocks_body, 0,
        [((part, hidden), bf16), ((rows + part, width), bf16), ((rows + part, width), bf16)],
        [], place, up_weight, after(cotangent, own_q))
    x2 = after(x2, own_u)
    blocks = block, x1, x2, by_core(x2)
    segc, segr, sin, par, nrm, nrm_late, unit, inv, ids = call(
        norm_body, 0,
        [((seq, 1), f32), ((8, seq), f32), ((rows, width), f32), ((16, width), f32), ((seq, width), bf16),
         ((seq, width), bf16), ((seq, width), bf16), ((seq, 1), f32), ((8, rows), f32)], [], place, seg_ids, *blocks)
    far_q = after(far_q, ids)
    wq = own_q, by_core(near_q), far_q, by_core(far_q[part:])
    far_u = by_row(far_u)
    group = by_core(near_u), far_u, by_core(far_u)
    pair_u = lax.ppermute(far_u[rows:], ("replica", "shard"), [
        (4 * r + s, 4 * (r ^ 1) + (s ^ (r & 1))) for r in range(replicas) for s in range(4)])

    heads = part // HD
    half_f, half_b, row_f, row_b = ((2 * rows, width), f32), ((2 * rows, width), bf16), ((rows, width), f32), ((rows, width), bf16)
    send, keep, far, qkv, ctx, lse, wq_full = call(
        front_body, 4,
        [half_b, row_f, row_f, ((seq, 3 * part), bf16), ((seq, part), bf16), ((8, seq), f32), ((width, 3 * part), bf16)],
        [((seq, 128), f32), ((3 * heads, seq, HD), bf16), ((heads, seq, HD), bf16), ((heads, seq, 1), f32)],
        place, segc, segr, nrm, *wq, out_weight)
    half = rows // 2
    hrow_f, hrow_b = ((half, width), f32), ((half, width), bf16)
    keep, recv, (first, second), _ = scatter_sum(after(send, far_u), keep, far, rows)
    def middle(start, part_far):
        return call(functools.partial(mid_body, start), 1, [hrow_f, hrow_b], [], sin, par, keep, recv, part_far,
                    ranked=False)

    mid_a, nrm_a = middle(0, first)
    near_a = by_core(nrm_a)
    mid_b, nrm_b = middle(half, after(second, pair_u, near_a))
    mids = mid_a, mid_b
    n2 = gather_halves(nrm_a, nrm_b, near_a)
    send, keep, far, act, pg = call(
        feed_body, 5, [half_b, row_f, row_f, ((seq, hidden), bf16), ((seq, hidden), bf16)],
        [((width, hidden), bf16)],
        place, *n2, cotangent, *group, own_u, pair_u, up_bias, down_weight)
    keep, recv, fars, onward = scatter_sum(send, keep, far, rows)
    feed_rows = hidden // replicas + 4 * (part // replicas)
    if packed:
        grads = [((replicas // 2, feed_rows, width), bf16)] * 2
    else:
        grads = [((hidden, width), f32), ((width, hidden), f32)]
    place_g = after(place, *onward)
    up_b, gkeep, gsend = call(
        functools.partial(feed_grad_body, replicas), 8, [((8, hidden), f32)] + grads,
        [((hidden, width), f32), ((width, hidden), f32)],
        place_g, *n2, cotangent, *group, act, pg)
    if not packed:
        nat = chunk_at(rank, me, replicas, jnp.arange(replicas))
        downs = gkeep.reshape(replicas, -1, width)[nat]
        ups = gsend.reshape(4, replicas, -1, hidden)[rank ^ jnp.arange(4)][:, nat].transpose(1, 0, 2, 3)
        both = jnp.concatenate([downs, ups.reshape(replicas, -1, width)], 1)
        both = both.astype(bf16)
        gkeep, gsend = both[:replicas // 2], both[replicas // 2:]
    got = plane_swap(gsend, replicas, 0)
    mid_grads, halves, smalls_mid = [], [], []
    for start, value, part_far in ((0, mids[0], fars[0]), (half, mids[1], fars[1])):
        outs = call(functools.partial(mid_back_body, start), 8, [hrow_f, hrow_b, ((16, width), f32)], [],
                    value, par, cotangent, after(ids, up_b), keep, recv, part_far, ranked=False)
        for group_of, out in zip((mid_grads, halves, smalls_mid), outs):
            group_of.append(out)
    branches = gather_halves(*halves, by_core(halves[0]))
    got = after(got, branches[2])
    for phase in range(1, max(phases - 1, 1)):
        gkeep, gsend = split_step(gkeep, got)
        got = plane_swap(gsend, replicas, phase)

    small = max(16, replicas)
    step = part // replicas + small // replicas
    qkv_rows = 4 * step + part // replicas + part // replicas // 3
    if packed:
        grads = [((replicas // 2, qkv_rows, 3 * part), bf16)] * 2
    else:
        grads = [((width, 3 * part), f32), ((part, width), f32)]
    dctx, delta, grad_out, dqkv = call(
        functools.partial(attn_back_one_body, range(heads)), 9,
        [((seq, part), bf16), ((8, seq), f32), ((part, width), f32), ((seq, 3 * part), bf16)],
        [((seq, 128), f32), ((seq, HD), f32)],
        place, segc, segr, *branches, qkv, ctx, lse, out_weight)
    if phases > 1:
        gkeep, gsend = split_step(gkeep, after(got, delta))
        got = plane_swap(gsend, replicas, phases - 1)
    send, keep, far, qkeep, qsend, smalls = call(
        functools.partial(attn_back_two_body, replicas), 5,
        [half_b, row_f, row_f] + grads + [((4, 16, part), f32)],
        [((width, 3 * part), f32), ((4, 16, part), f32)],
        after(place, gsend), dqkv, grad_out, nrm_late, unit, inv, ids, par, *smalls_mid, up_b,
        wq_full)
    if not packed:
        qs = qkeep.reshape(4, replicas, -1, 3 * part)[rank ^ jnp.arange(4)][:, nat].transpose(1, 0, 2, 3)
        sm = jnp.pad(smalls, ((0, 0), (0, small - 16), (0, 2 * part)))
        sm = sm.reshape(4, replicas, -1, 3 * part)[:, nat].transpose(1, 0, 2, 3)
        os = qsend.reshape(replicas, -1, width)[nat]
        both = jnp.concatenate([
            jnp.concatenate([qs, sm], 2).reshape(replicas, -1, 3 * part), os[:, :, :3 * part],
            os[:, :, 3 * part:].reshape(replicas, -1, 3 * part)], 1)
        both = both.astype(bf16)
        qkeep, qsend = both[:replicas // 2], both[replicas // 2:]
    qgot = plane_swap(qsend, replicas, 0)
    lo, ur = hidden // replicas, part // replicas

    last_phase = phases - 1
    now = {"turn": qkeep, "feed": got, "qkv": qgot}

    def swap_piece(at):
        return by_core(at(1)), by_row(at(2)), lax.ppermute(at(3), "shard", BOTH)

    def feed_swap():
        piece = (gkeep.astype(f32) + after(now["feed"], now["turn"]).astype(f32))[0].astype(bf16)
        now["swapped"] = swap_piece(lambda k: piece[lo + k * ur:lo + (k + 1) * ur])
        now["piece"], now["turn"] = piece, now["swapped"][0]

    def feed_first():
        now["feed_all"] = jnp.concatenate(
            [now["piece"][:lo + ur]] + [after(s, now["turn"]) for s in now["swapped"]], 0)[None]
        now["feed"] = plane_swap(now["feed_all"], replicas, last_phase)
        now["turn"] = now["feed_all"]

    def feed_join(phase):
        now["feed_all"] = jnp.concatenate([now["feed_all"], after(now["feed"], now["turn"])], 0)
        now["feed"] = plane_swap(now["feed_all"], replicas, phase)
        now["turn"] = now["feed_all"]

    def qkv_split(phase):
        now["qkeep"], qsend = split_step(now.get("qkeep", qkeep), after(now["qkv"], now["turn"]))
        now["qkv"] = plane_swap(qsend, replicas, phase)
        now["turn"] = qsend

    def qkv_swap():
        low = (now.get("qkeep", qkeep).astype(f32) + after(now["qkv"], now["turn"]).astype(f32))[0].astype(bf16)
        now["quads"] = swap_piece(lambda k: low[k * step:(k + 1) * step])
        now["low"], now["turn"] = low, now["quads"][0]

    def qkv_first():
        low = now["low"]
        quads = [after(s, now["turn"]) for s in now["quads"]]
        if packed:
            joined, = call(join_qkv_body, 0, [((qkv_rows - 3 * (small // replicas), 3 * part), bf16)], [], low, *quads,
                           ranked=False)
        else:
            quads = [low[:step]] + quads
            own_small = sum(q[ur:].astype(f32) for q in quads).astype(bf16)
            joined = jnp.concatenate([q[:ur] for q in quads] + [own_small, low[4 * step:]], 0)
        now["qkv_all"] = joined[None]
        now["qkv"] = plane_swap(now["qkv_all"], replicas, last_phase)
        now["turn"] = now["qkv_all"]

    def qkv_join(phase):
        now["qkv_all"] = jnp.concatenate([now["qkv_all"], after(now["qkv"], now["turn"])], 0)
        now["qkv"] = plane_swap(now["qkv_all"], replicas, phase)
        now["turn"] = now["qkv_all"]

    recv = by_core(send)

    def tokens_onward():
        onward = (far + after(recv, now["turn"])[rows:].astype(f32)).astype(bf16)
        now["tokens"], now["turn"] = by_row(onward), onward

    def tokens_end():
        now["tokens_grad"], = call(last_body, 0, [row_b], [], sin, after(par, now["turn"]), *mid_grads, keep, recv,
                                   now["tokens"], ranked=False)
        now["turn"] = now["tokens_grad"]

    def out_start():
        now["out"] = call(feed_out_body, 0, [half_b, row_f, row_f], [], after(place, now["turn"]), down_weight, act)
        now["turn"] = now["out"][0]
        now["recv_o"] = by_core(now["out"][0])

    def out_onward():
        onward = (now["out"][2] + after(now["recv_o"], now["turn"])[rows:].astype(f32)).astype(bf16)
        now["far_o"], now["turn"] = by_row(onward), onward

    def out_end():
        now["output"] = (jnp.concatenate(mids, 0) + now["out"][1] + now["recv_o"][:rows].astype(f32)
                         + after(now["far_o"], now["turn"]).astype(f32) + par[10:11]).astype(bf16)
        now["turn"] = now["output"]

    def feed_place():
        if packed:
            now["filled"] = placed(place_feed_body, now["feed_all"], 0, *feed_shapes, [], [], {}, now["turn"])
            now["turn"] = now["filled"][0]

    def qkv_place():
        if packed:
            now["qfilled"] = placed(
                functools.partial(place_qkv_body, replicas, 0), now["qkv_all"], 0,
                qkv_shapes[0] + [sm_shape], qkv_shapes[1] + [None], [], [stage], {}, now["turn"])
            now["turn"] = now["qfilled"][0]

    feed_shapes = [(hidden, width), (part, 4 * hidden)], [(lo, width), (ur, 4 * hidden)]
    qkv_shapes = [(part, 12 * part), (part, width)], [(ur, 12 * part), (ur, width)]
    stage, sm_shape = (4 * ur, 3 * part), (replicas, 16 // replicas, part)
    feed_joins = [functools.partial(feed_join, p) for p in reversed(range(last_phase))]
    qkv_joins = [functools.partial(qkv_join, p) for p in reversed(range(last_phase))]
    splits = [functools.partial(qkv_split, p) for p in range(1, phases)]
    for run in ([feed_swap, tokens_onward, out_start, feed_first] + splits[:1] + [tokens_end] + splits[1:]
                + feed_joins[:-1] + [qkv_swap, out_onward, qkv_first] + feed_joins[-1:] + [feed_place]
                + qkv_joins + [out_end, qkv_place]):
        run()
    tokens_grad, output, feed_all, got, qkv_all, qgot = (
        now[n] for n in ("tokens_grad", "output", "feed_all", "feed", "qkv_all", "qkv"))

    if packed:
        final_down, final_up = placed(
            place_feed_body, after(got, now["turn"]), replicas // 2, *feed_shapes, list(now["filled"]), [], {2: 0, 3: 1})
        filled = now["qfilled"]
        shapes, split = qkv_shapes
        vectors = [pass_table.T.shape] + [(part,)] * 6 + [(hidden,)]
        final_qkv, final_out, table, g1, b1, ob, g2, b2, db, ub = placed(
            functools.partial(place_qkv_body, replicas, replicas // 2), after(qgot, final_down), replicas // 2, shapes + vectors,
            split + [None] * 8, [filled[2], filled[0], filled[1]], [stage, sm_shape], {3: 0, 4: 1})
    else:
        back_at = jnp.argsort(nat)
        feed_all = jnp.concatenate([feed_all, got], 0)[back_at].astype(f32)
        qkv_all = jnp.concatenate([qkv_all, qgot], 0)[back_at].astype(f32)
        final_down = feed_all[:, :lo].reshape(hidden, width)
        final_up = feed_all[:, lo:].reshape(replicas, 4, ur, hidden)[:, rank ^ jnp.arange(4)]
        final_up = final_up.transpose(0, 2, 1, 3).reshape(part, 4 * hidden)
        final_qkv = qkv_all[:, :4 * ur].reshape(replicas, 4, ur, 3, part)[:, rank ^ jnp.arange(4)]
        final_qkv = final_qkv.transpose(0, 2, 3, 1, 4).reshape(part, 12 * part)
        hi = 4 * ur + small // replicas
        mine = qkv_all[:, 4 * ur:hi, :part].reshape(small, part)
        final_out = jnp.concatenate(
            [qkv_all[:, hi:hi + ur].reshape(part, 3 * part), qkv_all[:, hi + ur:].reshape(part, part)], 1)
        table, g1, b1, ob, g2, b2, db = mine[0:5], mine[5], mine[6], mine[9], mine[7], mine[8], mine[10]
        ub = mine[11:15].reshape(hidden)
    return (output, tokens_grad, table.T, g1, b1, final_qkv, final_out, ob, g2, b2, final_up, ub, final_down, db)


def solution(mesh):
    row = P(("replica", "shard"), None)
    flat = P(("replica", "shard"))
    w2, w1 = P("shard", None), P("shard")
    return jax.shard_map(
        functools.partial(shards, mesh.shape["replica"]),
        mesh=mesh,
        in_specs=(row, flat, P("replica"), row, w2, w1, w1, w2, w2, w1, w1, w1, w2, w1, w2, w1),
        out_specs=(row, row, w2, w1, w1, w2, w2, w1, w1, w1, w2, w1, w2, w1),
        check_vma=False,
    )
```

```python
import functools

import jax
import jax.numpy as jnp
from jax import lax
from jax.experimental import pallas as pl
from jax.experimental.pallas import tpu as pltpu
from jax.sharding import PartitionSpec as P

HD = 64
epsilon = 1e-05
score_scale = 0.125
masked_score = -1e30
f32 = jnp.float32
bf16 = jnp.bfloat16

CORE = [(i, i ^ 1) for i in range(4)]
ROWY = [(i, i ^ 2) for i in range(4)]
BOTH = [(i, i ^ 3) for i in range(4)]


def contract(left, right, ld, rd):
    return lax.dot_general(left, right, (((ld,), (rd,)), ((), ())), preferred_element_type=f32)


def unit_of(values):
    centred = values - jnp.mean(values, -1, keepdims=True)
    inverse = lax.rsqrt(jnp.mean(centred * centred, -1, keepdims=True) + epsilon)
    return centred * inverse, inverse


def norm_back(grad_rows, unit_rows, inverse, gain):
    scaled = grad_rows * gain
    return inverse * (
        scaled
        - jnp.mean(scaled, -1, keepdims=True)
        - unit_rows * jnp.mean(scaled * unit_rows, -1, keepdims=True)
    )


def at_rows(index, size):
    return pl.ds(pl.multiple_of(index * size, size), size)


def pack_body(x_ref, ids_ref, table_ref, g1_ref, b1_ref, ob_ref, g2_ref, b2_ref, db_ref, out_ref):
    passes, part = table_ref.shape
    rows = ids_ref.shape[0]
    out_ref[0:rows] = x_ref[...]
    ext = jnp.zeros((16, out_ref.shape[1]), bf16)
    out_ref[rows:] = ext
    out_ref[rows:rows + passes, 0:part] = table_ref[...]
    for i, ref in enumerate((g1_ref, b1_ref, ob_ref, g2_ref, b2_ref, db_ref)):
        out_ref[rows + 5 + i:rows + 6 + i, 0:part] = ref[...].astype(f32).reshape(1, part).astype(bf16)
    out_ref[rows + 11:rows + 12, 0:rows] = ids_ref[...].astype(f32).reshape(1, rows).astype(bf16)


def norm_body(rank_ref, seg_ref, x0, x1, x2, x3,
              segc_ref, segr_ref, sin_ref, par_ref, nrm_ref, late_ref, unit_ref, inv_ref, ids_ref):
    rank = rank_ref[0]
    rows, width = sin_ref.shape
    part = width // 4
    seg = seg_ref[...].astype(f32).reshape(1, seg_ref.shape[0])
    segr_ref[...] = jnp.broadcast_to(seg, segr_ref.shape)
    segc_ref[...] = jnp.broadcast_to(seg, (128, seg.shape[1])).T[:, 0:1]
    ext = [b[rows:rows + 16, 0:part].astype(f32) for b in (x0, x1, x2, x3)]
    cols = []
    for j in range(4):
        acc = jnp.zeros_like(ext[0])
        for k in range(4):
            acc = jnp.where((rank ^ k) == j, ext[k], acc)
        cols.append(acc)
    par = jnp.concatenate(cols, axis=1)
    par_ref[...] = par
    table = par[0:8].astype(bf16)
    gain, bias = par[5:6], par[6:7]
    for k, b in enumerate((x0, x1, x2, x3)):
        ids = b[rows + 11:rows + 12, 0:rows].astype(f32)
        ids_ref[k:k + 1] = ids
        one = (lax.broadcasted_iota(jnp.int32, (8, rows), 0).astype(f32) == ids).astype(bf16)
        x = b[0:rows].astype(f32) + contract(one, table, 0, 0)
        if k == 0:
            sin_ref[...] = x
        unit, inverse = unit_of(x)
        at = at_rows(rank ^ k, rows)
        unit_ref[at] = unit.astype(bf16)
        inv_ref[at] = inverse
        normed = (unit * gain + bias).astype(bf16)
        nrm_ref[at] = normed
        late_ref[at] = normed


def front_body(rank_ref, segc_ref, segr_ref, nrm_ref, w0, w1, w2, w3, wout_ref,
               near_ref, both_ref, keep_ref, far_ref, qkv_ref, ctx_ref, lse_ref, wq_ref, lse_s, head_s, ctx_s, top_s, bias_s):
    rank = rank_ref[0]
    rows, width = keep_ref.shape
    part = width // 4
    for k, w in enumerate((w0[...], w1[...], w2[0:part], w3[...])):
        wq_ref[at_rows(rank ^ k, part)] = w
    qkv_ref[...] = jnp.dot(nrm_ref[...], wq_ref[...], preferred_element_type=f32).astype(bf16)
    heads = part // HD
    total_rows = nrm_ref.shape[0]
    for i in range(3 * heads):
        head = qkv_ref[:, i * HD:(i + 1) * HD]
        head_s[i] = head * jnp.asarray(score_scale, bf16) if i < heads else head

    for i in range(total_rows // rows):
        lo, nk = i * rows, (i + 1) * rows
        qpos = lo + lax.broadcasted_iota(jnp.int32, (rows, nk), 0)
        kpos = lax.broadcasted_iota(jnp.int32, (rows, nk), 1)
        seen = (segc_ref[lo:nk] == segr_ref[0:1, :nk]) & (kpos <= qpos)
        bias_s[lo:nk, :nk] = jnp.where(seen, 0.0, masked_score)

    def one_head(h, carry):
        q, key, val = head_s[h], head_s[heads + h], head_s[2 * heads + h]
        for i in range(total_rows // rows):
            lo, nk = i * rows, (i + 1) * rows
            sc = contract(q[lo:nk], key[:nk], 1, 1) + bias_s[lo:nk, :nk]
            top = jnp.max(sc, -1, keepdims=True)
            e = jnp.exp(sc - top)
            total = jnp.sum(e, -1, keepdims=True)
            value_sum = jnp.dot(e.astype(bf16), val[:nk], preferred_element_type=f32)
            ctx_s[h, lo:nk] = (value_sum * (1.0 / total)).astype(bf16)
            top_s[h, lo:nk] = top + jnp.log(total)
        return carry

    lax.fori_loop(0, heads, one_head, 0)
    for h in range(heads):
        ctx_ref[:, h * HD:(h + 1) * HD] = ctx_s[h]
        lse_s[:, h:h + 1] = top_s[h]
    lse_ref[...] = lse_s[...].T[0:8]
    for ref, k in ((both_ref, 3), (near_ref, 1)):
        ref[...] = jnp.dot(
            ctx_ref[at_rows(rank ^ k, rows)], wout_ref[...], preferred_element_type=f32).astype(bf16)
    for ref, k in ((keep_ref, 0), (far_ref, 2)):
        ref[...] = jnp.dot(ctx_ref[at_rows(rank ^ k, rows)], wout_ref[...], preferred_element_type=f32)


def mid_body(start, sin_ref, par_ref, keep_ref, recv_ref, yrecv_ref, mid_ref, nrm_ref):
    at = slice(start, start + yrecv_ref.shape[0])
    mid = (sin_ref[at] + keep_ref[at] + recv_ref[at].astype(f32)
           + yrecv_ref[...].astype(f32) + par_ref[7:8])
    mid_ref[...] = mid
    unit, _ = unit_of(mid)
    nrm_ref[...] = (unit * par_ref[8:9] + par_ref[9:10]).astype(bf16)


def gelu_pair(v):
    c0, c1 = 0.7978845608028654, 0.044715
    sq = v * v
    t = jnp.tanh(c0 * v * (1.0 + c1 * sq))
    half = 0.5 * (1.0 + t)
    return v * half, half + 0.5 * v * (1.0 - t * t) * (c0 * (1.0 + 3.0 * c1 * sq))


def whole_block(halves):
    return jnp.concatenate([half[...] for half in halves], 0)


def feed_body(rank_ref, n0, m0, n1, m1, n2, m2, n3, m3, c0, g1, g2, g3, u0, pair_ref, ub_ref, dw_ref,
              near_ref, both_ref, keep_ref, far_ref, act_ref, pg_ref, wu_s):
    rank = rank_ref[0]
    rows, width = c0.shape
    part = width // 4
    ub_row = ub_ref[...].astype(f32).reshape(1, ub_ref.shape[0])
    side = rank_ref[2]
    wu_s[at_rows(rank, part)] = u0[...]
    wu_s[at_rows(rank ^ 1, part)] = g1[rows:]

    @pl.when(side == 0)
    def _():
        wu_s[at_rows(rank ^ 2, part)] = g2[rows:]
        wu_s[at_rows(rank ^ 3, part)] = pair_ref[...]

    @pl.when(side == 1)
    def _():
        wu_s[at_rows(rank ^ 2, part)] = pair_ref[...]
        wu_s[at_rows(rank ^ 3, part)] = g3[rows:]

    for k, (n, c) in enumerate((
            ((n0, m0), c0[...]), ((n1, m1), g1[0:rows]), ((n2, m2), g2[0:rows]), ((n3, m3), g3[0:rows]))):
        pre = jnp.dot(whole_block(n), wu_s[...], preferred_element_type=f32) + ub_row
        act, slope = gelu_pair(pre)
        act_ref[k * rows:(k + 1) * rows] = act.astype(bf16)
        pg = (contract(c, dw_ref[...], 1, 1) * slope).astype(bf16)
        pg_ref[k * rows:(k + 1) * rows] = pg
        back = contract(pg, wu_s[...], 1, 1)
        if k % 2:
            (near_ref if k == 1 else both_ref)[...] = back.astype(bf16)
        else:
            (far_ref if k else keep_ref)[...] = back


def chunk_at(rank, me, count, p):
    top, next_bit = count // 2, count // 4
    turned = p
    if next_bit:
        turned = (p % next_bit) + jnp.where((p & top) != 0, next_bit, 0) + jnp.where((p & next_bit) != 0, top, 0)
    return me ^ jnp.where((rank & 1) == 0, p, turned)


def chunk_feed(rank, me, count, gd_s, gu_s, keep_ref, gsend_ref):
    down_rows, up_rows = gd_s.shape[0] // count, gu_s.shape[0] // count // 4
    part = gu_s.shape[0] // 4

    def store(target, start):
        def one(p, carry):
            nat = chunk_at(rank, me, count, p + start)
            target[p, 0:down_rows] = gd_s[at_rows(nat, down_rows)].astype(target.dtype)
            for k in range(4):
                at = pl.ds(pl.multiple_of((rank ^ k) * part + nat * up_rows, 8), up_rows)
                lo = down_rows + k * up_rows
                target[p, lo:lo + up_rows] = gu_s[at].astype(target.dtype)
            return carry

        lax.fori_loop(0, count // 2, one, 0)

    store(keep_ref, 0)
    store(gsend_ref, count // 2)


def feed_grad_body(count, rank_ref, n0, m0, n1, m1, n2, m2, n3, m3, c0, g1, g2, g3, act_ref, pg_ref,
                   upb_ref, gkeep_ref, gsend_ref, gd_s, gu_s):
    rank, me = rank_ref[0], rank_ref[1]
    rows, width = c0.shape
    part = width // 4
    up_b = jnp.zeros((1, pg_ref.shape[1]), f32)
    blocks = (
        ((n0, m0), c0[...]), ((n1, m1), g1[0:rows]), ((n2, m2), g2[0:rows]), ((n3, m3), g3[0:rows]))
    for k, (n, c) in enumerate(blocks):
        act = act_ref[k * rows:(k + 1) * rows]
        pg = pg_ref[k * rows:(k + 1) * rows]
        gd = contract(act, c, 0, 0)
        gu = contract(whole_block(n), pg, 0, 0)
        gd_s[...] = gd if k == 0 else gd_s[...] + gd
        gu_s[...] = gu if k == 0 else gu_s[...] + gu
        up_b = up_b + jnp.sum(pg.astype(f32), 0, keepdims=True)
    upb_ref[0:1] = up_b
    if in_kernel(count, width):
        chunk_feed(rank, me, count, gd_s, gu_s, gkeep_ref, gsend_ref)
    else:
        gkeep_ref[...] = gd_s[...]
        gsend_ref[...] = gu_s[...]


def feed_out_body(rank_ref, dw_ref, act_ref, send_ref, keep_ref, far_ref):
    rows = keep_ref.shape[0]
    del rank_ref
    for k in range(4):
        out = jnp.dot(act_ref[k * rows:(k + 1) * rows], dw_ref[...], preferred_element_type=f32)
        if k % 2:
            send_ref[(k // 2) * rows:(k // 2 + 1) * rows] = out.astype(bf16)
        else:
            (far_ref if k else keep_ref)[...] = out


def in_kernel(count, width):
    return (width // 4 // count) % 24 == 0


def mid_back_body(start, mid_ref, par_ref, cot_ref, ids_ref, keep_ref, recv_ref, yrecv_ref,
                  grad_ref, branch_ref, small_ref):
    rows = mid_ref.shape[0]
    at = slice(start, start + rows)
    back = keep_ref[at] + recv_ref[at].astype(f32) + yrecv_ref[...].astype(f32)
    unit, inverse = unit_of(mid_ref[...])
    cot = cot_ref[at].astype(f32)
    grad = cot + norm_back(back, unit, inverse, par_ref[8:9])
    grad_ref[...] = grad
    branch = grad.astype(bf16)
    branch_ref[...] = branch
    one = (lax.broadcasted_iota(jnp.int32, (8, rows), 0).astype(f32) == ids_ref[0:1, at]).astype(bf16)
    small_ref[0:8] = contract(one, branch, 1, 0)
    small_ref[8:9] = jnp.sum(back * unit, 0, keepdims=True)
    small_ref[9:10] = jnp.sum(back, 0, keepdims=True)
    small_ref[10:11] = jnp.sum(branch.astype(f32), 0, keepdims=True)
    small_ref[11:12] = jnp.sum(cot, 0, keepdims=True)


def heads_back(heads, segc_ref, segr_ref, qkv_ref, lse_ref, delta_ref, dctx_ref, dqkv_ref, dq_s, bias_s):
    part = dctx_ref.shape[1]
    total_rows = qkv_ref.shape[0]
    rows = total_rows // 4
    for j in range(total_rows // rows):
        lo, hi, nq = j * rows, (j + 1) * rows, total_rows - j * rows
        kpos = lax.broadcasted_iota(jnp.int32, (rows, nq), 0)
        qpos = lax.broadcasted_iota(jnp.int32, (rows, nq), 1)
        seen = (segc_ref[lo:hi] == segr_ref[0:1, lo:]) & (kpos <= qpos)
        bias_s[lo:hi, lo:] = jnp.where(seen, 0.0, masked_score)
    for h in heads:
        q = qkv_ref[:, h * HD:(h + 1) * HD] * jnp.asarray(score_scale, bf16)
        key = qkv_ref[:, part + h * HD:part + (h + 1) * HD]
        val = qkv_ref[:, 2 * part + h * HD:2 * part + (h + 1) * HD]
        dctx = dctx_ref[:, h * HD:(h + 1) * HD]
        for j in range(total_rows // rows):
            lo = j * rows
            hi = lo + rows
            sc = contract(key[lo:hi], q[lo:], 1, 1) + bias_s[lo:hi, lo:]
            prob = jnp.exp(sc - lse_ref[h:h + 1, lo:])
            dv = jnp.dot(prob.astype(bf16), dctx[lo:], preferred_element_type=f32)
            dprob = contract(val[lo:hi], dctx[lo:], 1, 1)
            ds = (prob * (dprob - delta_ref[h:h + 1, lo:])).astype(bf16)
            dk = jnp.dot(ds, q[lo:], preferred_element_type=f32)
            dq = contract(ds, key[lo:hi], 0, 0)
            if j == 0:
                dq_s[...] = dq
            else:
                dq_s[lo:] += dq
            dqkv_ref[lo:hi, part + h * HD:part + (h + 1) * HD] = dk.astype(bf16)
            dqkv_ref[lo:hi, 2 * part + h * HD:2 * part + (h + 1) * HD] = dv.astype(bf16)
        dqkv_ref[:, h * HD:(h + 1) * HD] = (dq_s[...] * score_scale).astype(bf16)


def attn_back_one_body(heads, rank_ref, segc_ref, segr_ref, g0, f0, g1, f1, g2, f2, g3, f3, qkv_ref, ctx_ref, lse_ref, wout_ref,
                       dctx_ref, delta_ref, go_ref, dqkv_ref, del_s, dq_s, bias_s):
    rank = rank_ref[0]
    rows, width = 2 * g0.shape[0], g0.shape[1]
    part = width // 4
    go = jnp.zeros((part, width), f32)
    for k, halves in enumerate(((g0, f0), (g1, f1), (g2, f2), (g3, f3))):
        at = at_rows(rank ^ k, rows)
        g = whole_block(halves)
        dctx_ref[at] = contract(g, wout_ref[...], 1, 1).astype(bf16)
        go = go + contract(ctx_ref[at], g, 0, 0)
    go_ref[...] = go
    prod = dctx_ref[...].astype(f32) * ctx_ref[...].astype(f32)
    for h in range(part // HD):
        del_s[:, h:h + 1] = jnp.sum(prod[:, h * HD:(h + 1) * HD], -1, keepdims=True)
    delta_ref[...] = del_s[...].T[0:8]
    heads_back(heads, segc_ref, segr_ref, qkv_ref, lse_ref, delta_ref, dctx_ref, dqkv_ref, dq_s, bias_s)


def attn_back_two_body(count, rank_ref, dqkv_s, go_s, nrm_ref, wq_ref,
                       send_ref, keep_ref, far_ref, gkeep_ref, gsend_ref, gq_s):
    rank, me = rank_ref[0], rank_ref[1]
    rows, width = keep_ref.shape
    for k in range(4):
        back = contract(dqkv_s[at_rows(rank ^ k, rows)], wq_ref[...], 1, 1)
        if k % 2:
            send_ref[(k // 2) * rows:(k // 2 + 1) * rows] = back.astype(bf16)
        else:
            (far_ref if k else keep_ref)[...] = back
    gq_s[...] = contract(nrm_ref[...], dqkv_s[...], 0, 0)
    if in_kernel(count, width):
        chunk_qkv(rank, me, count, gq_s, go_s, gkeep_ref, gsend_ref)
    else:
        gkeep_ref[...] = gq_s[...]
        gsend_ref[...] = go_s[...]


def chunk_qkv(rank, me, count, gq_s, go_s, keep_ref, gsend_ref):
    part = go_s.shape[0]
    rows, third = part // count, part // count // 3
    wide = gq_s.shape[1]
    for p in range(count):
        target, place = (keep_ref, p) if p < count // 2 else (gsend_ref, p - count // 2)
        nat = chunk_at(rank, me, count, p)
        for k in range(4):
            at = pl.ds(pl.multiple_of((rank ^ k) * part + nat * rows, 8), rows)
            target[place, k * rows:(k + 1) * rows] = gq_s[at].astype(target.dtype)
        out = go_s[at_rows(nat, rows)]
        target[place, 4 * rows:5 * rows] = out[:, 0:wide].astype(target.dtype)
        tail = out[:, wide:]
        packed = jnp.concatenate([tail[i * third:(i + 1) * third] for i in range(3)], 1)
        target[place, 5 * rows:5 * rows + third] = packed.astype(target.dtype)
        target[place, 5 * rows + third:] = jnp.zeros((target.shape[1] - 5 * rows - third, wide), target.dtype)


def small_body(rank_ref, send_ref, keep_ref, far_ref, unit_ref, inv_ref, ids_ref, par_ref, smid_ref, smid2_ref, upb_ref,
               sm_ref, sm_s):
    rank = rank_ref[0]
    rows, width = keep_ref.shape
    part = width // 4
    gain = par_ref[5:6]
    smid = smid_ref[...] + smid2_ref[...]
    by_pass = smid[0:8]
    gain_sum = jnp.zeros((1, width), f32)
    bias_sum = jnp.zeros((1, width), f32)
    for k in range(4):
        at = at_rows(rank ^ k, rows)
        back = send_ref[(k // 2) * rows:(k // 2 + 1) * rows].astype(f32) if k % 2 else (far_ref if k else keep_ref)[...]
        unit = unit_ref[at].astype(f32)
        gain_sum = gain_sum + jnp.sum(back * unit, 0, keepdims=True)
        bias_sum = bias_sum + jnp.sum(back, 0, keepdims=True)
        one = (lax.broadcasted_iota(jnp.int32, (8, rows), 0).astype(f32) == ids_ref[k:k + 1]).astype(bf16)
        by_pass = by_pass + contract(one, norm_back(back, unit, inv_ref[at], gain).astype(bf16), 1, 0)
    full = jnp.concatenate([by_pass[0:5], gain_sum, bias_sum, smid[8:12],
                            jnp.zeros((5, width), f32)], 0)
    up_b = upb_ref[0:1]
    mine = lax.broadcasted_iota(jnp.int32, (16, part), 0)
    for j in range(4):
        sm = full[:, j * part:(j + 1) * part]
        for i in range(4):
            sm = jnp.where((mine == 11 + i) & (rank == j), up_b[:, i * part:(i + 1) * part], sm)
        sm_s[j] = sm
    for k in range(4):
        sm_ref[k, :, 0:part] = sm_s[rank ^ k].astype(bf16)
        sm_ref[k, :, part:] = jnp.zeros((16, sm_ref.shape[2] - part), bf16)


def cut_qkv_body(keep_ref, got_ref, sm_ref, low_ref, n1, n2, n3):
    total = keep_ref[0].astype(f32) + got_ref[0].astype(f32)
    low_ref[...] = total.astype(bf16)
    rows = n1.shape[0] - 16
    for k, ref in ((1, n1), (2, n2), (3, n3)):
        ref[0:rows] = total[k * rows:(k + 1) * rows].astype(bf16)
        ref[rows:] = sm_ref[k]


def split_qkv_body(keep_ref, got_ref, kept_ref, send_ref):
    half = kept_ref.shape[0]
    for p in range(half):
        kept_ref[p] = (keep_ref[p].astype(f32) + got_ref[p].astype(f32)).astype(bf16)
        send_ref[p] = (keep_ref[half + p].astype(f32) + got_ref[half + p].astype(f32)).astype(bf16)


def grow_feed_body(a_ref, b_ref, out_ref):
    count = a_ref.shape[0]
    for p in range(count):
        out_ref[p] = a_ref[p]
        out_ref[count + p] = b_ref[p]


def join_qkv_body(low_ref, sm_ref, b1, b2, b3, out_ref):
    rows = b1.shape[0] - 16
    pieces = low_ref.shape[0]
    total = sm_ref[0].astype(f32)
    out_ref[0:rows] = low_ref[0:rows]
    for k, b in ((1, b1), (2, b2), (3, b3)):
        out_ref[k * rows:(k + 1) * rows] = b[0:rows]
        total = total + b[rows:].astype(f32)
    out_ref[4 * rows:pieces] = low_ref[4 * rows:]
    out_ref[pieces:] = total.astype(bf16)


def grow_qkv_body(a_ref, b_ref, out_ref):
    n = a_ref.shape[0] - 16
    out_ref[0:n] = a_ref[0:n]
    out_ref[n:2 * n] = b_ref[0:n]
    out_ref[2 * n:] = (a_ref[n:].astype(f32) + b_ref[n:].astype(f32)).astype(bf16)


def last_body(sin_ref, par_ref, grad_a, grad_b, keep_ref, recv_ref, yrecv_ref, tok_ref):
    rows = sin_ref.shape[0]
    back = keep_ref[...] + recv_ref[0:rows].astype(f32) + yrecv_ref[...].astype(f32)
    unit, inverse = unit_of(sin_ref[...])
    tok_ref[...] = (whole_block((grad_a, grad_b)) + norm_back(back, unit, inverse, par_ref[5:6])).astype(bf16)


def place_feed_body(rank_ref, g_ref, *refs):
    down_ref, up_ref = refs[-2:]
    rank = rank_ref[0]
    down_rows = down_ref.shape[0]
    up_rows, hidden = up_ref.shape[0], up_ref.shape[1] // 4
    down_ref[...] = g_ref[0, 0:down_rows].astype(f32)
    for k in range(4):
        lo = down_rows + k * up_rows
        up_ref[:, pl.ds(pl.multiple_of((rank ^ k) * hidden, hidden), hidden)] = g_ref[0, lo:lo + up_rows].astype(f32)


def place_qkv_body(ends, rank_ref, g_ref, *refs):
    rank = rank_ref[0]
    if ends:
        sm_a, sm_b, _, _, qkv_ref, out_ref = refs[:6]
        small_refs, stage_s = refs[6:-1], refs[-1]
    else:
        qkv_ref, out_ref, stage_s = refs
    rows, third = out_ref.shape[0], out_ref.shape[0] // 3
    width = out_ref.shape[1]
    part = width // 4
    wide = g_ref.shape[1]
    stage_s[...] = g_ref[0:4 * rows].astype(f32)
    for j in range(4):
        block = stage_s[at_rows(rank ^ j, rows)]
        for i in range(3):
            qkv_ref[:, i * width + j * part:i * width + (j + 1) * part] = block[:, i * part:(i + 1) * part]
    out_ref[:, 0:wide] = g_ref[4 * rows:5 * rows].astype(f32)
    packed = g_ref[5 * rows:5 * rows + third].astype(f32)
    out_ref[:, wide:] = jnp.concatenate([packed[:, i * part:(i + 1) * part] for i in range(3)], 0)
    if ends:
        @pl.when(pl.program_id(0) == 0)
        def _():
            total = (sm_a[...].astype(f32) + sm_b[...].astype(f32))[:, 0:part]
            table_ref = small_refs[0]
            table_ref[...] = total[0:table_ref.shape[0]]
            for ref, i in zip(small_refs[1:7], (5, 6, 9, 7, 8, 10)):
                ref[...] = total[i:i + 1].reshape(part)
            for i in range(4):
                small_refs[7][i * part:(i + 1) * part] = total[11 + i:12 + i].reshape(part)


def qkv_blocks_body(rank_ref, w_ref, own_ref, near_ref, far_ref, stage_s):
    rank = rank_ref[0]
    part = w_ref.shape[0]
    for t in range(4):
        stage_s[t] = jnp.concatenate(
            [w_ref[:, (4 * i + t) * part:(4 * i + t + 1) * part] for i in range(3)], 1)
    own_ref[...] = stage_s[rank]
    near_ref[...] = stage_s[rank ^ 1]
    far_ref[0:part] = stage_s[rank ^ 2]
    far_ref[part:] = stage_s[rank ^ 3]


def up_blocks_body(rank_ref, w_ref, cot_ref, own_ref, near_ref, far_ref):
    rank, side = rank_ref[0], rank_ref[2]
    rows = cot_ref.shape[0]
    hidden = own_ref.shape[1]

    def block(k):
        return w_ref[:, pl.ds(pl.multiple_of((rank ^ k) * hidden, hidden), hidden)]

    own_ref[...] = block(0)
    near_ref[0:rows] = cot_ref[...]
    near_ref[rows:] = block(1)
    far_ref[0:rows] = cot_ref[...]
    far_ref[rows:] = block(2 + side)


def by_core(value):
    return lax.ppermute(value, "shard", CORE)


def by_row(value):
    return lax.ppermute(value, "shard", ROWY)


def gather_rows(block):
    far = by_row(block)
    return block, by_core(block), far, by_core(far)


def scatter_sum(near, both, keep, far, *first):
    recv_far = by_core(both)
    recv = by_core(near)
    if first:
        recv_far = after(recv_far, *first)
    half = far.shape[0] // 2
    onward = [(far[i:i + half] + recv_far[i:i + half].astype(f32)).astype(bf16) for i in (0, half)]
    return keep, recv, [by_row(o) for o in onward], onward


def gather_halves(first, second, near):
    far = by_row(first), by_row(second)
    return first, second, near, by_core(second), *far, by_core(far[0]), by_core(far[1])


def after(value, *others):
    return lax.optimization_barrier((value,) + others)[0]


def phases_of(count):
    return (count - 1).bit_length()


def order_of(count, core):
    order = list(range(phases_of(count)))
    if core and len(order) > 1:
        order[0], order[1] = order[1], order[0]
    return order


def plane_pairs(count, phase):
    pairs = []
    for r in range(count):
        for s in range(4):
            pairs.append((4 * r + s, 4 * (r ^ (1 << order_of(count, s % 2)[phase])) + s))
    return pairs


def chunk_index(count, replica):
    total = jnp.zeros((), jnp.int32)
    for position in order_of(count, 0):
        total = total * 2 + ((replica >> position) & 1)
    return total


def plane_swap(value, count, phase):
    return lax.ppermute(value, ("replica", "shard"), plane_pairs(count, phase))


def split_step(keep, got):
    half = keep.shape[0] // 2
    total = (keep.astype(f32) + got.astype(f32)).astype(bf16)
    return total[:half], total[half:]


def shards(replicas, tokens, pass_ids, seg_ids, cotangent, pass_table, norm1_gain, norm1_bias, qkv_weight, out_weight,
           out_bias, norm2_gain, norm2_bias, up_weight, up_bias, down_weight, down_bias):
    rows, width = tokens.shape
    part = width // 4
    seq = seg_ids.shape[0]
    hidden = up_bias.shape[0]
    phases = phases_of(replicas)
    packed = in_kernel(replicas, width)
    rank = lax.axis_index("shard").astype(jnp.int32)
    replica = lax.axis_index("replica").astype(jnp.int32)
    me = chunk_index(replicas, replica)
    place = jnp.stack([rank, me, replica & 1])
    smem = pl.BlockSpec(memory_space=pltpu.SMEM)
    vmem = pl.BlockSpec(memory_space=pltpu.VMEM)

    def call(body, micros, outs, scratch, *args, ranked=True, aliases=None, wide=False, limit=8):
        specs = [smem] * ranked + [vmem] * (len(args) - ranked)
        return pl.pallas_call(
            body,
            out_shape=[jax.ShapeDtypeStruct(s, d) for s, d in outs],
            in_specs=specs,
            out_specs=[vmem] * len(outs),
            scratch_shapes=[pltpu.VMEM(s, d) for s, d in scratch],
            input_output_aliases=aliases or {},
            compiler_params=pltpu.CompilerParams(vmem_limit_bytes=None if wide else limit * 2**20),
            cost_estimate=pl.CostEstimate(flops=int(micros * 1.1e9), bytes_accessed=0, transcendentals=0),
        )(*args)

    ur = part // replicas
    pieces = 5 * ur + ur // 3 + 8 * packed

    def placed(body, values, start, shapes, blocks_of, extra, scratch, aliases, *first):
        def at_chunk(p, s):
            return (chunk_at(s[0], s[1], replicas, p + start), 0)

        def whole(shape):
            return pl.BlockSpec(shape, lambda p, s: (0,) * len(shape))

        return pl.pallas_call(
            body,
            out_shape=[jax.ShapeDtypeStruct(s, f32) for s in shapes],
            grid_spec=pltpu.PrefetchScalarGridSpec(
                num_scalar_prefetch=1, grid=(replicas // 2,),
                in_specs=[pl.BlockSpec((1,) + values.shape[1:], lambda p, s: (p, 0, 0)) if values.ndim == 3
                          else pl.BlockSpec((pieces, values.shape[1]), lambda p, s: (p, 0))]
                + [pl.BlockSpec((16, e.shape[1]), lambda p, s, at=e.shape[0] // 16 - 1: (at, 0))
                   if e.dtype == bf16 else pl.BlockSpec(memory_space=pl.ANY) for e in extra],
                out_specs=[pl.BlockSpec(b, at_chunk) if b else whole(s) for s, b in zip(shapes, blocks_of)],
                scratch_shapes=[pltpu.VMEM(s, f32) for s in scratch]),
            input_output_aliases=aliases,
            compiler_params=pltpu.CompilerParams(vmem_limit_bytes=8 * 2**20),
            cost_estimate=pl.CostEstimate(flops=int(2.2e9), bytes_accessed=0, transcendentals=0),
        )(after(place, *first) if first else place, values, *extra)

    block, = call(pack_body, 1, [((rows + 16, width), bf16)], [], tokens, pass_ids, pass_table.T, norm1_gain, norm1_bias,
                  out_bias, norm2_gain, norm2_bias, down_bias, ranked=False, wide=True)
    x1, x2 = by_core(block), by_row(block)
    own_q, near_q, far_q = call(
        qkv_blocks_body, 0, [((part, 3 * part), bf16), ((part, 3 * part), bf16), ((2 * part, 3 * part), bf16)],
        [((4, part, 3 * part), bf16)], place, after(qkv_weight, block))
    far_q = by_row(far_q)
    own_u, near_u, far_u = call(
        up_blocks_body, 0,
        [((part, hidden), bf16), ((rows + part, width), bf16), ((rows + part, width), bf16)],
        [], place, up_weight, after(cotangent, own_q))
    x2 = after(x2, own_u)
    blocks = block, x1, x2, by_core(x2)
    segc, segr, sin, par, nrm, nrm_late, unit, inv, ids = call(
        norm_body, 0,
        [((seq, 1), f32), ((8, seq), f32), ((rows, width), f32), ((16, width), f32), ((seq, width), bf16),
         ((seq, width), bf16), ((seq, width), bf16), ((seq, 1), f32), ((8, rows), f32)], [], place, seg_ids, *blocks)
    far_q = after(far_q, ids)
    wq = own_q, by_core(near_q), far_q, by_core(far_q[part:])
    far_u = by_row(far_u)
    group = by_core(near_u), far_u, by_core(far_u)
    pair_u = lax.ppermute(far_u[rows:], ("replica", "shard"), [
        (4 * r + s, 4 * (r ^ 1) + (s ^ (r & 1))) for r in range(replicas) for s in range(4)])

    heads = part // HD
    half_f, half_b, row_f, row_b = ((2 * rows, width), f32), ((2 * rows, width), bf16), ((rows, width), f32), ((rows, width), bf16)
    near, both, keep, far, qkv, ctx, lse, wq_full = call(
        front_body, 0,
        [row_b, row_b, row_f, row_f, ((seq, 3 * part), bf16), ((seq, part), bf16), ((8, seq), f32),
         ((width, 3 * part), bf16)],
        [((seq, 128), f32), ((3 * heads, seq, HD), bf16), ((heads, seq, HD), bf16), ((heads, seq, 1), f32),
         ((seq, seq), f32)],
        place, segc, segr, nrm, *wq, out_weight, limit=20)
    half = rows // 2
    hrow_f, hrow_b = ((half, width), f32), ((half, width), bf16)
    keep, recv, (first, second), _ = scatter_sum(near, both, keep, far, far_u)
    def middle(start, part_far):
        return call(functools.partial(mid_body, start), 1, [hrow_f, hrow_b], [], sin, par, keep, recv, part_far,
                    ranked=False)

    mid_a, nrm_a = middle(0, first)
    near_a = by_core(nrm_a)
    mid_b, nrm_b = middle(half, after(second, pair_u, near_a))
    mids = mid_a, mid_b
    n2 = gather_halves(nrm_a, nrm_b, near_a)
    near, both, keep, far, act, pg = call(
        feed_body, 5, [row_b, row_b, row_f, row_f, ((seq, hidden), bf16), ((seq, hidden), bf16)],
        [((width, hidden), bf16)],
        place, *n2, cotangent, *group, own_u, pair_u, up_bias, down_weight)
    keep, recv, fars, onward = scatter_sum(near, both, keep, far)
    feed_rows = hidden // replicas + 4 * (part // replicas)
    if packed:
        grads = [((replicas // 2, feed_rows, width), bf16)] * 2
    else:
        grads = [((hidden, width), f32), ((width, hidden), f32)]
    place_g = after(place, *onward)
    up_b, gkeep, gsend = call(
        functools.partial(feed_grad_body, replicas), 8, [((8, hidden), f32)] + grads,
        [((hidden, width), f32), ((width, hidden), f32)],
        place_g, *n2, cotangent, *group, act, pg)
    if not packed:
        nat = chunk_at(rank, me, replicas, jnp.arange(replicas))
        downs = gkeep.reshape(replicas, -1, width)[nat]
        ups = gsend.reshape(4, replicas, -1, hidden)[rank ^ jnp.arange(4)][:, nat].transpose(1, 0, 2, 3)
        both = jnp.concatenate([downs, ups.reshape(replicas, -1, width)], 1)
        both = both.astype(bf16)
        gkeep, gsend = both[:replicas // 2], both[replicas // 2:]
    got = plane_swap(gsend, replicas, 0)
    mid_grads, halves, smalls_mid = [], [], []
    for start, value, part_far in ((0, mids[0], fars[0]), (half, mids[1], fars[1])):
        outs = call(functools.partial(mid_back_body, start), 8, [hrow_f, hrow_b, ((16, width), f32)], [],
                    value, par, cotangent, after(ids, up_b), keep, recv, part_far, ranked=False)
        for group_of, out in zip((mid_grads, halves, smalls_mid), outs):
            group_of.append(out)
    branches = gather_halves(*halves, by_core(halves[0]))
    got = after(got, branches[2])
    for phase in range(1, max(phases - 1, 1)):
        gkeep, gsend = split_step(gkeep, got)
        got = plane_swap(gsend, replicas, phase)

    if packed:
        grads = [((replicas // 2, pieces, 3 * part), bf16)] * 2
    else:
        grads = [((width, 3 * part), f32), ((part, width), f32)]
    dctx, delta, grad_out, dqkv = call(
        functools.partial(attn_back_one_body, range(heads)), 9,
        [((seq, part), bf16), ((8, seq), f32), ((part, width), f32), ((seq, 3 * part), bf16)],
        [((seq, 128), f32), ((seq, HD), f32), ((seq, seq), f32)],
        place, segc, segr, *branches, qkv, ctx, lse, out_weight, limit=20)
    if phases > 1:
        gkeep, gsend = split_step(gkeep, after(got, delta))
        got = plane_swap(gsend, replicas, phases - 1)
    send, keep, far, qkeep, qsend = call(
        functools.partial(attn_back_two_body, replicas), 3, [half_b, row_f, row_f] + grads, [((width, 3 * part), f32)],
        after(place, gsend), dqkv, grad_out, nrm_late, wq_full)
    if not packed:
        qs = qkeep.reshape(4, replicas, -1, 3 * part)[rank ^ jnp.arange(4)][:, nat].transpose(1, 0, 2, 3)
        os = qsend.reshape(replicas, -1, width)[nat]
        both = jnp.concatenate([
            qs.reshape(replicas, -1, 3 * part), os[:, :, :3 * part], os[:, :, 3 * part:].reshape(replicas, -1, 3 * part)], 1)
        both = both.astype(bf16)
        qkeep, qsend = both[:replicas // 2], both[replicas // 2:]
    qgot = plane_swap(qsend, replicas, 0)
    lo = hidden // replicas

    last_phase = phases - 1
    now = {"turn": qkeep, "feed": got, "qkv": qgot}

    def swap_piece(at):
        return by_core(at(1)), by_row(at(2)), lax.ppermute(at(3), "shard", BOTH)

    def feed_swap():
        piece = (gkeep.astype(f32) + after(now["feed"], now["turn"]).astype(f32))[0].astype(bf16)
        now["swapped"] = swap_piece(lambda k: piece[lo + k * ur:lo + (k + 1) * ur])
        now["piece"], now["turn"] = piece, now["swapped"][0]

    def feed_first():
        now["feed_all"] = jnp.concatenate(
            [now["piece"][:lo + ur]] + [after(s, now["turn"]) for s in now["swapped"]], 0)[None]
        now["feed"] = plane_swap(now["feed_all"], replicas, last_phase)
        now["turn"] = now["feed_all"]

    def feed_join(phase):
        held, got = now["feed_all"], after(now["feed"], now["turn"])
        now["feed_all"], = call(grow_feed_body, 4, [((2 * held.shape[0],) + held.shape[1:], bf16)], [], held, got,
                                ranked=False)
        now["feed"] = plane_swap(now["feed_all"], replicas, phase)
        now["turn"] = now["feed_all"]

    def qkv_split(phase):
        kept, got = now.get("qkeep", qkeep), after(now["qkv"], now["turn"])
        shape = (kept.shape[0] // 2,) + kept.shape[1:]
        now["qkeep"], qsend = call(split_qkv_body, 0, [(shape, bf16)] * 2, [], kept, got, ranked=False)
        now["qkv"] = plane_swap(qsend, replicas, phase)
        now["turn"] = qsend

    def small_sums():
        now["small"], = call(
            small_body, 0, [((4, 16, 3 * part), bf16)], [((4, 16, part), f32)], after(place, now["turn"]), send, keep, far,
            unit, inv, ids, par, *smalls_mid, up_b)
        now["turn"] = now["small"]

    def qkv_swap():
        kept, got = now.get("qkeep", qkeep), after(now["qkv"], now["turn"])
        if packed:
            low, *cuts = call(cut_qkv_body, 1, [((pieces, 3 * part), bf16)] + [((ur + 16, 3 * part), bf16)] * 3, [],
                              kept, got, now["small"], ranked=False)
        else:
            low = (kept.astype(f32) + got.astype(f32))[0].astype(bf16)
            cuts = [jnp.concatenate([low[k * ur:(k + 1) * ur], now["small"][k]], 0) for k in (1, 2, 3)]
        now["quads"] = swap_piece(lambda k: cuts[k - 1])
        now["low"], now["turn"] = low, now["quads"][0]

    def qkv_first():
        low, small = now["low"], now["small"]
        quads = [after(s, now["turn"]) for s in now["quads"]]
        if packed:
            now["qkv_all"], = call(join_qkv_body, 1, [((pieces + 16, 3 * part), bf16)], [], low, small, *quads,
                                   ranked=False)
        else:
            total = small[0].astype(f32) + sum(q[ur:].astype(f32) for q in quads)
            now["qkv_all"] = jnp.concatenate(
                [low[:ur]] + [q[:ur] for q in quads] + [low[4 * ur:], total.astype(bf16)], 0)
        now["qkv"] = plane_swap(now["qkv_all"], replicas, last_phase)
        now["turn"] = now["qkv_all"]

    def qkv_join(phase):
        held, got = now["qkv_all"], after(now["qkv"], now["turn"])
        if packed:
            now["qkv_all"], = call(grow_qkv_body, 1, [((2 * held.shape[0] - 16, 3 * part), bf16)], [], held, got,
                                   ranked=False)
        else:
            total = held[-16:].astype(f32) + got[-16:].astype(f32)
            now["qkv_all"] = jnp.concatenate([held[:-16], got[:-16], total.astype(bf16)], 0)
        now["qkv"] = plane_swap(now["qkv_all"], replicas, phase)
        now["turn"] = now["qkv_all"]

    recv = by_core(send)

    def tokens_onward():
        onward = (far + after(recv, now["turn"])[rows:].astype(f32)).astype(bf16)
        now["tokens"], now["turn"] = by_row(onward), onward

    def tokens_end():
        now["tokens_grad"], = call(last_body, 0, [row_b], [], sin, after(par, now["turn"]), *mid_grads, keep, recv,
                                   now["tokens"], ranked=False)
        now["turn"] = now["tokens_grad"]

    def out_start():
        now["out"] = call(feed_out_body, 0, [half_b, row_f, row_f], [], after(place, now["turn"]), down_weight, act)
        now["turn"] = now["out"][0]
        now["recv_o"] = by_core(now["out"][0])

    def out_onward():
        onward = (now["out"][2] + after(now["recv_o"], now["turn"])[rows:].astype(f32)).astype(bf16)
        now["far_o"], now["turn"] = by_row(onward), onward

    def out_end():
        now["output"] = (jnp.concatenate(mids, 0) + now["out"][1] + now["recv_o"][:rows].astype(f32)
                         + after(now["far_o"], now["turn"]).astype(f32) + par[10:11]).astype(bf16)
        now["turn"] = now["output"]

    def feed_place():
        if packed:
            now["filled"] = placed(place_feed_body, now["feed_all"], 0, *feed_shapes, [], [], {}, now["turn"])
            now["turn"] = now["filled"][0]

    def qkv_place():
        if packed:
            now["qfilled"] = placed(
                functools.partial(place_qkv_body, False), now["qkv_all"], 0, *qkv_shapes, [], [stage], {}, now["turn"])
            now["turn"] = now["qfilled"][0]

    feed_shapes = [(hidden, width), (part, 4 * hidden)], [(lo, width), (ur, 4 * hidden)]
    qkv_shapes = [(part, 12 * part), (part, width)], [(ur, 12 * part), (ur, width)]
    stage = 4 * ur, 3 * part
    feed_joins = [functools.partial(feed_join, p) for p in reversed(range(last_phase))]
    qkv_joins = [functools.partial(qkv_join, p) for p in reversed(range(last_phase))]
    splits = [functools.partial(qkv_split, p) for p in range(1, phases)]
    for run in ([feed_swap] + splits[:1] + [tokens_onward, feed_first, out_start, small_sums, tokens_end] + splits[1:]
                + feed_joins[:-1] + [qkv_swap, out_onward, qkv_first] + feed_joins[-1:] + [feed_place]
                + qkv_joins + [out_end, qkv_place]):
        run()
    tokens_grad, output, feed_all, got, qkv_all, qgot = (
        now[n] for n in ("tokens_grad", "output", "feed_all", "feed", "qkv_all", "qkv"))

    if packed:
        final_down, final_up = placed(
            place_feed_body, after(got, now["turn"]), replicas // 2, *feed_shapes, list(now["filled"]), [], {2: 0, 3: 1})
        filled = now["qfilled"]
        shapes, split = qkv_shapes
        vectors = [pass_table.T.shape] + [(part,)] * 6 + [(hidden,)]
        final_qkv, final_out, table, g1, b1, ob, g2, b2, db, ub = placed(
            functools.partial(place_qkv_body, True), after(qgot, final_down), replicas // 2, shapes + vectors,
            split + [None] * 8, [qkv_all, qgot, *filled], [stage], {4: 0, 5: 1})
    else:
        back_at = jnp.argsort(nat)
        feed_all = jnp.concatenate([feed_all, got], 0)[back_at].astype(f32)
        mine = (qkv_all[-16:].astype(f32) + qgot[-16:].astype(f32))[:, :part]
        qkv_all = jnp.concatenate([qkv_all[:-16], qgot[:-16]], 0).reshape(replicas, pieces, -1)[back_at].astype(f32)
        final_down = feed_all[:, :lo].reshape(hidden, width)
        final_up = feed_all[:, lo:].reshape(replicas, 4, ur, hidden)[:, rank ^ jnp.arange(4)]
        final_up = final_up.transpose(0, 2, 1, 3).reshape(part, 4 * hidden)
        final_qkv = qkv_all[:, :4 * ur].reshape(replicas, 4, ur, 3, part)[:, rank ^ jnp.arange(4)]
        final_qkv = final_qkv.transpose(0, 2, 3, 1, 4).reshape(part, 12 * part)
        final_out = jnp.concatenate(
            [qkv_all[:, 4 * ur:5 * ur].reshape(part, 3 * part), qkv_all[:, 5 * ur:].reshape(part, part)], 1)
        table, g1, b1, ob, g2, b2, db = mine[0:5], mine[5], mine[6], mine[9], mine[7], mine[8], mine[10]
        ub = mine[11:15].reshape(hidden)
    return (output, tokens_grad, table.T, g1, b1, final_qkv, final_out, ob, g2, b2, final_up, ub, final_down, db)


def solution(mesh):
    row = P(("replica", "shard"), None)
    flat = P(("replica", "shard"))
    w2, w1 = P("shard", None), P("shard")
    return jax.shard_map(
        functools.partial(shards, mesh.shape["replica"]),
        mesh=mesh,
        in_specs=(row, flat, P("replica"), row, w2, w1, w1, w2, w2, w1, w1, w1, w2, w1, w2, w1),
        out_specs=(row, row, w2, w1, w1, w2, w2, w1, w1, w1, w2, w1, w2, w1),
        check_vma=False,
    )
```

```python
import functools

import jax
import jax.numpy as jnp
from jax import lax
from jax.experimental import pallas as pl
from jax.experimental.pallas import tpu as pltpu
from jax.sharding import PartitionSpec as P

HD = 64
epsilon = 1e-05
score_scale = 0.125
masked_score = -1e30
f32 = jnp.float32
bf16 = jnp.bfloat16

CORE = [(i, i ^ 1) for i in range(4)]
ROWY = [(i, i ^ 2) for i in range(4)]
BOTH = [(i, i ^ 3) for i in range(4)]


def contract(left, right, ld, rd):
    return lax.dot_general(left, right, (((ld,), (rd,)), ((), ())), preferred_element_type=f32)


def unit_of(values):
    centred = values - jnp.mean(values, -1, keepdims=True)
    inverse = lax.rsqrt(jnp.mean(centred * centred, -1, keepdims=True) + epsilon)
    return centred * inverse, inverse


def norm_back(grad_rows, unit_rows, inverse, gain):
    scaled = grad_rows * gain
    return inverse * (
        scaled
        - jnp.mean(scaled, -1, keepdims=True)
        - unit_rows * jnp.mean(scaled * unit_rows, -1, keepdims=True)
    )


def at_rows(index, size):
    return pl.ds(pl.multiple_of(index * size, size), size)


def pack_body(x_ref, ids_ref, table_ref, g1_ref, b1_ref, ob_ref, g2_ref, b2_ref, db_ref, out_ref):
    passes, part = table_ref.shape
    rows = ids_ref.shape[0]
    out_ref[0:rows] = x_ref[...]
    ext = jnp.zeros((16, out_ref.shape[1]), bf16)
    out_ref[rows:] = ext
    out_ref[rows:rows + passes, 0:part] = table_ref[...]
    for i, ref in enumerate((g1_ref, b1_ref, ob_ref, g2_ref, b2_ref, db_ref)):
        out_ref[rows + 5 + i:rows + 6 + i, 0:part] = ref[...].astype(f32).reshape(1, part).astype(bf16)
    out_ref[rows + 11:rows + 12, 0:rows] = ids_ref[...].astype(f32).reshape(1, rows).astype(bf16)


def norm_body(rank_ref, seg_ref, x0, x1, x2, x3,
              segc_ref, segr_ref, sin_ref, par_ref, nrm_ref, late_ref, unit_ref, inv_ref, ids_ref):
    rank = rank_ref[0]
    rows, width = sin_ref.shape
    part = width // 4
    seg = seg_ref[...].astype(f32).reshape(1, seg_ref.shape[0])
    segr_ref[...] = jnp.broadcast_to(seg, segr_ref.shape)
    segc_ref[...] = jnp.broadcast_to(seg, (128, seg.shape[1])).T[:, 0:1]
    ext = [b[rows:rows + 16, 0:part].astype(f32) for b in (x0, x1, x2, x3)]
    cols = []
    for j in range(4):
        acc = jnp.zeros_like(ext[0])
        for k in range(4):
            acc = jnp.where((rank ^ k) == j, ext[k], acc)
        cols.append(acc)
    par = jnp.concatenate(cols, axis=1)
    par_ref[...] = par
    table = par[0:8].astype(bf16)
    gain, bias = par[5:6], par[6:7]
    for k, b in enumerate((x0, x1, x2, x3)):
        ids = b[rows + 11:rows + 12, 0:rows].astype(f32)
        ids_ref[k:k + 1] = ids
        one = (lax.broadcasted_iota(jnp.int32, (8, rows), 0).astype(f32) == ids).astype(bf16)
        x = b[0:rows].astype(f32) + contract(one, table, 0, 0)
        if k == 0:
            sin_ref[...] = x
        unit, inverse = unit_of(x)
        at = at_rows(rank ^ k, rows)
        unit_ref[at] = unit.astype(bf16)
        inv_ref[at] = inverse
        normed = (unit * gain + bias).astype(bf16)
        nrm_ref[at] = normed
        late_ref[at] = normed


def front_body(rank_ref, segc_ref, segr_ref, nrm_ref, w0, w1, w2, w3, wout_ref,
               near_ref, both_ref, keep_ref, far_ref, qkv_ref, ctx_ref, lse_ref, wq_ref, lse_s, head_s, ctx_s, top_s, bias_s):
    rank = rank_ref[0]
    rows, width = keep_ref.shape
    part = width // 4
    fold = w0.shape[0]
    rest = part - fold
    for k, w in enumerate((w0, w1, w2, w3)):
        base = (rank ^ k) * part
        wq_ref[pl.ds(pl.multiple_of(base, rest), fold)] = w[0:fold, 0:3 * part]
        for i in range(3):
            wq_ref[pl.ds(pl.multiple_of(base + fold, rest), rest), i * part:(i + 1) * part] = w[
                i * rest:(i + 1) * rest, 3 * part:]
    qkv_ref[...] = jnp.dot(nrm_ref[...], wq_ref[...], preferred_element_type=f32).astype(bf16)
    heads = part // HD
    total_rows = nrm_ref.shape[0]
    for i in range(3 * heads):
        head = qkv_ref[:, i * HD:(i + 1) * HD]
        head_s[i] = head * jnp.asarray(score_scale, bf16) if i < heads else head

    for i in range(total_rows // rows):
        lo, nk = i * rows, (i + 1) * rows
        qpos = lo + lax.broadcasted_iota(jnp.int32, (rows, nk), 0)
        kpos = lax.broadcasted_iota(jnp.int32, (rows, nk), 1)
        seen = (segc_ref[lo:nk] == segr_ref[0:1, :nk]) & (kpos <= qpos)
        bias_s[lo:nk, :nk] = jnp.where(seen, 0.0, masked_score)

    def one_head(h, carry):
        q, key, val = head_s[h], head_s[heads + h], head_s[2 * heads + h]
        for i in range(total_rows // rows):
            lo, nk = i * rows, (i + 1) * rows
            sc = contract(q[lo:nk], key[:nk], 1, 1) + bias_s[lo:nk, :nk]
            top = jnp.max(sc, -1, keepdims=True)
            e = jnp.exp(sc - top)
            total = jnp.sum(e, -1, keepdims=True)
            value_sum = jnp.dot(e.astype(bf16), val[:nk], preferred_element_type=f32)
            ctx_s[h, lo:nk] = (value_sum * (1.0 / total)).astype(bf16)
            top_s[h, lo:nk] = top + jnp.log(total)
        return carry

    lax.fori_loop(0, heads, one_head, 0)
    for h in range(heads):
        ctx_ref[:, h * HD:(h + 1) * HD] = ctx_s[h]
        lse_s[:, h:h + 1] = top_s[h]
    lse_ref[...] = lse_s[...].T[0:8]
    for ref, k in ((both_ref, 3), (near_ref, 1)):
        ref[...] = jnp.dot(
            ctx_ref[at_rows(rank ^ k, rows)], wout_ref[...], preferred_element_type=f32).astype(bf16)
    for ref, k in ((keep_ref, 0), (far_ref, 2)):
        ref[...] = jnp.dot(ctx_ref[at_rows(rank ^ k, rows)], wout_ref[...], preferred_element_type=f32)


def mid_body(start, sin_ref, par_ref, keep_ref, recv_ref, yrecv_ref, mid_ref, nrm_ref):
    at = slice(start, start + yrecv_ref.shape[0])
    mid = (sin_ref[at] + keep_ref[at] + recv_ref[at].astype(f32)
           + yrecv_ref[...].astype(f32) + par_ref[7:8])
    mid_ref[...] = mid
    unit, _ = unit_of(mid)
    nrm_ref[...] = (unit * par_ref[8:9] + par_ref[9:10]).astype(bf16)


def gelu_pair(v):
    c0, c1 = 0.7978845608028654, 0.044715
    sq = v * v
    t = jnp.tanh(c0 * v * (1.0 + c1 * sq))
    half = 0.5 * (1.0 + t)
    return v * half, half + 0.5 * v * (1.0 - t * t) * (c0 * (1.0 + 3.0 * c1 * sq))


def whole_block(halves):
    return jnp.concatenate([half[...] for half in halves], 0)


def feed_body(rank_ref, n0, m0, n1, m1, n2, m2, n3, m3, c0, g1, g2, g3, u0, pair_ref, ub_ref, dw_ref,
              near_ref, both_ref, keep_ref, far_ref, act_ref, pg_ref, wu_s):
    rank = rank_ref[0]
    rows, width = c0.shape
    part = width // 4
    ub_row = ub_ref[...].astype(f32).reshape(1, ub_ref.shape[0])
    side = rank_ref[2]
    wu_s[at_rows(rank, part)] = u0[...]
    wu_s[at_rows(rank ^ 1, part)] = g1[rows:]

    @pl.when(side == 0)
    def _():
        wu_s[at_rows(rank ^ 2, part)] = g2[rows:]
        wu_s[at_rows(rank ^ 3, part)] = pair_ref[...]

    @pl.when(side == 1)
    def _():
        wu_s[at_rows(rank ^ 2, part)] = pair_ref[...]
        wu_s[at_rows(rank ^ 3, part)] = g3[rows:]

    for k, (n, c) in enumerate((
            ((n0, m0), c0[...]), ((n1, m1), g1[0:rows]), ((n2, m2), g2[0:rows]), ((n3, m3), g3[0:rows]))):
        pre = jnp.dot(whole_block(n), wu_s[...], preferred_element_type=f32) + ub_row
        act, slope = gelu_pair(pre)
        act_ref[k * rows:(k + 1) * rows] = act.astype(bf16)
        pg = (contract(c, dw_ref[...], 1, 1) * slope).astype(bf16)
        pg_ref[k * rows:(k + 1) * rows] = pg
        back = contract(pg, wu_s[...], 1, 1)
        if k % 2:
            (near_ref if k == 1 else both_ref)[...] = back.astype(bf16)
        else:
            (far_ref if k else keep_ref)[...] = back


def chunk_at(rank, me, count, p):
    top, next_bit = count // 2, count // 4
    turned = p
    if next_bit:
        turned = (p % next_bit) + jnp.where((p & top) != 0, next_bit, 0) + jnp.where((p & next_bit) != 0, top, 0)
    return me ^ jnp.where((rank & 1) == 0, p, turned)


def chunk_feed(rank, me, count, gd_s, gu_s, keep_ref, gsend_ref):
    down_rows, up_rows = gd_s.shape[0] // count, gu_s.shape[0] // count // 4
    part = gu_s.shape[0] // 4

    def store(target, start):
        def one(p, carry):
            nat = chunk_at(rank, me, count, p + start)
            target[p, 0:down_rows] = gd_s[at_rows(nat, down_rows)].astype(target.dtype)
            for k in range(4):
                at = pl.ds(pl.multiple_of((rank ^ k) * part + nat * up_rows, 8), up_rows)
                lo = down_rows + k * up_rows
                target[p, lo:lo + up_rows] = gu_s[at].astype(target.dtype)
            return carry

        lax.fori_loop(0, count // 2, one, 0)

    store(keep_ref, 0)
    store(gsend_ref, count // 2)


def feed_grad_body(count, rank_ref, n0, m0, n1, m1, n2, m2, n3, m3, c0, g1, g2, g3, act_ref, pg_ref,
                   upb_ref, gkeep_ref, gsend_ref, gd_s, gu_s):
    rank, me = rank_ref[0], rank_ref[1]
    rows, width = c0.shape
    part = width // 4
    up_b = jnp.zeros((1, pg_ref.shape[1]), f32)
    blocks = (
        ((n0, m0), c0[...]), ((n1, m1), g1[0:rows]), ((n2, m2), g2[0:rows]), ((n3, m3), g3[0:rows]))
    for k, (n, c) in enumerate(blocks):
        act = act_ref[k * rows:(k + 1) * rows]
        pg = pg_ref[k * rows:(k + 1) * rows]
        gd = contract(act, c, 0, 0)
        gu = contract(whole_block(n), pg, 0, 0)
        gd_s[...] = gd if k == 0 else gd_s[...] + gd
        gu_s[...] = gu if k == 0 else gu_s[...] + gu
        up_b = up_b + jnp.sum(pg.astype(f32), 0, keepdims=True)
    upb_ref[0:1] = up_b
    if in_kernel(count, width):
        chunk_feed(rank, me, count, gd_s, gu_s, gkeep_ref, gsend_ref)
    else:
        gkeep_ref[...] = gd_s[...]
        gsend_ref[...] = gu_s[...]


def feed_out_body(rank_ref, dw_ref, act_ref, send_ref, keep_ref, far_ref):
    rows = keep_ref.shape[0]
    del rank_ref
    for k in range(4):
        out = jnp.dot(act_ref[k * rows:(k + 1) * rows], dw_ref[...], preferred_element_type=f32)
        if k % 2:
            send_ref[(k // 2) * rows:(k // 2 + 1) * rows] = out.astype(bf16)
        else:
            (far_ref if k else keep_ref)[...] = out


def in_kernel(count, width):
    return (width // 4 // count) % 24 == 0


def mid_back_body(start, mid_ref, par_ref, cot_ref, ids_ref, keep_ref, recv_ref, yrecv_ref,
                  grad_ref, branch_ref, small_ref):
    rows = mid_ref.shape[0]
    at = slice(start, start + rows)
    back = keep_ref[at] + recv_ref[at].astype(f32) + yrecv_ref[...].astype(f32)
    unit, inverse = unit_of(mid_ref[...])
    cot = cot_ref[at].astype(f32)
    grad = cot + norm_back(back, unit, inverse, par_ref[8:9])
    grad_ref[...] = grad
    branch = grad.astype(bf16)
    branch_ref[...] = branch
    one = (lax.broadcasted_iota(jnp.int32, (8, rows), 0).astype(f32) == ids_ref[0:1, at]).astype(bf16)
    small_ref[0:8] = contract(one, branch, 1, 0)
    small_ref[8:9] = jnp.sum(back * unit, 0, keepdims=True)
    small_ref[9:10] = jnp.sum(back, 0, keepdims=True)
    small_ref[10:11] = jnp.sum(branch.astype(f32), 0, keepdims=True)
    small_ref[11:12] = jnp.sum(cot, 0, keepdims=True)


def heads_back(heads, segc_ref, segr_ref, qkv_ref, lse_ref, delta_ref, dctx_ref, dqkv_ref, dq_s, bias_s):
    part = dctx_ref.shape[1]
    total_rows = qkv_ref.shape[0]
    rows = total_rows // 4
    for j in range(total_rows // rows):
        lo, hi, nq = j * rows, (j + 1) * rows, total_rows - j * rows
        kpos = lax.broadcasted_iota(jnp.int32, (rows, nq), 0)
        qpos = lax.broadcasted_iota(jnp.int32, (rows, nq), 1)
        seen = (segc_ref[lo:hi] == segr_ref[0:1, lo:]) & (kpos <= qpos)
        bias_s[lo:hi, lo:] = jnp.where(seen, 0.0, masked_score)
    for h in heads:
        q = qkv_ref[:, h * HD:(h + 1) * HD] * jnp.asarray(score_scale, bf16)
        key = qkv_ref[:, part + h * HD:part + (h + 1) * HD]
        val = qkv_ref[:, 2 * part + h * HD:2 * part + (h + 1) * HD]
        dctx = dctx_ref[:, h * HD:(h + 1) * HD]
        for j in range(total_rows // rows):
            lo = j * rows
            hi = lo + rows
            sc = contract(key[lo:hi], q[lo:], 1, 1) + bias_s[lo:hi, lo:]
            prob = jnp.exp(sc - lse_ref[h:h + 1, lo:])
            dv = jnp.dot(prob.astype(bf16), dctx[lo:], preferred_element_type=f32)
            dprob = contract(val[lo:hi], dctx[lo:], 1, 1)
            ds = (prob * (dprob - delta_ref[h:h + 1, lo:])).astype(bf16)
            dk = jnp.dot(ds, q[lo:], preferred_element_type=f32)
            dq = contract(ds, key[lo:hi], 0, 0)
            if j == 0:
                dq_s[...] = dq
            else:
                dq_s[lo:] += dq
            dqkv_ref[lo:hi, part + h * HD:part + (h + 1) * HD] = dk.astype(bf16)
            dqkv_ref[lo:hi, 2 * part + h * HD:2 * part + (h + 1) * HD] = dv.astype(bf16)
        dqkv_ref[:, h * HD:(h + 1) * HD] = (dq_s[...] * score_scale).astype(bf16)


def attn_back_one_body(heads, rank_ref, segc_ref, segr_ref, g0, f0, g1, f1, g2, f2, g3, f3, qkv_ref, ctx_ref, lse_ref, wout_ref,
                       dctx_ref, delta_ref, go_ref, dqkv_ref, del_s, dq_s, bias_s):
    rank = rank_ref[0]
    rows, width = 2 * g0.shape[0], g0.shape[1]
    part = width // 4
    go = jnp.zeros((part, width), f32)
    for k, halves in enumerate(((g0, f0), (g1, f1), (g2, f2), (g3, f3))):
        at = at_rows(rank ^ k, rows)
        g = whole_block(halves)
        dctx_ref[at] = contract(g, wout_ref[...], 1, 1).astype(bf16)
        go = go + contract(ctx_ref[at], g, 0, 0)
    go_ref[...] = go
    prod = dctx_ref[...].astype(f32) * ctx_ref[...].astype(f32)
    for h in range(part // HD):
        del_s[:, h:h + 1] = jnp.sum(prod[:, h * HD:(h + 1) * HD], -1, keepdims=True)
    delta_ref[...] = del_s[...].T[0:8]
    heads_back(heads, segc_ref, segr_ref, qkv_ref, lse_ref, delta_ref, dctx_ref, dqkv_ref, dq_s, bias_s)


def attn_back_two_body(count, rank_ref, dqkv_s, go_s, nrm_ref, wq_ref,
                       send_ref, keep_ref, far_ref, gkeep_ref, gsend_ref, gq_s):
    rank, me = rank_ref[0], rank_ref[1]
    rows, width = keep_ref.shape
    for k in range(4):
        back = contract(dqkv_s[at_rows(rank ^ k, rows)], wq_ref[...], 1, 1)
        if k % 2:
            send_ref[(k // 2) * rows:(k // 2 + 1) * rows] = back.astype(bf16)
        else:
            (far_ref if k else keep_ref)[...] = back
    gq_s[...] = contract(nrm_ref[...], dqkv_s[...], 0, 0)
    if in_kernel(count, width):
        chunk_qkv(rank, me, count, gq_s, go_s, gkeep_ref, gsend_ref)
    else:
        gkeep_ref[...] = gq_s[...]
        gsend_ref[...] = go_s[...]


def chunk_qkv(rank, me, count, gq_s, go_s, keep_ref, gsend_ref):
    part = go_s.shape[0]
    rows = part // count
    wide = gq_s.shape[1]
    for p in range(count):
        target, place = (keep_ref, p) if p < count // 2 else (gsend_ref, p - count // 2)
        nat = chunk_at(rank, me, count, p)
        for k in range(4):
            block = gq_s[pl.ds(pl.multiple_of((rank ^ k) * part + nat * rows, 8), rows)].astype(bf16)
            if k < 3:
                target[place, k * rows:(k + 1) * rows, 0:wide] = block
            else:
                for i in range(3):
                    target[place, i * rows:(i + 1) * rows, wide:] = block[:, i * part:(i + 1) * part]
        target[place, 3 * rows:4 * rows] = go_s[at_rows(nat, rows)].astype(bf16)


def small_body(rank_ref, send_ref, keep_ref, far_ref, unit_ref, inv_ref, ids_ref, par_ref, smid_ref, smid2_ref, upb_ref,
               sm_ref, sm_s):
    rank = rank_ref[0]
    rows, width = keep_ref.shape
    part = width // 4
    gain = par_ref[5:6]
    smid = smid_ref[...] + smid2_ref[...]
    by_pass = smid[0:8]
    gain_sum = jnp.zeros((1, width), f32)
    bias_sum = jnp.zeros((1, width), f32)
    for k in range(4):
        at = at_rows(rank ^ k, rows)
        back = send_ref[(k // 2) * rows:(k // 2 + 1) * rows].astype(f32) if k % 2 else (far_ref if k else keep_ref)[...]
        unit = unit_ref[at].astype(f32)
        gain_sum = gain_sum + jnp.sum(back * unit, 0, keepdims=True)
        bias_sum = bias_sum + jnp.sum(back, 0, keepdims=True)
        one = (lax.broadcasted_iota(jnp.int32, (8, rows), 0).astype(f32) == ids_ref[k:k + 1]).astype(bf16)
        by_pass = by_pass + contract(one, norm_back(back, unit, inv_ref[at], gain).astype(bf16), 1, 0)
    full = jnp.concatenate([by_pass[0:5], gain_sum, bias_sum, smid[8:12],
                            jnp.zeros((5, width), f32)], 0)
    up_b = upb_ref[0:1]
    mine = lax.broadcasted_iota(jnp.int32, (16, part), 0)
    for j in range(4):
        sm = full[:, j * part:(j + 1) * part]
        for i in range(4):
            sm = jnp.where((mine == 11 + i) & (rank == j), up_b[:, i * part:(i + 1) * part], sm)
        sm_s[j] = sm
    for k in range(4):
        sm_ref[k, :, 0:part] = sm_s[rank ^ k].astype(bf16)
        sm_ref[k, :, part:] = jnp.zeros((16, sm_ref.shape[2] - part), bf16)


def cut_qkv_body(keep_ref, got_ref, sm_ref, low_ref, n1, n2, n3):
    total = keep_ref[0].astype(f32) + got_ref[0].astype(f32)
    low_ref[...] = total.astype(bf16)
    rows, wide = n1.shape[0] - 16, n1.shape[1]
    part = wide // 3
    for k, ref in ((1, n1), (2, n2)):
        ref[0:rows] = total[k * rows:(k + 1) * rows, 0:wide].astype(bf16)
        ref[rows:] = sm_ref[k]
    for i in range(3):
        n3[0:rows, i * part:(i + 1) * part] = total[i * rows:(i + 1) * rows, wide:].astype(bf16)
    n3[rows:] = sm_ref[3]


def split_qkv_body(keep_ref, got_ref, kept_ref, send_ref):
    half = kept_ref.shape[0]
    for p in range(half):
        kept_ref[p] = (keep_ref[p].astype(f32) + got_ref[p].astype(f32)).astype(bf16)
        send_ref[p] = (keep_ref[half + p].astype(f32) + got_ref[half + p].astype(f32)).astype(bf16)


def grow_feed_body(a_ref, b_ref, out_ref):
    count = a_ref.shape[0]
    for p in range(count):
        out_ref[p] = a_ref[p]
        out_ref[count + p] = b_ref[p]


def join_qkv_body(low_ref, sm_ref, b1, b2, b3, out_ref):
    rows, wide = b1.shape[0] - 16, b1.shape[1]
    part = wide // 3
    pieces = low_ref.shape[0]
    total = sm_ref[0].astype(f32)
    out_ref[0:rows, 0:wide] = low_ref[0:rows, 0:wide]
    for k, b in ((1, b1), (2, b2)):
        out_ref[k * rows:(k + 1) * rows, 0:wide] = b[0:rows]
    for i in range(3):
        out_ref[i * rows:(i + 1) * rows, wide:] = b3[0:rows, i * part:(i + 1) * part]
    for b in (b1, b2, b3):
        total = total + b[rows:].astype(f32)
    out_ref[3 * rows:pieces] = low_ref[3 * rows:]
    out_ref[pieces:, 0:wide] = total.astype(bf16)
    out_ref[pieces:, wide:] = jnp.zeros((16, part), bf16)


def grow_qkv_body(a_ref, b_ref, out_ref):
    n = a_ref.shape[0] - 16
    out_ref[0:n] = a_ref[0:n]
    out_ref[n:2 * n] = b_ref[0:n]
    out_ref[2 * n:] = (a_ref[n:].astype(f32) + b_ref[n:].astype(f32)).astype(bf16)


def last_body(sin_ref, par_ref, grad_a, grad_b, keep_ref, recv_ref, yrecv_ref, tok_ref):
    rows = sin_ref.shape[0]
    back = keep_ref[...] + recv_ref[0:rows].astype(f32) + yrecv_ref[...].astype(f32)
    unit, inverse = unit_of(sin_ref[...])
    tok_ref[...] = (whole_block((grad_a, grad_b)) + norm_back(back, unit, inverse, par_ref[5:6])).astype(bf16)


def place_feed_body(rank_ref, g_ref, *refs):
    down_ref, up_ref = refs[-2:]
    rank = rank_ref[0]
    down_rows = down_ref.shape[0]
    up_rows, hidden = up_ref.shape[0], up_ref.shape[1] // 4
    down_ref[...] = g_ref[0, 0:down_rows].astype(f32)
    for k in range(4):
        lo = down_rows + k * up_rows
        up_ref[:, pl.ds(pl.multiple_of((rank ^ k) * hidden, hidden), hidden)] = g_ref[0, lo:lo + up_rows].astype(f32)


def place_qkv_body(ends, rank_ref, g_ref, *refs):
    rank = rank_ref[0]
    if ends:
        sm_a, sm_b, _, _, qkv_ref, out_ref = refs[:6]
        small_refs, stage_s = refs[6:-1], refs[-1]
    else:
        qkv_ref, out_ref, stage_s = refs
    rows, width = out_ref.shape
    part = width // 4
    wide = 3 * part
    stage_s[0:3 * rows] = g_ref[0:3 * rows, 0:wide].astype(f32)
    for i in range(3):
        stage_s[3 * rows:, i * part:(i + 1) * part] = g_ref[i * rows:(i + 1) * rows, wide:].astype(f32)
    for j in range(4):
        block = stage_s[at_rows(rank ^ j, rows)]
        for i in range(3):
            qkv_ref[:, i * width + j * part:i * width + (j + 1) * part] = block[:, i * part:(i + 1) * part]
    out_ref[...] = g_ref[3 * rows:4 * rows].astype(f32)
    if ends:
        @pl.when(pl.program_id(0) == 0)
        def _():
            total = (sm_a[...].astype(f32) + sm_b[...].astype(f32))[:, 0:part]
            table_ref = small_refs[0]
            table_ref[...] = total[0:table_ref.shape[0]]
            for ref, i in zip(small_refs[1:7], (5, 6, 9, 7, 8, 10)):
                ref[...] = total[i:i + 1].reshape(part)
            for i in range(4):
                small_refs[7][i * part:(i + 1) * part] = total[11 + i:12 + i].reshape(part)


def qkv_blocks_body(rank_ref, w_ref, own_ref, near_ref, far_ref, stage_s):
    rank = rank_ref[0]
    part = w_ref.shape[0]
    fold = own_ref.shape[0]
    rest = part - fold
    for t in range(4):
        for i in range(3):
            at = slice((4 * i + t) * part, (4 * i + t + 1) * part)
            stage_s[t, :, i * part:(i + 1) * part] = w_ref[0:fold, at]
            stage_s[t, i * rest:(i + 1) * rest, 3 * part:] = w_ref[fold:, at]
    own_ref[...] = stage_s[rank]
    near_ref[...] = stage_s[rank ^ 1]
    far_ref[0:fold] = stage_s[rank ^ 2]
    far_ref[fold:] = stage_s[rank ^ 3]


def up_blocks_body(rank_ref, w_ref, cot_ref, own_ref, near_ref, far_ref):
    rank, side = rank_ref[0], rank_ref[2]
    rows = cot_ref.shape[0]
    hidden = own_ref.shape[1]

    def block(k):
        return w_ref[:, pl.ds(pl.multiple_of((rank ^ k) * hidden, hidden), hidden)]

    own_ref[...] = block(0)
    near_ref[0:rows] = cot_ref[...]
    near_ref[rows:] = block(1)
    far_ref[0:rows] = cot_ref[...]
    far_ref[rows:] = block(2 + side)


def by_core(value):
    return lax.ppermute(value, "shard", CORE)


def by_row(value):
    return lax.ppermute(value, "shard", ROWY)


def gather_rows(block):
    far = by_row(block)
    return block, by_core(block), far, by_core(far)


def scatter_sum(near, both, keep, far, *first):
    recv_far = by_core(both)
    recv = by_core(near)
    if first:
        recv_far = after(recv_far, *first)
    half = far.shape[0] // 2
    onward = [(far[i:i + half] + recv_far[i:i + half].astype(f32)).astype(bf16) for i in (0, half)]
    return keep, recv, [by_row(o) for o in onward], onward


def gather_halves(first, second, near):
    far = by_row(first), by_row(second)
    return first, second, near, by_core(second), *far, by_core(far[0]), by_core(far[1])


def after(value, *others):
    return lax.optimization_barrier((value,) + others)[0]


def phases_of(count):
    return (count - 1).bit_length()


def order_of(count, core):
    order = list(range(phases_of(count)))
    if core and len(order) > 1:
        order[0], order[1] = order[1], order[0]
    return order


def plane_pairs(count, phase):
    pairs = []
    for r in range(count):
        for s in range(4):
            pairs.append((4 * r + s, 4 * (r ^ (1 << order_of(count, s % 2)[phase])) + s))
    return pairs


def chunk_index(count, replica):
    total = jnp.zeros((), jnp.int32)
    for position in order_of(count, 0):
        total = total * 2 + ((replica >> position) & 1)
    return total


def plane_swap(value, count, phase):
    return lax.ppermute(value, ("replica", "shard"), plane_pairs(count, phase))


def split_step(keep, got):
    half = keep.shape[0] // 2
    total = (keep.astype(f32) + got.astype(f32)).astype(bf16)
    return total[:half], total[half:]


def shards(replicas, tokens, pass_ids, seg_ids, cotangent, pass_table, norm1_gain, norm1_bias, qkv_weight, out_weight,
           out_bias, norm2_gain, norm2_bias, up_weight, up_bias, down_weight, down_bias):
    rows, width = tokens.shape
    part = width // 4
    seq = seg_ids.shape[0]
    hidden = up_bias.shape[0]
    phases = phases_of(replicas)
    packed = in_kernel(replicas, width)
    rank = lax.axis_index("shard").astype(jnp.int32)
    replica = lax.axis_index("replica").astype(jnp.int32)
    me = chunk_index(replicas, replica)
    place = jnp.stack([rank, me, replica & 1])
    smem = pl.BlockSpec(memory_space=pltpu.SMEM)
    vmem = pl.BlockSpec(memory_space=pltpu.VMEM)

    def call(body, micros, outs, scratch, *args, ranked=True, aliases=None, wide=False, limit=8):
        specs = [smem] * ranked + [vmem] * (len(args) - ranked)
        return pl.pallas_call(
            body,
            out_shape=[jax.ShapeDtypeStruct(s, d) for s, d in outs],
            in_specs=specs,
            out_specs=[vmem] * len(outs),
            scratch_shapes=[pltpu.VMEM(s, d) for s, d in scratch],
            input_output_aliases=aliases or {},
            compiler_params=pltpu.CompilerParams(vmem_limit_bytes=None if wide else limit * 2**20),
            cost_estimate=pl.CostEstimate(flops=int(micros * 1.1e9), bytes_accessed=0, transcendentals=0),
        )(*args)

    ur = part // replicas
    pieces, wide_cols = (4 * ur, width) if packed else (5 * ur + ur // 3, 3 * part)

    def placed(body, values, start, shapes, blocks_of, extra, scratch, aliases, *first):
        def at_chunk(p, s):
            return (chunk_at(s[0], s[1], replicas, p + start), 0)

        def whole(shape):
            return pl.BlockSpec(shape, lambda p, s: (0,) * len(shape))

        return pl.pallas_call(
            body,
            out_shape=[jax.ShapeDtypeStruct(s, f32) for s in shapes],
            grid_spec=pltpu.PrefetchScalarGridSpec(
                num_scalar_prefetch=1, grid=(replicas // 2,),
                in_specs=[pl.BlockSpec((1,) + values.shape[1:], lambda p, s: (p, 0, 0)) if values.ndim == 3
                          else pl.BlockSpec((pieces, values.shape[1]), lambda p, s: (p, 0))]
                + [pl.BlockSpec((16, e.shape[1]), lambda p, s, at=e.shape[0] // 16 - 1: (at, 0))
                   if e.dtype == bf16 else pl.BlockSpec(memory_space=pl.ANY) for e in extra],
                out_specs=[pl.BlockSpec(b, at_chunk) if b else whole(s) for s, b in zip(shapes, blocks_of)],
                scratch_shapes=[pltpu.VMEM(s, f32) for s in scratch]),
            input_output_aliases=aliases,
            compiler_params=pltpu.CompilerParams(vmem_limit_bytes=8 * 2**20),
            cost_estimate=pl.CostEstimate(flops=int(2.2e9), bytes_accessed=0, transcendentals=0),
        )(after(place, *first) if first else place, values, *extra)

    block, = call(pack_body, 1, [((rows + 16, width), bf16)], [], tokens, pass_ids, pass_table.T, norm1_gain, norm1_bias,
                  out_bias, norm2_gain, norm2_bias, down_bias, ranked=False, wide=True)
    x1, x2 = by_core(block), by_row(block)
    fold = part * 3 // 4
    own_q, near_q, far_q = call(
        qkv_blocks_body, 0, [((fold, width), bf16), ((fold, width), bf16), ((2 * fold, width), bf16)],
        [((4, fold, width), bf16)], place, after(qkv_weight, block))
    far_q = by_row(far_q)
    own_u, near_u, far_u = call(
        up_blocks_body, 0,
        [((part, hidden), bf16), ((rows + part, width), bf16), ((rows + part, width), bf16)],
        [], place, up_weight, after(cotangent, own_q))
    x2 = after(x2, own_u)
    blocks = block, x1, x2, by_core(x2)
    segc, segr, sin, par, nrm, nrm_late, unit, inv, ids = call(
        norm_body, 0,
        [((seq, 1), f32), ((8, seq), f32), ((rows, width), f32), ((16, width), f32), ((seq, width), bf16),
         ((seq, width), bf16), ((seq, width), bf16), ((seq, 1), f32), ((8, rows), f32)], [], place, seg_ids, *blocks)
    far_q = after(far_q, ids)
    wq = own_q, by_core(near_q), far_q, by_core(far_q[fold:])
    far_u = by_row(far_u)
    group = by_core(near_u), far_u, by_core(far_u)
    pair_u = lax.ppermute(far_u[rows:], ("replica", "shard"), [
        (4 * r + s, 4 * (r ^ 1) + (s ^ (r & 1))) for r in range(replicas) for s in range(4)])

    heads = part // HD
    half_f, half_b, row_f, row_b = ((2 * rows, width), f32), ((2 * rows, width), bf16), ((rows, width), f32), ((rows, width), bf16)
    near, both, keep, far, qkv, ctx, lse, wq_full = call(
        front_body, 0,
        [row_b, row_b, row_f, row_f, ((seq, 3 * part), bf16), ((seq, part), bf16), ((8, seq), f32),
         ((width, 3 * part), bf16)],
        [((seq, 128), f32), ((3 * heads, seq, HD), bf16), ((heads, seq, HD), bf16), ((heads, seq, 1), f32),
         ((seq, seq), f32)],
        place, segc, segr, nrm, *wq, out_weight, limit=20)
    half = rows // 2
    hrow_f, hrow_b = ((half, width), f32), ((half, width), bf16)
    keep, recv, (first, second), _ = scatter_sum(near, both, keep, far, far_u)
    def middle(start, part_far):
        return call(functools.partial(mid_body, start), 1, [hrow_f, hrow_b], [], sin, par, keep, recv, part_far,
                    ranked=False)

    mid_a, nrm_a = middle(0, first)
    near_a = by_core(nrm_a)
    mid_b, nrm_b = middle(half, after(second, pair_u, near_a))
    mids = mid_a, mid_b
    n2 = gather_halves(nrm_a, nrm_b, near_a)
    near, both, keep, far, act, pg = call(
        feed_body, 5, [row_b, row_b, row_f, row_f, ((seq, hidden), bf16), ((seq, hidden), bf16)],
        [((width, hidden), bf16)],
        place, *n2, cotangent, *group, own_u, pair_u, up_bias, down_weight)
    keep, recv, fars, onward = scatter_sum(near, both, keep, far)
    feed_rows = hidden // replicas + 4 * (part // replicas)
    if packed:
        grads = [((replicas // 2, feed_rows, width), bf16)] * 2
    else:
        grads = [((hidden, width), f32), ((width, hidden), f32)]
    place_g = after(place, *onward)
    up_b, gkeep, gsend = call(
        functools.partial(feed_grad_body, replicas), 8, [((8, hidden), f32)] + grads,
        [((hidden, width), f32), ((width, hidden), f32)],
        place_g, *n2, cotangent, *group, act, pg)
    if not packed:
        nat = chunk_at(rank, me, replicas, jnp.arange(replicas))
        downs = gkeep.reshape(replicas, -1, width)[nat]
        ups = gsend.reshape(4, replicas, -1, hidden)[rank ^ jnp.arange(4)][:, nat].transpose(1, 0, 2, 3)
        both = jnp.concatenate([downs, ups.reshape(replicas, -1, width)], 1)
        both = both.astype(bf16)
        gkeep, gsend = both[:replicas // 2], both[replicas // 2:]
    got = plane_swap(gsend, replicas, 0)
    mid_grads, halves, smalls_mid = [], [], []
    for start, value, part_far in ((0, mids[0], fars[0]), (half, mids[1], fars[1])):
        outs = call(functools.partial(mid_back_body, start), 8, [hrow_f, hrow_b, ((16, width), f32)], [],
                    value, par, cotangent, after(ids, up_b), keep, recv, part_far, ranked=False)
        for group_of, out in zip((mid_grads, halves, smalls_mid), outs):
            group_of.append(out)
    branches = gather_halves(*halves, by_core(halves[0]))
    got = after(got, branches[2])
    for phase in range(1, max(phases - 1, 1)):
        gkeep, gsend = split_step(gkeep, got)
        got = plane_swap(gsend, replicas, phase)

    if packed:
        grads = [((replicas // 2, pieces, wide_cols), bf16)] * 2
    else:
        grads = [((width, 3 * part), f32), ((part, width), f32)]
    dctx, delta, grad_out, dqkv = call(
        functools.partial(attn_back_one_body, range(heads)), 9,
        [((seq, part), bf16), ((8, seq), f32), ((part, width), f32), ((seq, 3 * part), bf16)],
        [((seq, 128), f32), ((seq, HD), f32), ((seq, seq), f32)],
        place, segc, segr, *branches, qkv, ctx, lse, out_weight, limit=20)
    if phases > 1:
        gkeep, gsend = split_step(gkeep, after(got, delta))
        got = plane_swap(gsend, replicas, phases - 1)
    send, keep, far, qkeep, qsend = call(
        functools.partial(attn_back_two_body, replicas), 3, [half_b, row_f, row_f] + grads, [((width, 3 * part), f32)],
        after(place, gsend), dqkv, grad_out, nrm_late, wq_full)
    if not packed:
        qs = qkeep.reshape(4, replicas, -1, 3 * part)[rank ^ jnp.arange(4)][:, nat].transpose(1, 0, 2, 3)
        os = qsend.reshape(replicas, -1, width)[nat]
        both = jnp.concatenate([
            qs.reshape(replicas, -1, 3 * part), os[:, :, :3 * part], os[:, :, 3 * part:].reshape(replicas, -1, 3 * part)], 1)
        both = both.astype(bf16)
        qkeep, qsend = both[:replicas // 2], both[replicas // 2:]
    qgot = plane_swap(qsend, replicas, 0)
    lo = hidden // replicas

    last_phase = phases - 1
    now = {"turn": qkeep, "feed": got, "qkv": qgot}

    def swap_piece(at):
        return by_core(at(1)), by_row(at(2)), lax.ppermute(at(3), "shard", BOTH)

    def feed_swap():
        piece = (gkeep.astype(f32) + after(now["feed"], now["turn"]).astype(f32))[0].astype(bf16)
        now["swapped"] = swap_piece(lambda k: piece[lo + k * ur:lo + (k + 1) * ur])
        now["piece"], now["turn"] = piece, now["swapped"][0]

    def feed_first():
        now["feed_all"] = jnp.concatenate(
            [now["piece"][:lo + ur]] + [after(s, now["turn"]) for s in now["swapped"]], 0)[None]
        now["feed"] = plane_swap(now["feed_all"], replicas, last_phase)
        now["turn"] = now["feed_all"]

    def feed_join(phase):
        held, got = now["feed_all"], after(now["feed"], now["turn"])
        now["feed_all"], = call(grow_feed_body, 4, [((2 * held.shape[0],) + held.shape[1:], bf16)], [], held, got,
                                ranked=False)
        now["feed"] = plane_swap(now["feed_all"], replicas, phase)
        now["turn"] = now["feed_all"]

    def qkv_split(phase):
        kept, got = now.get("qkeep", qkeep), after(now["qkv"], now["turn"])
        shape = (kept.shape[0] // 2,) + kept.shape[1:]
        now["qkeep"], qsend = call(split_qkv_body, 0, [(shape, bf16)] * 2, [], kept, got, ranked=False)
        now["qkv"] = plane_swap(qsend, replicas, phase)
        now["turn"] = qsend

    def small_sums():
        now["small"], = call(
            small_body, 0, [((4, 16, 3 * part), bf16)], [((4, 16, part), f32)], after(place, now["turn"]), send, keep, far,
            unit, inv, ids, par, *smalls_mid, up_b)
        now["turn"] = now["small"]

    def qkv_swap():
        kept, got = now.get("qkeep", qkeep), after(now["qkv"], now["turn"])
        if packed:
            low, *cuts = call(cut_qkv_body, 1, [((pieces, wide_cols), bf16)] + [((ur + 16, 3 * part), bf16)] * 3, [],
                              kept, got, now["small"], ranked=False)
        else:
            low = (kept.astype(f32) + got.astype(f32))[0].astype(bf16)
            cuts = [jnp.concatenate([low[k * ur:(k + 1) * ur], now["small"][k]], 0) for k in (1, 2, 3)]
        now["quads"] = swap_piece(lambda k: cuts[k - 1])
        now["low"], now["turn"] = low, now["quads"][0]

    def qkv_first():
        low, small = now["low"], now["small"]
        quads = [after(s, now["turn"]) for s in now["quads"]]
        if packed:
            now["qkv_all"], = call(join_qkv_body, 1, [((pieces + 16, wide_cols), bf16)], [], low, small, *quads,
                                   ranked=False)
        else:
            total = small[0].astype(f32) + sum(q[ur:].astype(f32) for q in quads)
            now["qkv_all"] = jnp.concatenate(
                [low[:ur]] + [q[:ur] for q in quads] + [low[4 * ur:], total.astype(bf16)], 0)
        now["qkv"] = plane_swap(now["qkv_all"], replicas, last_phase)
        now["turn"] = now["qkv_all"]

    def qkv_join(phase):
        held, got = now["qkv_all"], after(now["qkv"], now["turn"])
        if packed:
            now["qkv_all"], = call(grow_qkv_body, 1, [((2 * held.shape[0] - 16, wide_cols), bf16)], [], held, got,
                                   ranked=False)
        else:
            total = held[-16:].astype(f32) + got[-16:].astype(f32)
            now["qkv_all"] = jnp.concatenate([held[:-16], got[:-16], total.astype(bf16)], 0)
        now["qkv"] = plane_swap(now["qkv_all"], replicas, phase)
        now["turn"] = now["qkv_all"]

    recv = by_core(send)

    def tokens_onward():
        onward = (far + after(recv, now["turn"])[rows:].astype(f32)).astype(bf16)
        now["tokens"], now["turn"] = by_row(onward), onward

    def tokens_end():
        now["tokens_grad"], = call(last_body, 0, [row_b], [], sin, after(par, now["turn"]), *mid_grads, keep, recv,
                                   now["tokens"], ranked=False)
        now["turn"] = now["tokens_grad"]

    def out_start():
        now["out"] = call(feed_out_body, 0, [half_b, row_f, row_f], [], after(place, now["turn"]), down_weight, act)
        now["turn"] = now["out"][0]
        now["recv_o"] = by_core(now["out"][0])

    def out_onward():
        onward = (now["out"][2] + after(now["recv_o"], now["turn"])[rows:].astype(f32)).astype(bf16)
        now["far_o"], now["turn"] = by_row(onward), onward

    def out_end():
        now["output"] = (jnp.concatenate(mids, 0) + now["out"][1] + now["recv_o"][:rows].astype(f32)
                         + after(now["far_o"], now["turn"]).astype(f32) + par[10:11]).astype(bf16)
        now["turn"] = now["output"]

    def feed_place():
        if packed:
            now["filled"] = placed(place_feed_body, now["feed_all"], 0, *feed_shapes, [], [], {}, now["turn"])
            now["turn"] = now["filled"][0]

    def qkv_place():
        if packed:
            now["qfilled"] = placed(
                functools.partial(place_qkv_body, False), now["qkv_all"], 0, *qkv_shapes, [], [stage], {}, now["turn"])
            now["turn"] = now["qfilled"][0]

    feed_shapes = [(hidden, width), (part, 4 * hidden)], [(lo, width), (ur, 4 * hidden)]
    qkv_shapes = [(part, 12 * part), (part, width)], [(ur, 12 * part), (ur, width)]
    stage = 4 * ur, 3 * part
    feed_joins = [functools.partial(feed_join, p) for p in reversed(range(last_phase))]
    qkv_joins = [functools.partial(qkv_join, p) for p in reversed(range(last_phase))]
    splits = [functools.partial(qkv_split, p) for p in range(1, phases)]
    for run in ([feed_swap] + splits[:1] + [tokens_onward, feed_first, out_start, small_sums, tokens_end] + splits[1:]
                + feed_joins[:-1] + [qkv_swap, out_onward, qkv_first] + feed_joins[-1:] + [feed_place]
                + qkv_joins + [out_end, qkv_place]):
        run()
    tokens_grad, output, feed_all, got, qkv_all, qgot = (
        now[n] for n in ("tokens_grad", "output", "feed_all", "feed", "qkv_all", "qkv"))

    if packed:
        final_down, final_up = placed(
            place_feed_body, after(got, now["turn"]), replicas // 2, *feed_shapes, list(now["filled"]), [], {2: 0, 3: 1})
        filled = now["qfilled"]
        shapes, split = qkv_shapes
        vectors = [pass_table.T.shape] + [(part,)] * 6 + [(hidden,)]
        final_qkv, final_out, table, g1, b1, ob, g2, b2, db, ub = placed(
            functools.partial(place_qkv_body, True), after(qgot, final_down), replicas // 2, shapes + vectors,
            split + [None] * 8, [qkv_all, qgot, *filled], [stage], {4: 0, 5: 1})
    else:
        back_at = jnp.argsort(nat)
        feed_all = jnp.concatenate([feed_all, got], 0)[back_at].astype(f32)
        mine = (qkv_all[-16:].astype(f32) + qgot[-16:].astype(f32))[:, :part]
        qkv_all = jnp.concatenate([qkv_all[:-16], qgot[:-16]], 0).reshape(replicas, pieces, -1)[back_at].astype(f32)
        final_down = feed_all[:, :lo].reshape(hidden, width)
        final_up = feed_all[:, lo:].reshape(replicas, 4, ur, hidden)[:, rank ^ jnp.arange(4)]
        final_up = final_up.transpose(0, 2, 1, 3).reshape(part, 4 * hidden)
        final_qkv = qkv_all[:, :4 * ur].reshape(replicas, 4, ur, 3, part)[:, rank ^ jnp.arange(4)]
        final_qkv = final_qkv.transpose(0, 2, 3, 1, 4).reshape(part, 12 * part)
        final_out = jnp.concatenate(
            [qkv_all[:, 4 * ur:5 * ur].reshape(part, 3 * part), qkv_all[:, 5 * ur:].reshape(part, part)], 1)
        table, g1, b1, ob, g2, b2, db = mine[0:5], mine[5], mine[6], mine[9], mine[7], mine[8], mine[10]
        ub = mine[11:15].reshape(hidden)
    return (output, tokens_grad, table.T, g1, b1, final_qkv, final_out, ob, g2, b2, final_up, ub, final_down, db)


def solution(mesh):
    row = P(("replica", "shard"), None)
    flat = P(("replica", "shard"))
    w2, w1 = P("shard", None), P("shard")
    return jax.shard_map(
        functools.partial(shards, mesh.shape["replica"]),
        mesh=mesh,
        in_specs=(row, flat, P("replica"), row, w2, w1, w1, w2, w2, w1, w1, w1, w2, w1, w2, w1),
        out_specs=(row, row, w2, w1, w1, w2, w2, w1, w1, w1, w2, w1, w2, w1),
        check_vma=False,
    )
```
